32 devices in a mesh: dp: 16 (over z, y, core), fsdp: 2 (over x).
Axes of the slice: x: 2, y: 2, z: 4, core: 2. Of those that a mesh axis runs over, the one named last changes fastest.
Arguments:
- activations: bfloat16 [32, 768, 960], P(('dp', 'fsdp')), may hold values from -6 to 6
- doc_ids: int32 [32, 768], P(('dp', 'fsdp')), may hold values from 0 to 2, never falling along the last dimension, each value on 1 to 384 neighbouring positions
- w_query: bfloat16 [960, 960], P('fsdp'), may hold values from -0.1875 to 0.1875
- key_projection: bfloat16 [960, 320], P('fsdp'), may hold values from -0.1875 to 0.1875
- value_projection: bfloat16 [960, 320], P('fsdp'), may hold values from -0.1875 to 0.1875
- w_out: bfloat16 [960, 960], P('fsdp'), may hold values from -0.75 to 0.75
- gain_attn: bfloat16 [960], P('fsdp'), may hold values from 0.5 to 1.5
- gain_ffn: bfloat16 [960], P('fsdp'), may hold values from 0.5 to 1.5
- w_gate: bfloat16 [960, 2560], P('fsdp'), may hold values from -0.1875 to 0.1875
- w_up: bfloat16 [960, 2560], P('fsdp'), may hold values from -0.1875 to 0.1875
- w_down: bfloat16 [2560, 960], P('fsdp'), may hold values from -0.15625 to 0.15625
- cotangent: bfloat16 [32, 768, 960], P(('dp', 'fsdp')), may hold values from -6 to 6
Outputs:
- block_out: bfloat16 [32, 768, 960], P(('dp', 'fsdp'))
- grad_in: bfloat16 [32, 768, 960], P(('dp', 'fsdp'))
- grad_query: float32 [960, 960], P('fsdp')
- grad_key: float32 [960, 320], P('fsdp')
- grad_value: float32 [960, 320], P('fsdp')
- grad_out: float32 [960, 960], P('fsdp')
- grad_gain_attn: float32 [960], P('fsdp')
- grad_gain_ffn: float32 [960], P('fsdp')
- grad_gate: float32 [960, 2560], P('fsdp')
- grad_up: float32 [960, 2560], P('fsdp')
- grad_down: float32 [2560, 960], P('fsdp')
The draws below stay inside these ranges and needn't reach their ends.
Inputs may be any that keep to these rules, and one draw needn't show every extreme that they name: `doc_ids`: document numbers never fall along a sequence; a document holds at most 384 tokens, and some document holds exactly that many.
All inputs are finite; a program needn't handle non-finite values.
Results may differ from the reference program's by a relative error of at most 0.03.
Values may be sent and summed in bfloat16 or wider, within the bound.
No kernel may reach another device: no remote copies, remote signals or barrier semaphores. Data moves between devices by JAX's collectives and lax.ppermute only.
A program may use at most 192 MiB of HBM per device.

```python
import math
from functools import partial
import jax
import jax.numpy as jnp
import numpy as np
from jax import lax

D = 960
QUERY_HEADS = 15
KEY_VALUE_HEADS = 5
HEAD_SIZE = 64
FF = 2560
LEN = 768
KVD = 320
BATCH = 32


def block_scale(own_key, shape, shards, least, high):
    gain = 1.0
    for axis_at, blocks in shards:
        draws = jax.random.uniform(jax.random.fold_in(jax.random.fold_in(own_key, 6), axis_at), (blocks,), jnp.float32, least / len(shards), high / len(shards))
        gain = gain * jnp.repeat(jnp.exp(draws), shape[axis_at] // blocks).reshape((-1,) + (1,) * (len(shape) - 1 - axis_at))
    return gain


def profile(amount, total, limit, lean):
    portions = [(1 << 20) // math.isqrt(rank ** lean) + 1 for rank in range(2, amount + 1)]
    surplus, holding = total - limit - (amount - 1), [1] * (amount - 1)
    while surplus > 0:
        free = [i for i in range(amount - 1) if holding[i] < limit]
        pool, budget = sum([portions[i] for i in free]), surplus
        for i in free:
            more = min(limit - holding[i], max(1, budget * portions[i] // pool), surplus)
            holding[i] = holding[i] + more
            surplus = surplus - more
    return np.array([limit] + holding)


def uneven_parts(own_key, number_of, total, limit, slope):
    if number_of == 2:
        one = jax.random.randint(own_key, (), max(1, total - limit), min(limit, total - 1) + 1)
        return jnp.stack([one, total - one])
    lengths = jnp.asarray(profile(number_of, total, limit, slope), jnp.int32)
    pairs = (number_of - 1) // 2
    donor, sink = lengths[1:1 + 2 * pairs:2], lengths[2:2 + 2 * pairs:2]
    room = jnp.minimum(donor - 1, limit - sink)
    passed = jax.random.randint(jax.random.fold_in(own_key, 1), (pairs,), 0, 1 << 20) % (room + 1)
    lengths = lengths.at[1:1 + 2 * pairs:2].set(donor - passed).at[2:2 + 2 * pairs:2].set(sink + passed)
    return lengths[jax.random.permutation(jax.random.fold_in(own_key, 2), number_of)]


def scatter_about(stream_key, extent, deviation, most, cuts=(), dtype=jnp.bfloat16):
    level = block_scale(stream_key, extent, cuts, -0.22, 0.18) if cuts else 1.0
    result = jax.random.normal(stream_key, extent, jnp.float32) * deviation * level
    return jnp.minimum(jnp.maximum(result, -most), most).astype(dtype)


def setup_inputs(seed: int = 0) -> dict:
    seeds = jax.random.split(jax.random.key(seed), 13)
    activations = scatter_about(seeds[0], (BATCH, LEN, D), 1.0, 6.0, ((0, 32),))
    doc_ids = jax.vmap(lambda own: jnp.searchsorted(jnp.cumsum(uneven_parts(own, 3, LEN, LEN // 2, 0)), jnp.arange(LEN), side="right"))(jax.random.split(seeds[1], BATCH)).reshape((BATCH, LEN)).astype(jnp.int32)
    w_query = scatter_about(seeds[2], (D, D), D ** -0.5, 0.1875, ((0, 2),))
    key_projection = scatter_about(seeds[3], (D, KVD), D ** -0.5, 0.1875, ((0, 2),))
    value_projection = scatter_about(seeds[4], (D, KVD), D ** -0.5, 0.1875, ((0, 2),))
    w_out = scatter_about(seeds[5], (D, D), (D // 16) ** -0.5, 0.75, ((0, 2),))
    gain_attn = jnp.clip(1.0 + 0.1 * jax.random.normal(seeds[6], (D,), jnp.float32), 0.5, 1.5).astype(jnp.bfloat16)
    gain_ffn = jnp.clip(1.0 + 0.1 * jax.random.normal(seeds[7], (D,), jnp.float32), 0.5, 1.5).astype(jnp.bfloat16)
    w_gate = scatter_about(seeds[8], (D, FF), D ** -0.5, 0.1875, ((0, 2),))
    w_up = scatter_about(seeds[9], (D, FF), D ** -0.5, 0.1875, ((0, 2),))
    w_down = scatter_about(seeds[10], (FF, D), (FF // 2) ** -0.5, 0.15625, ((0, 2),))
    cotangent = scatter_about(seeds[11], (BATCH, LEN, D), 1.0, 6.0, ((0, 32),))
    return dict(activations=activations, doc_ids=doc_ids, w_query=w_query, key_projection=key_projection, value_projection=value_projection, w_out=w_out, gain_attn=gain_attn, gain_ffn=gain_ffn, w_gate=w_gate, w_up=w_up, w_down=w_down, cotangent=cotangent)


@jax.custom_vjp
def lowered_product(v):
    return lax.optimization_barrier(v.astype(jnp.bfloat16)).astype(jnp.float32)

@jax.custom_vjp
def lowered_product_backward(v):
    return v

def low_keep(v):
    return (lowered_product(v), None)

def low_pass(kept, grad):
    return (grad,)

def back_keep(v):
    return (v, None)

def back_low(kept, grad):
    return (lowered_product(grad),)
lowered_product.defvjp(low_keep, low_pass)
lowered_product_backward.defvjp(back_keep, back_low)
EPSILON = 1e-05
ROPE_BASE = 10000.0
HIGHEST = lax.Precision.HIGHEST

def matrix_product(left_mat, right_mat):
    return jnp.dot(left_mat, right_mat, precision=HIGHEST, preferred_element_type=jnp.float32)

def rms_scale(inputs, gain_vec):
    return inputs * lax.rsqrt(lax.optimization_barrier(jnp.mean(inputs * inputs, axis=-1, keepdims=True)) + EPSILON) * gain_vec

def doc_tables(doc_row):
    token_index = jnp.arange(doc_row.shape[0])
    same_doc = doc_row[:, None] == doc_row[None, :]
    earlier = token_index[None, :] < token_index[:, None]
    places = lax.optimization_barrier(jnp.sum(jnp.where(same_doc & earlier, 1.0, 0.0), axis=1))
    halves = HEAD_SIZE // 2
    frequency = ROPE_BASE ** (-2.0 * jnp.arange(halves) / HEAD_SIZE)
    angles = places[:, None] * frequency[None, :]
    allowed = same_doc & (token_index[None, :] <= token_index[:, None])
    return (jnp.cos(angles), jnp.sin(angles), allowed)

def apply_rotation(inputs, cosine_table, sine_table):
    halves = inputs.shape[-1] // 2
    first_half = inputs[..., :halves]
    second_half = inputs[..., halves:]
    cosine_row = cosine_table[:, None, :]
    sine_row = sine_table[:, None, :]
    return jnp.concatenate([first_half * cosine_row - second_half * sine_row, second_half * cosine_row + first_half * sine_row], axis=-1)

def layer_apply(inputs, params, tables):
    w_query, key_projection, value_projection, w_out, gain_attn, gain_ffn, w_gate, w_up, w_down = params
    cosine_table, sine_table, allowed = tables
    sequence_length = inputs.shape[0]
    group_count = QUERY_HEADS // KEY_VALUE_HEADS
    normalized_input = lowered_product(rms_scale(inputs, gain_attn))
    query_rows = lowered_product(apply_rotation(lowered_product_backward(matrix_product(normalized_input, w_query)).reshape(sequence_length, QUERY_HEADS, HEAD_SIZE), cosine_table, sine_table))
    rotated_keys = lowered_product(apply_rotation(lowered_product_backward(matrix_product(normalized_input, key_projection)).reshape(sequence_length, KEY_VALUE_HEADS, HEAD_SIZE), cosine_table, sine_table))
    value_rows = lowered_product(lowered_product_backward(matrix_product(normalized_input, value_projection))).reshape(sequence_length, KEY_VALUE_HEADS, HEAD_SIZE)
    grouped_rows = query_rows.reshape(sequence_length, KEY_VALUE_HEADS, group_count, HEAD_SIZE)
    scores = lowered_product_backward(jnp.einsum('qkgd,skd->kgqs', grouped_rows, rotated_keys, precision=HIGHEST) * HEAD_SIZE ** (-0.5))
    scores = jnp.where(allowed[None, None], scores, -1e+30)
    attn_probs = lowered_product(jax.nn.softmax(scores, axis=-1))
    attn_mix = jnp.einsum('kgqs,skd->qkgd', attn_probs, value_rows, precision=HIGHEST).reshape(sequence_length, QUERY_HEADS * HEAD_SIZE)
    attn_mix = lowered_product(lowered_product_backward(attn_mix))
    middle = inputs + lowered_product_backward(matrix_product(attn_mix, w_out))
    normed_ffn = lowered_product(rms_scale(middle, gain_ffn))
    gate_pre = lowered_product_backward(matrix_product(normed_ffn, w_gate))
    up_pre = lowered_product_backward(matrix_product(normed_ffn, w_up))
    activated = lowered_product(jax.nn.silu(gate_pre) * up_pre)
    return middle + lowered_product_backward(matrix_product(activated, w_down))

def two_layers(inputs, params, tables):
    return layer_apply(layer_apply(inputs, params, tables), params, tables)

def reference(activations, doc_ids, w_query, key_projection, value_projection, w_out, gain_attn, gain_ffn, w_gate, w_up, w_down, cotangent):
    params = tuple((weight.astype(jnp.float32) for weight in (w_query, key_projection, value_projection, w_out, gain_attn, gain_ffn, w_gate, w_up, w_down)))

    def one_sequence(totals, seq_item):
        inputs, doc_row, seed_grad = seq_item
        tables = doc_tables(doc_row)
        outputs, pullback = jax.vjp(partial(two_layers, tables=tables), inputs.astype(jnp.float32), params)
        grad_inputs, grad_params = pullback(seed_grad.astype(jnp.float32))
        totals = jax.tree.map(jnp.add, totals, grad_params)
        return (totals, (outputs.astype(jnp.bfloat16), grad_inputs.astype(jnp.bfloat16)))
    zero_grads = tuple((jnp.zeros_like(weight) for weight in params))
    totals, (block_out, grad_in) = lax.scan(one_sequence, zero_grads, (activations, doc_ids, cotangent))
    grad_query, grad_key, grad_value, grad_out, grad_gain_attn, grad_gain_ffn, grad_gate, grad_up, grad_down = totals
    return (block_out, grad_in, grad_query, grad_key, grad_value, grad_out, grad_gain_attn, grad_gain_ffn, grad_gate, grad_up, grad_down)
```

```python
import jax
import jax.numpy as jnp
from jax import lax
from jax.experimental import pallas as pl
from jax.experimental.pallas import tpu as pltpu
from jax.sharding import PartitionSpec as P

QUERY_HEADS = 15
KEY_VALUE_HEADS = 5
GROUP = QUERY_HEADS // KEY_VALUE_HEADS
HEAD_SIZE = 64
HALF = HEAD_SIZE // 2
LONGEST_DOC = 384
EPSILON = 1e-05
ROPE_BASE = 10000.0
NEGATIVE = -1e30
SCALE = HEAD_SIZE ** (-0.5)
QUERY_BLOCK = 128
BF16 = jnp.bfloat16
F32 = jnp.float32


def dot(left, right, contract):
    return lax.dot_general(left, right, ((contract[:1], contract[1:]), ((), ())), preferred_element_type=F32)


def key_window(block):
    return (max(0, block * QUERY_BLOCK - LONGEST_DOC), (block + 1) * QUERY_BLOCK)


def fill_mask(start_ref, mask_ref):
    for block in range(mask_ref.shape[0] // QUERY_BLOCK):
        low, high = key_window(block)
        cols = slice(block * QUERY_BLOCK, high)
        shape = (high - low, QUERY_BLOCK)
        key = low + lax.broadcasted_iota(jnp.int32, shape, 0)
        query = block * QUERY_BLOCK + lax.broadcasted_iota(jnp.int32, shape, 1)
        allowed = (key >= start_ref[:, cols]) & (key <= query)
        mask_ref[low:high, cols] = jnp.where(allowed, 0.0, NEGATIVE)


def side_by_side(ref, cols):
    return jnp.concatenate([ref[j * HEAD_SIZE : (j + 1) * HEAD_SIZE, cols] for j in range(GROUP)], axis=1)


def attention_kernel(start_ref, query_ref, key_ref, value_ref, mix_ref, logsum_ref, mask_ref, key_rows_ref):
    @pl.when(pl.program_id(0) == 0)
    def _():
        fill_mask(start_ref, mask_ref)

    key_rows_ref[...] = key_ref[...].T
    for block in range(query_ref.shape[1] // QUERY_BLOCK):
        low, high = key_window(block)
        cols = slice(block * QUERY_BLOCK, high)
        queries = side_by_side(query_ref, cols)
        mask = jnp.concatenate([mask_ref[low:high, cols]] * GROUP, axis=1)
        scores = dot(key_rows_ref[low:high, :], queries, (1, 0)) * SCALE + mask
        top = jnp.max(scores, axis=0, keepdims=True)
        weights = jnp.exp(scores - top)
        total = jnp.sum(weights, axis=0, keepdims=True)
        mix = dot(value_ref[:, low:high], weights.astype(BF16), (1, 0))
        mix = (mix / total).astype(BF16)
        logsum = top + jnp.log(total)
        for j in range(GROUP):
            part = slice(j * QUERY_BLOCK, (j + 1) * QUERY_BLOCK)
            mix_ref[j * HEAD_SIZE : (j + 1) * HEAD_SIZE, cols] = mix[:, part]
            logsum_ref[0, j : j + 1, cols] = logsum[:, part]


def attention(start, qkv):
    length = qkv.shape[1]
    rows = GROUP * HEAD_SIZE
    return pl.pallas_call(
        attention_kernel,
        grid=(KEY_VALUE_HEADS,),
        in_specs=[
            pl.BlockSpec((1, length), lambda g: (0, 0)),
            pl.BlockSpec((rows, length), lambda g: (g, 0)),
            pl.BlockSpec((HEAD_SIZE, length), lambda g: (QUERY_HEADS + g, 0)),
            pl.BlockSpec((HEAD_SIZE, length), lambda g: (QUERY_HEADS + KEY_VALUE_HEADS + g, 0)),
        ],
        out_specs=[
            pl.BlockSpec((rows, length), lambda g: (g, 0)),
            pl.BlockSpec((1, 8, length), lambda g: (g, 0, 0)),
        ],
        out_shape=[
            jax.ShapeDtypeStruct((QUERY_HEADS * HEAD_SIZE, length), BF16),
            jax.ShapeDtypeStruct((KEY_VALUE_HEADS, 8, length), F32),
        ],
        scratch_shapes=[pltpu.VMEM((length, length), F32), pltpu.VMEM((length, HEAD_SIZE), BF16)],
        compiler_params=pltpu.CompilerParams(vmem_limit_bytes=32 << 20),
        cost_estimate=pl.CostEstimate(flops=6_000_000_000, bytes_accessed=4_000_000, transcendentals=4_500_000),
        name="attention",
    )(start, qkv, qkv, qkv)


def unrotate(rows, cosine, sine):
    first = rows[:HALF]
    second = rows[HALF:]
    return (first * cosine + second * sine, second * cosine - first * sine)


def attention_back_kernel(
    start_ref, cosine_ref, sine_ref, query_ref, key_ref, value_ref, mix_ref, logsum_ref, mix_grad_ref,
    out_ref, mask_ref, key_rows_ref, value_rows_ref, key_grad_ref, value_grad_ref,
):
    group = pl.program_id(0)

    @pl.when(group == 0)
    def _():
        fill_mask(start_ref, mask_ref)

    key_rows_ref[...] = key_ref[...].T
    value_rows_ref[...] = value_ref[...].T
    key_grad_ref[...] = jnp.zeros_like(key_grad_ref)
    value_grad_ref[...] = jnp.zeros_like(value_grad_ref)
    for block in range(query_ref.shape[1] // QUERY_BLOCK):
        low, high = key_window(block)
        cols = slice(block * QUERY_BLOCK, high)
        queries = side_by_side(query_ref, cols)
        mix_grads = side_by_side(mix_grad_ref, cols)
        mixes = side_by_side(mix_ref, cols)
        inner = jnp.sum(mix_grads.astype(F32) * mixes.astype(F32), axis=0, keepdims=True)
        logsum = jnp.concatenate([logsum_ref[0, j : j + 1, cols] for j in range(GROUP)], axis=1)
        mask = jnp.concatenate([mask_ref[low:high, cols]] * GROUP, axis=1)
        scores = dot(key_rows_ref[low:high, :], queries, (1, 0)) * SCALE + mask
        weights = jnp.exp(scores - logsum)
        weight_grads = dot(value_rows_ref[low:high, :], mix_grads, (1, 0))
        score_grads = (weights * (weight_grads - inner)).astype(BF16)
        value_grad_ref[:, low:high] += dot(mix_grads, weights.astype(BF16), (1, 1))
        key_grad_ref[:, low:high] += dot(queries, score_grads, (1, 1))
        query_grads = dot(key_ref[:, low:high], score_grads, (1, 0)) * SCALE
        cosine = cosine_ref[:, cols]
        sine = sine_ref[:, cols]
        for j in range(GROUP):
            first, second = unrotate(query_grads[:, j * QUERY_BLOCK : (j + 1) * QUERY_BLOCK], cosine, sine)
            base = group * (GROUP * HEAD_SIZE) + j * HEAD_SIZE
            out_ref[pl.ds(pl.multiple_of(base, HALF), HALF), cols] = first.astype(BF16)
            out_ref[pl.ds(pl.multiple_of(base + HALF, HALF), HALF), cols] = second.astype(BF16)
    first, second = unrotate(key_grad_ref[...] * SCALE, cosine_ref[...], sine_ref[...])
    base = (QUERY_HEADS + group) * HEAD_SIZE
    out_ref[pl.ds(pl.multiple_of(base, HALF), HALF), :] = first.astype(BF16)
    out_ref[pl.ds(pl.multiple_of(base + HALF, HALF), HALF), :] = second.astype(BF16)
    base = (QUERY_HEADS + KEY_VALUE_HEADS + group) * HEAD_SIZE
    out_ref[pl.ds(pl.multiple_of(base, HEAD_SIZE), HEAD_SIZE), :] = value_grad_ref[...].astype(BF16)


def attention_back(start, cosine, sine, qkv, mix, logsum, mix_grad):
    length = qkv.shape[1]
    rows = GROUP * HEAD_SIZE
    return pl.pallas_call(
        attention_back_kernel,
        grid=(KEY_VALUE_HEADS,),
        in_specs=[
            pl.BlockSpec((1, length), lambda g: (0, 0)),
            pl.BlockSpec((HALF, length), lambda g: (0, 0)),
            pl.BlockSpec((HALF, length), lambda g: (0, 0)),
            pl.BlockSpec((rows, length), lambda g: (g, 0)),
            pl.BlockSpec((HEAD_SIZE, length), lambda g: (QUERY_HEADS + g, 0)),
            pl.BlockSpec((HEAD_SIZE, length), lambda g: (QUERY_HEADS + KEY_VALUE_HEADS + g, 0)),
            pl.BlockSpec((rows, length), lambda g: (g, 0)),
            pl.BlockSpec((1, 8, length), lambda g: (g, 0, 0)),
            pl.BlockSpec((rows, length), lambda g: (g, 0)),
        ],
        out_specs=pl.BlockSpec(qkv.shape, lambda g: (0, 0)),
        out_shape=jax.ShapeDtypeStruct(qkv.shape, BF16),
        scratch_shapes=[
            pltpu.VMEM((length, length), F32),
            pltpu.VMEM((length, HEAD_SIZE), BF16),
            pltpu.VMEM((length, HEAD_SIZE), BF16),
            pltpu.VMEM((HEAD_SIZE, length), F32),
            pltpu.VMEM((HEAD_SIZE, length), F32),
        ],
        compiler_params=pltpu.CompilerParams(vmem_limit_bytes=32 << 20),
        cost_estimate=pl.CostEstimate(flops=9_000_000_000, bytes_accessed=9_000_000, transcendentals=4_500_000),
        name="attention_back",
    )(start, cosine, sine, qkv, qkv, qkv, mix, logsum, mix_grad)


def doc_tables(doc_row):
    token_index = jnp.arange(doc_row.shape[0])
    start = jnp.sum((doc_row[:, None] < doc_row[None, :]).astype(jnp.int32), axis=0)
    places = (token_index - start).astype(F32)
    frequency = ROPE_BASE ** (-2.0 * jnp.arange(HALF, dtype=F32) / HEAD_SIZE)
    angles = frequency[:, None] * places[None, :]
    return (start[None, :], jnp.cos(angles), jnp.sin(angles))


def norm_forward(inputs, gain):
    inverse = lax.rsqrt(jnp.mean(inputs * inputs, axis=-1, keepdims=True) + EPSILON)
    return ((inputs * inverse * gain).astype(BF16), inverse)


def norm_backward(inputs, inverse, gain, grad):
    scaled = gain * grad
    inner = jnp.mean(scaled * inputs, axis=-1, keepdims=True)
    return (inverse * scaled - inputs * inverse**3 * inner, jnp.sum(grad * inputs * inverse, axis=0))


def layer_forward(inputs, weights, gains, tables):
    w_qkv, w_out, w_gate, w_up, w_down = weights
    start, cosine, sine = tables
    length = inputs.shape[0]
    normed, inverse = norm_forward(inputs, gains[0])
    raw = dot(w_qkv, normed, (0, 1))
    heads = QUERY_HEADS + KEY_VALUE_HEADS
    pairs = raw[: heads * HEAD_SIZE].reshape(heads, 2, HALF, length)
    first, second = pairs[:, 0], pairs[:, 1]
    rotated = jnp.stack([first * cosine - second * sine, second * cosine + first * sine], axis=1)
    qkv = jnp.concatenate(
        [rotated.reshape(heads * HEAD_SIZE, length).astype(BF16), raw[heads * HEAD_SIZE :].astype(BF16)], axis=0
    )
    mix, logsum = attention(start, qkv)
    middle = inputs + dot(mix, w_out, (0, 0))
    normed_ffn, inverse_ffn = norm_forward(middle, gains[1])
    gate = dot(normed_ffn, w_gate, (1, 0))
    up = dot(normed_ffn, w_up, (1, 0))
    hidden = (jax.nn.silu(gate) * up).astype(BF16)
    outputs = middle + dot(hidden, w_down, (1, 0))
    kept = (inputs, inverse, normed, qkv, logsum, mix, middle, inverse_ffn, normed_ffn, gate, up, hidden)
    return (outputs, kept)


def layer_backward(kept, grad, weights, gains, tables):
    w_qkv, w_out, w_gate, w_up, w_down = weights
    start, cosine, sine = tables
    inputs, inverse, normed, qkv, logsum, mix, middle, inverse_ffn, normed_ffn, gate, up, hidden = kept
    branch = grad.astype(BF16)
    hidden_grad = dot(branch, w_down, (1, 1))
    sigmoid = jax.nn.sigmoid(gate)
    up_grad = (hidden_grad * gate * sigmoid).astype(BF16)
    gate_grad = (hidden_grad * up * sigmoid * (1.0 + gate * (1.0 - sigmoid))).astype(BF16)
    normed_ffn_grad = dot(gate_grad, w_gate, (1, 1)) + dot(up_grad, w_up, (1, 1))
    middle_grad, gain_ffn_grad = norm_backward(middle, inverse_ffn, gains[1], normed_ffn_grad)
    middle_grad = middle_grad + grad
    attn_grad = middle_grad.astype(BF16)
    mix_grad = dot(w_out, attn_grad, (1, 1)).astype(BF16)
    qkv_grad = attention_back(start, cosine, sine, qkv, mix, logsum, mix_grad)
    normed_grad = dot(qkv_grad, w_qkv, (0, 1))
    inputs_grad, gain_attn_grad = norm_backward(inputs, inverse, gains[0], normed_grad)
    products = (
        (hidden, branch),
        (normed_ffn, gate_grad),
        (normed_ffn, up_grad),
        (mix, attn_grad),
        (normed, qkv_grad),
    )
    return (inputs_grad + middle_grad, (gain_attn_grad, gain_ffn_grad), products)


def swap_fsdp(value):
    return lax.ppermute(value, "fsdp", [(0, 1), (1, 0)])


def swap_dp(value, bit, size):
    return lax.ppermute(value, "dp", [(i, i ^ bit) for i in range(size)])


def gather_rows(shard, dp_size):
    count = shard.shape[0]
    quarter = count // 4
    fsdp = lax.axis_index("fsdp")
    place = lax.axis_index("dp") % 4
    mine = swap_fsdp(lax.dynamic_slice_in_dim(shard, place * quarter, quarter, 0))
    across = swap_dp(mine, 2, dp_size)
    beside = swap_dp(mine, 1, dp_size)
    corner = swap_dp(across, 1, dp_size)
    whole = jnp.zeros((2 * count,) + shard.shape[1:], shard.dtype)
    whole = lax.dynamic_update_slice_in_dim(whole, shard, fsdp * count, 0)
    other = (1 - fsdp) * count
    for flip, piece in ((0, mine), (2, across), (1, beside), (3, corner)):
        whole = lax.dynamic_update_slice_in_dim(whole, piece, other + (place ^ flip) * quarter, 0)
    return whole


def pick(parts, index):
    return lax.dynamic_index_in_dim(parts, index, 0, keepdims=False)


def add(left, right):
    return (left.astype(F32) + right.astype(F32)).astype(BF16)


def reduce_rows(grad, dp_size):
    count, width = grad.shape[0] // 2, grad.shape[1]
    fsdp = lax.axis_index("fsdp")
    place = lax.axis_index("dp")
    core, side = place % 2, (place // 2) % 2
    parts = grad.reshape(2, 2, count // 2, width)
    take = lambda which: lax.dynamic_index_in_dim(parts, which, 1, keepdims=False)
    parts = add(take(core), swap_dp(take(1 - core), 1, dp_size))
    parts = add(pick(parts, fsdp), swap_fsdp(pick(parts, 1 - fsdp)))
    parts = parts.reshape(2, count // 4, width)
    part = add(pick(parts, side), swap_dp(pick(parts, 1 - side), 2, dp_size))
    bit = 4
    while bit < dp_size:
        part = add(part, swap_dp(part, bit, dp_size))
        bit *= 2
    across = swap_dp(part, 2, dp_size)
    half = jnp.stack([jnp.where(side == 0, part, across), jnp.where(side == 0, across, part)]).reshape(
        count // 2, width
    )
    beside = swap_dp(half, 1, dp_size)
    whole = jnp.zeros((2, count // 2, width), F32)
    whole = lax.dynamic_update_slice_in_dim(whole, half.astype(F32)[None], core, 0)
    whole = lax.dynamic_update_slice_in_dim(whole, beside.astype(F32)[None], 1 - core, 0)
    return whole.reshape(count, width)


def reduce_vector(values, dp_size):
    total = values
    bit = 1
    while bit < dp_size:
        total = add(total, swap_dp(total, bit, dp_size))
        bit *= 2
    total = add(total, swap_fsdp(total))
    count = values.shape[1] // 2
    return lax.dynamic_slice_in_dim(total, lax.axis_index("fsdp") * count, count, 1)


def pair_transfers(dp_size):
    def gather_gains(gains):
        other = swap_fsdp(gains)
        first = lax.axis_index("fsdp") == 0
        return jnp.concatenate([jnp.where(first, gains, other), jnp.where(first, other, gains)], axis=1)

    return (
        lambda shard: gather_rows(shard, dp_size),
        gather_gains,
        lambda grad: reduce_rows(grad, dp_size),
        lambda grads: reduce_vector(grads, dp_size),
    )


def native_transfers():
    def reduce_over(axis):
        def reduce(grad):
            part = lax.psum_scatter(grad, "fsdp", scatter_dimension=axis, tiled=True)
            return lax.psum(part, "dp").astype(F32)

        return reduce

    return (
        lambda shard: lax.all_gather(shard, "fsdp", axis=0, tiled=True),
        lambda gains: lax.all_gather(gains, "fsdp", axis=1, tiled=True),
        reduce_over(0),
        reduce_over(1),
    )


def make_body(fsdp_size, dp_size):
    if fsdp_size == 2 and dp_size >= 4 and dp_size & (dp_size - 1) == 0:
        gather, gather_gains, reduce, reduce_gains = pair_transfers(dp_size)
    else:
        gather, gather_gains, reduce, reduce_gains = native_transfers()

    def body(
        activations, doc_ids, w_query, key_projection, value_projection, w_out,
        gain_attn, gain_ffn, w_gate, w_up, w_down, cotangent,
    ):
        gains = gather_gains(jnp.stack([gain_attn, gain_ffn])).astype(F32)
        weights = (
            gather(jnp.concatenate([w_query, key_projection, value_projection], axis=1)),
            gather(w_out),
            gather(w_gate),
            gather(w_up),
            gather(w_down),
        )
        tables = doc_tables(doc_ids[0])
        middle, first_kept = layer_forward(activations[0].astype(F32), weights, gains, tables)
        outputs, second_kept = layer_forward(middle, weights, gains, tables)
        grad, second_gains, second_products = layer_backward(
            second_kept, cotangent[0].astype(F32), weights, gains, tables
        )
        grad, first_gains, first_products = layer_backward(first_kept, grad, weights, gains, tables)
        axes = ((0, 0), (0, 0), (0, 0), (1, 0), (0, 1))
        reduced = []
        for contract, (left, right), (more_left, more_right) in zip(axes, second_products, first_products):
            total = dot(left, right, contract) + dot(more_left, more_right, contract)
            reduced.append(reduce(total.astype(BF16)))
        grad_down, grad_gate, grad_up, grad_out, grad_qkv = reduced
        gain_grads = jnp.stack([a + b for a, b in zip(second_gains, first_gains)]).astype(BF16)
        gain_grads = reduce_gains(gain_grads).astype(F32)
        width = w_query.shape[1]
        key_end = width + key_projection.shape[1]
        return (
            outputs.astype(BF16)[None],
            grad.astype(BF16)[None],
            grad_qkv[:, :width],
            grad_qkv[:, width:key_end],
            grad_qkv[:, key_end:],
            grad_out,
            gain_grads[0],
            gain_grads[1],
            grad_gate,
            grad_up,
            grad_down,
        )

    return body


def solution(mesh):
    sequences = P(("dp", "fsdp"), None, None)
    rows = P("fsdp", None)
    vector = P("fsdp")
    in_specs = (
        sequences, P(("dp", "fsdp"), None), rows, rows, rows, rows, vector, vector, rows, rows, rows, sequences,
    )
    out_specs = (sequences, sequences, rows, rows, rows, rows, vector, vector, rows, rows, rows)
    body = make_body(mesh.shape["fsdp"], mesh.shape["dp"])
    return jax.shard_map(body, mesh=mesh, in_specs=in_specs, out_specs=out_specs, check_vma=False)
```

```python
from functools import partial

import jax
import jax.numpy as jnp
from jax import lax
from jax.experimental import pallas as pl
from jax.experimental.pallas import tpu as pltpu
from jax.sharding import PartitionSpec as P

QUERY_HEADS = 15
KEY_VALUE_HEADS = 5
GROUP = QUERY_HEADS // KEY_VALUE_HEADS
HEAD_SIZE = 64
HALF = HEAD_SIZE // 2
LONGEST_DOC = 384
EPSILON = 1e-05
ROPE_BASE = 10000.0
NEGATIVE = -1e30
SCALE = HEAD_SIZE ** (-0.5)
QUERY_BLOCK = 128
BF16 = jnp.bfloat16
F32 = jnp.float32
HBM = pltpu.HBM
FFN_GRANT = 24 << 20
BACK_GRANT = 40 << 20
GRAD_GRANT = 24 << 20
MIXED_GRANT = 36 << 20


def dot(left, right, contract):
    return lax.dot_general(left, right, ((contract[:1], contract[1:]), ((), ())), preferred_element_type=F32)


def key_window(block):
    return (max(0, block * QUERY_BLOCK - LONGEST_DOC), (block + 1) * QUERY_BLOCK)


def fill_mask(start_ref, mask_ref):
    for block in range(mask_ref.shape[0] // QUERY_BLOCK):
        low, high = key_window(block)
        cols = slice(block * QUERY_BLOCK, high)
        shape = (high - low, QUERY_BLOCK)
        key = low + lax.broadcasted_iota(jnp.int32, shape, 0)
        query = block * QUERY_BLOCK + lax.broadcasted_iota(jnp.int32, shape, 1)
        allowed = (key >= start_ref[:, cols]) & (key <= query)
        mask_ref[low:high, cols] = jnp.where(allowed, 0.0, NEGATIVE)


def side_by_side(ref, cols):
    return jnp.concatenate([ref[j * HEAD_SIZE : (j + 1) * HEAD_SIZE, cols] for j in range(GROUP)], axis=1)


def attention_kernel(start_ref, query_ref, key_ref, value_ref, mix_ref, logsum_ref, mask_ref, key_rows_ref):
    @pl.when(pl.program_id(0) == 0)
    def _():
        fill_mask(start_ref, mask_ref)

    key_rows_ref[...] = key_ref[...].T
    for block in range(query_ref.shape[1] // QUERY_BLOCK):
        low, high = key_window(block)
        cols = slice(block * QUERY_BLOCK, high)
        queries = side_by_side(query_ref, cols)
        mask = jnp.concatenate([mask_ref[low:high, cols]] * GROUP, axis=1)
        scores = dot(key_rows_ref[low:high, :], queries, (1, 0)) * SCALE + mask
        top = jnp.max(scores, axis=0, keepdims=True)
        weights = jnp.exp(scores - top)
        total = jnp.sum(weights, axis=0, keepdims=True)
        mix = dot(value_ref[:, low:high], weights.astype(BF16), (1, 0))
        mix = (mix / total).astype(BF16)
        logsum = top + jnp.log(total)
        for j in range(GROUP):
            part = slice(j * QUERY_BLOCK, (j + 1) * QUERY_BLOCK)
            mix_ref[j * HEAD_SIZE : (j + 1) * HEAD_SIZE, cols] = mix[:, part]
            logsum_ref[0, j : j + 1, cols] = logsum[:, part]


def attention(start, qkv):
    length = qkv.shape[1]
    rows = GROUP * HEAD_SIZE
    return pl.pallas_call(
        attention_kernel,
        grid=(KEY_VALUE_HEADS,),
        in_specs=[
            pl.BlockSpec((1, length), lambda g: (0, 0)),
            pl.BlockSpec((rows, length), lambda g: (g, 0)),
            pl.BlockSpec((HEAD_SIZE, length), lambda g: (QUERY_HEADS + g, 0)),
            pl.BlockSpec((HEAD_SIZE, length), lambda g: (QUERY_HEADS + KEY_VALUE_HEADS + g, 0)),
        ],
        out_specs=[
            pl.BlockSpec((rows, length), lambda g: (g, 0)),
            pl.BlockSpec((1, 8, length), lambda g: (g, 0, 0)),
        ],
        out_shape=[
            jax.ShapeDtypeStruct((QUERY_HEADS * HEAD_SIZE, length), BF16),
            jax.ShapeDtypeStruct((KEY_VALUE_HEADS, 8, length), F32),
        ],
        scratch_shapes=[pltpu.VMEM((length, length), F32), pltpu.VMEM((length, HEAD_SIZE), BF16)],
        compiler_params=pltpu.CompilerParams(vmem_limit_bytes=8 << 20),
        cost_estimate=pl.CostEstimate(flops=6_000_000_000, bytes_accessed=4_000_000, transcendentals=4_500_000),
        name="attention",
    )(start, qkv, qkv, qkv)


def unrotate(rows, cosine, sine):
    first = rows[:HALF]
    second = rows[HALF:]
    return (first * cosine + second * sine, second * cosine - first * sine)


def attention_back_kernel(
    start_ref, cosine_ref, sine_ref, query_ref, key_ref, value_ref, mix_ref, logsum_ref, mix_grad_ref,
    out_ref, mask_ref, key_rows_ref, value_rows_ref, key_grad_ref, value_grad_ref,
):
    group = pl.program_id(0)

    @pl.when(group == 0)
    def _():
        fill_mask(start_ref, mask_ref)

    key_rows_ref[...] = key_ref[...].T
    value_rows_ref[...] = value_ref[...].T
    key_grad_ref[...] = jnp.zeros_like(key_grad_ref)
    value_grad_ref[...] = jnp.zeros_like(value_grad_ref)
    for block in range(query_ref.shape[1] // QUERY_BLOCK):
        low, high = key_window(block)
        cols = slice(block * QUERY_BLOCK, high)
        queries = side_by_side(query_ref, cols)
        mix_grads = side_by_side(mix_grad_ref, cols)
        mixes = side_by_side(mix_ref, cols)
        inner = jnp.sum(mix_grads.astype(F32) * mixes.astype(F32), axis=0, keepdims=True)
        logsum = jnp.concatenate([logsum_ref[0, j : j + 1, cols] for j in range(GROUP)], axis=1)
        mask = jnp.concatenate([mask_ref[low:high, cols]] * GROUP, axis=1)
        scores = dot(key_rows_ref[low:high, :], queries, (1, 0)) * SCALE + mask
        weights = jnp.exp(scores - logsum)
        weight_grads = dot(value_rows_ref[low:high, :], mix_grads, (1, 0))
        score_grads = (weights * (weight_grads - inner)).astype(BF16)
        value_grad_ref[:, low:high] += dot(mix_grads, weights.astype(BF16), (1, 1))
        key_grad_ref[:, low:high] += dot(queries, score_grads, (1, 1))
        query_grads = dot(key_ref[:, low:high], score_grads, (1, 0)) * SCALE
        cosine = cosine_ref[:, cols]
        sine = sine_ref[:, cols]
        for j in range(GROUP):
            first, second = unrotate(query_grads[:, j * QUERY_BLOCK : (j + 1) * QUERY_BLOCK], cosine, sine)
            base = group * (GROUP * HEAD_SIZE) + j * HEAD_SIZE
            out_ref[pl.ds(pl.multiple_of(base, HALF), HALF), cols] = first.astype(BF16)
            out_ref[pl.ds(pl.multiple_of(base + HALF, HALF), HALF), cols] = second.astype(BF16)
    first, second = unrotate(key_grad_ref[...] * SCALE, cosine_ref[...], sine_ref[...])
    base = (QUERY_HEADS + group) * HEAD_SIZE
    out_ref[pl.ds(pl.multiple_of(base, HALF), HALF), :] = first.astype(BF16)
    out_ref[pl.ds(pl.multiple_of(base + HALF, HALF), HALF), :] = second.astype(BF16)
    base = (QUERY_HEADS + KEY_VALUE_HEADS + group) * HEAD_SIZE
    out_ref[pl.ds(pl.multiple_of(base, HEAD_SIZE), HEAD_SIZE), :] = value_grad_ref[...].astype(BF16)


def attention_back(start, cosine, sine, qkv, mix, logsum, mix_grad):
    length = qkv.shape[1]
    rows = GROUP * HEAD_SIZE
    return pl.pallas_call(
        attention_back_kernel,
        grid=(KEY_VALUE_HEADS,),
        in_specs=[
            pl.BlockSpec((1, length), lambda g: (0, 0)),
            pl.BlockSpec((HALF, length), lambda g: (0, 0)),
            pl.BlockSpec((HALF, length), lambda g: (0, 0)),
            pl.BlockSpec((rows, length), lambda g: (g, 0)),
            pl.BlockSpec((HEAD_SIZE, length), lambda g: (QUERY_HEADS + g, 0)),
            pl.BlockSpec((HEAD_SIZE, length), lambda g: (QUERY_HEADS + KEY_VALUE_HEADS + g, 0)),
            pl.BlockSpec((rows, length), lambda g: (g, 0)),
            pl.BlockSpec((1, 8, length), lambda g: (g, 0, 0)),
            pl.BlockSpec((rows, length), lambda g: (g, 0)),
        ],
        out_specs=pl.BlockSpec(qkv.shape, lambda g: (0, 0)),
        out_shape=jax.ShapeDtypeStruct(qkv.shape, BF16),
        scratch_shapes=[
            pltpu.VMEM((length, length), F32),
            pltpu.VMEM((length, HEAD_SIZE), BF16),
            pltpu.VMEM((length, HEAD_SIZE), BF16),
            pltpu.VMEM((HEAD_SIZE, length), F32),
            pltpu.VMEM((HEAD_SIZE, length), F32),
        ],
        compiler_params=pltpu.CompilerParams(vmem_limit_bytes=8 << 20),
        cost_estimate=pl.CostEstimate(flops=9_000_000_000, bytes_accessed=9_000_000, transcendentals=4_500_000),
        name="attention_back",
    )(start, cosine, sine, qkv, qkv, qkv, mix, logsum, mix_grad)


ROWS = 256
CHUNK = 512


def row_tiles(count):
    return [slice(row, row + ROWS) for row in range(0, count, ROWS)]


def whole(shape):
    return pl.BlockSpec(shape, lambda k: (0,) * len(shape))


def by_cols(rows):
    return pl.BlockSpec((rows, CHUNK), lambda k: (0, k))


def ffn_kernel(
    middle_ref, gain_ref, gate_w_ref, up_w_ref, down_w_ref,
    out_ref, normed_t_ref, gate_ref, up_ref, hidden_ref, normed_ref,
):
    tiles = row_tiles(middle_ref.shape[1])

    @pl.when(pl.program_id(0) == 0)
    def _():
        for cols in tiles:
            middle = middle_ref[:, cols]
            inverse = lax.rsqrt(jnp.mean(middle * middle, axis=0, keepdims=True) + EPSILON)
            normed = (middle * inverse * gain_ref[...]).astype(BF16)
            normed_t_ref[:, cols] = normed
            normed_ref[cols, :] = normed.T
            out_ref[:, cols] = middle

    for rows in tiles:
        normed = normed_ref[rows, :]
        gate = dot(normed, gate_w_ref[...], (1, 0))
        up = dot(normed, up_w_ref[...], (1, 0))
        gate_ref[rows, :] = gate.astype(BF16)
        up_ref[rows, :] = up.astype(BF16)
        hidden = (gate * jax.nn.sigmoid(gate) * up).astype(BF16)
        hidden_ref[rows, :] = hidden
    out_ref[...] += dot(down_w_ref[...], hidden_ref[...], (1, 1))


def ffn(middle, gain, w_gate, w_up, w_down_t):
    width, length = middle.shape
    hidden = w_gate.shape[1]
    return pl.pallas_call(
        ffn_kernel,
        grid=(hidden // CHUNK,),
        in_specs=[whole((width, length)), whole((width, 1)), by_cols(width), by_cols(width), by_cols(width)],
        out_specs=[whole((width, length)), whole((width, length)), by_cols(length), by_cols(length), by_cols(length)],
        out_shape=[
            jax.ShapeDtypeStruct((width, length), F32),
            HBM((width, length), BF16),
            HBM((length, hidden), BF16),
            HBM((length, hidden), BF16),
            HBM((length, hidden), BF16),
        ],
        scratch_shapes=[pltpu.VMEM((length, width), BF16)],
        compiler_params=pltpu.CompilerParams(vmem_limit_bytes=FFN_GRANT),
        cost_estimate=pl.CostEstimate(
            flops=6 * length * width * hidden, bytes_accessed=40_000_000, transcendentals=length * hidden
        ),
        name="ffn",
    )(middle, gain, w_gate, w_up, w_down_t)


def ffn_up_kernel(
    middle_ref, gain_ref, gate_w_ref, up_w_ref, normed_t_ref, gate_ref, up_ref, hidden_ref, normed_ref,
):
    tiles = row_tiles(middle_ref.shape[1])

    @pl.when(pl.program_id(0) == 0)
    def _():
        for cols in tiles:
            middle = middle_ref[:, cols]
            inverse = lax.rsqrt(jnp.mean(middle * middle, axis=0, keepdims=True) + EPSILON)
            normed = (middle * inverse * gain_ref[...]).astype(BF16)
            normed_t_ref[:, cols] = normed
            normed_ref[cols, :] = normed.T

    for rows in tiles:
        normed = normed_ref[rows, :]
        gate = dot(normed, gate_w_ref[...], (1, 0))
        up = dot(normed, up_w_ref[...], (1, 0))
        gate_ref[rows, :] = gate.astype(BF16)
        up_ref[rows, :] = up.astype(BF16)
        hidden_ref[rows, :] = (gate * jax.nn.sigmoid(gate) * up).astype(BF16)


def ffn_up(middle, gain, w_gate, w_up):
    width, length = middle.shape
    hidden = w_gate.shape[1]
    return pl.pallas_call(
        ffn_up_kernel,
        grid=(hidden // CHUNK,),
        in_specs=[whole((width, length)), whole((width, 1)), by_cols(width), by_cols(width)],
        out_specs=[whole((width, length)), by_cols(length), by_cols(length), by_cols(length)],
        out_shape=[HBM((width, length), BF16)] + [HBM((length, hidden), BF16)] * 3,
        scratch_shapes=[pltpu.VMEM((length, width), BF16)],
        compiler_params=pltpu.CompilerParams(vmem_limit_bytes=FFN_GRANT),
        cost_estimate=pl.CostEstimate(
            flops=4 * length * width * hidden, bytes_accessed=30_000_000, transcendentals=length * hidden
        ),
        name="ffn_up",
    )(middle, gain, w_gate, w_up)


def ffn_back_kernel(
    grad_ref, middle_ref, gain_ref, gate_ref, up_ref, gate_w_ref, up_w_ref, down_w_ref,
    out_ref, out_narrow_ref, gate_grad_ref, up_grad_ref, gain_grad_ref, branch_t_ref, total_ref, branch_ref,
):
    step = pl.program_id(0)
    tiles = row_tiles(middle_ref.shape[1])

    @pl.when(step == 0)
    def _():
        for cols in tiles:
            branch = grad_ref[:, cols].astype(BF16)
            branch_t_ref[:, cols] = branch
            branch_ref[cols, :] = branch.T

    for rows in tiles:
        hidden_grad = dot(branch_ref[rows, :], down_w_ref[...], (1, 0))
        gate = gate_ref[rows, :].astype(F32)
        up = up_ref[rows, :].astype(F32)
        sigmoid = jax.nn.sigmoid(gate)
        scaled = hidden_grad * sigmoid
        up_grad = (scaled * gate).astype(BF16)
        gate_grad = (scaled * up * (1.0 + gate * (1.0 - sigmoid))).astype(BF16)
        gate_grad_ref[rows, :] = gate_grad
        up_grad_ref[rows, :] = up_grad
    part = dot(gate_w_ref[...], gate_grad_ref[...], (1, 1)) + dot(up_w_ref[...], up_grad_ref[...], (1, 1))

    @pl.when(step == 0)
    def _():
        total_ref[...] = part

    @pl.when(step > 0)
    def _():
        total_ref[...] += part

    @pl.when(step == pl.num_programs(0) - 1)
    def _():
        gain_grad = jnp.zeros(gain_ref.shape, F32)
        for cols in tiles:
            middle = middle_ref[:, cols]
            normed_grad = total_ref[:, cols]
            inverse = lax.rsqrt(jnp.mean(middle * middle, axis=0, keepdims=True) + EPSILON)
            unit = middle * inverse
            gain_grad += jnp.sum(normed_grad * unit, axis=1, keepdims=True)
            scaled = gain_ref[...] * normed_grad
            inner = jnp.mean(scaled * unit, axis=0, keepdims=True)
            out = grad_ref[:, cols] + inverse * (scaled - unit * inner)
            out_ref[:, cols] = out
            out_narrow_ref[:, cols] = out.astype(BF16)
        gain_grad_ref[...] = gain_grad


def ffn_back(grad, middle, gain, gate, up, w_gate, w_up, w_down_t):
    width, length = middle.shape
    hidden = w_gate.shape[1]
    full = whole((width, length))
    return pl.pallas_call(
        ffn_back_kernel,
        grid=(hidden // CHUNK,),
        in_specs=[
            full, full, whole((width, 1)), by_cols(length), by_cols(length), by_cols(width), by_cols(width), by_cols(width),
        ],
        out_specs=[full, full, by_cols(length), by_cols(length), whole((width, 1)), full],
        out_shape=[
            HBM((width, length), F32),
            jax.ShapeDtypeStruct((width, length), BF16),
            HBM((length, hidden), BF16),
            HBM((length, hidden), BF16),
            jax.ShapeDtypeStruct((width, 1), F32),
            HBM((width, length), BF16),
        ],
        scratch_shapes=[pltpu.VMEM((width, length), F32), pltpu.VMEM((length, width), BF16)],
        compiler_params=pltpu.CompilerParams(vmem_limit_bytes=BACK_GRANT),
        cost_estimate=pl.CostEstimate(
            flops=6 * length * width * hidden, bytes_accessed=50_000_000, transcendentals=length * hidden
        ),
        name="ffn_back",
    )(grad, middle, gain, gate, up, w_gate, w_up, w_down_t)


def weight_grad_kernel(left_fsdp, transposed, places_ref, left_ref, right_ref, left2_ref, right2_ref, keep_ref, send_ref):
    step = pl.program_id(0)
    contract = (1, 1) if transposed else (1, 0)
    total = dot(left_ref[...], right_ref[...], contract) + dot(left2_ref[...], right2_ref[...], contract)
    total = total.astype(BF16)
    half = total.shape[0] // 2
    fsdp, core = places_ref[0], places_ref[1]
    if left_fsdp:
        for out_ref, here in ((keep_ref, step < 2), (send_ref, step >= 2)):

            @pl.when(here)
            def _():
                out_ref[fsdp] = total[:half]
                out_ref[1 - fsdp] = total[half:]

    else:
        for out_ref, first in ((keep_ref, core), (send_ref, 1 - core)):

            @pl.when(first == 0)
            def _():
                out_ref[0] = total[:half]

            @pl.when(first == 1)
            def _():
                out_ref[0] = total[half:]


def weight_grad(places, products, more_products, left_fsdp):
    left, right = products
    left2, right2 = more_products
    rows, length = left.shape
    cols = right.shape[1]
    block = cols // 4
    left_spec = pl.BlockSpec((rows, length), lambda j, places: (0, 0))
    if left_fsdp:
        right_spec = pl.BlockSpec((length, block), lambda j, places: (0, (2 * places[1] + j) % 4))
        keep_spec = pl.BlockSpec((2, rows // 2, block), lambda j, places: (0, 0, jnp.minimum(j, 1)))
        send_spec = pl.BlockSpec((2, rows // 2, block), lambda j, places: (0, 0, jnp.maximum(j - 2, 0)))
    else:
        right_spec = pl.BlockSpec((length, block), lambda j, places: (0, (2 * places[0] + j) % 4))
        keep_spec = pl.BlockSpec((1, rows // 2, block), lambda j, places: (j // 2, 0, j % 2))
        send_spec = keep_spec
    return pl.pallas_call(
        partial(weight_grad_kernel, left_fsdp, False),
        grid_spec=pltpu.PrefetchScalarGridSpec(
            num_scalar_prefetch=1,
            grid=(4,),
            in_specs=[left_spec, right_spec, left_spec, right_spec],
            out_specs=[keep_spec, send_spec],
        ),
        out_shape=[jax.ShapeDtypeStruct((2, rows // 2, cols // 2), BF16)] * 2,
        compiler_params=pltpu.CompilerParams(vmem_limit_bytes=GRAD_GRANT),
        cost_estimate=pl.CostEstimate(
            flops=4 * rows * length * cols, bytes_accessed=10 * rows * cols, transcendentals=0
        ),
        name="weight_grad",
    )(places, left, right, left2, right2)


def mixed_grad_kernel(
    places_ref, mix_ref, branch_ref, normed_ref, qkv_ref, mix2_ref, branch2_ref, normed2_ref, qkv2_ref,
    keep_ref, send_ref,
):
    width = branch_ref.shape[0]
    half_cols = keep_ref.shape[2]
    out_part = dot(mix_ref[...], branch_ref[...], (1, 1)) + dot(mix2_ref[...], branch2_ref[...], (1, 1))
    qkv_part = dot(normed_ref[...], qkv_ref[...], (1, 1)) + dot(normed2_ref[...], qkv2_ref[...], (1, 1))
    out_part = out_part.astype(BF16)
    qkv_part = qkv_part.astype(BF16)
    first = half_cols - width
    core = places_ref[1]
    for low_ref, high_ref, here in ((keep_ref, send_ref, core == 0), (send_ref, keep_ref, core == 1)):

        @pl.when(here)
        def _():
            low_ref[0, :, :width] = out_part
            low_ref[0, :, width:] = qkv_part[:, :first]
            high_ref[0] = qkv_part[:, first:]


def mixed_grad(places, products, more_products):
    (mix, branch), (normed, qkv) = products
    (mix2, branch2), (normed2, qkv2) = more_products
    rows, length = mix.shape
    cols = branch.shape[0] + qkv.shape[0]
    left = pl.BlockSpec((rows // 2, length), lambda j, places: ((places[0] + j) % 2, 0))
    fixed = lambda shape: pl.BlockSpec(shape, lambda j, places: (0, 0))
    specs = [left, fixed(branch.shape), left, fixed(qkv.shape)]
    return pl.pallas_call(
        mixed_grad_kernel,
        grid_spec=pltpu.PrefetchScalarGridSpec(
            num_scalar_prefetch=1,
            grid=(2,),
            in_specs=specs + specs,
            out_specs=[pl.BlockSpec((1, rows // 2, cols // 2), lambda j, places: (j, 0, 0))] * 2,
        ),
        out_shape=[jax.ShapeDtypeStruct((2, rows // 2, cols // 2), BF16)] * 2,
        compiler_params=pltpu.CompilerParams(vmem_limit_bytes=MIXED_GRANT),
        cost_estimate=pl.CostEstimate(
            flops=4 * rows * length * cols, bytes_accessed=10 * rows * cols, transcendentals=0
        ),
        name="mixed_grad",
    )(places, mix, branch, normed, qkv, mix2, branch2, normed2, qkv2)


def assemble_kernel(stack_cores, cuts, places_ref, *refs):
    core, side = places_ref[1], places_ref[2]
    inputs, outputs = refs[:4], refs[4:]
    count, cols = inputs[0].shape
    whole_ref = outputs[-1]
    for k, piece_ref in enumerate(inputs):
        at_side = jnp.bitwise_xor(side, k % 2)
        at_core = jnp.bitwise_xor(core, k // 2)
        row = at_side * count + (at_core * (2 * count) if stack_cores else 0)
        rows = pl.ds(pl.multiple_of(row, 8), count)
        value = piece_ref[...].astype(F32)
        if stack_cores:
            whole_ref[rows, :] = value
        else:
            whole_ref[rows, pl.ds(pl.multiple_of(at_core * cols, 128), cols)] = value
    for out_ref, (low, high) in zip(outputs[:-1], cuts):
        out_ref[...] = whole_ref[:, low:high]


def assemble(places, pieces, stack_cores, cuts=()):
    count, cols = pieces[0].shape
    shape = (4 * count, cols) if stack_cores else (2 * count, 2 * cols)
    out_shape = [jax.ShapeDtypeStruct((shape[0], high - low), F32) for low, high in cuts]
    out_shape = out_shape or [jax.ShapeDtypeStruct(shape, F32)]
    return pl.pallas_call(
        partial(assemble_kernel, stack_cores, cuts),
        grid_spec=pltpu.PrefetchScalarGridSpec(
            num_scalar_prefetch=1,
            grid=(1,),
            in_specs=[pl.BlockSpec((count, cols), lambda j, places: (0, 0))] * 4,
            out_specs=[pl.BlockSpec(out.shape, lambda j, places: (0, 0)) for out in out_shape],
            scratch_shapes=[pltpu.VMEM(shape, F32)] if cuts else [],
        ),
        out_shape=out_shape,
        compiler_params=pltpu.CompilerParams(vmem_limit_bytes=24 << 20),
        cost_estimate=pl.CostEstimate(flops=0, bytes_accessed=24 * count * cols, transcendentals=0),
        name="assemble",
    )(places, *pieces)


def doc_tables(doc_row):
    token_index = jnp.arange(doc_row.shape[0])
    start = jnp.sum((doc_row[:, None] < doc_row[None, :]).astype(jnp.int32), axis=0)
    places = (token_index - start).astype(F32)
    frequency = ROPE_BASE ** (-2.0 * jnp.arange(HALF, dtype=F32) / HEAD_SIZE)
    angles = frequency[:, None] * places[None, :]
    return (start[None, :], jnp.cos(angles), jnp.sin(angles))


def norm_forward(inputs, gain):
    inverse = lax.rsqrt(jnp.mean(inputs * inputs, axis=0, keepdims=True) + EPSILON)
    return (inputs * inverse * gain).astype(BF16)


def norm_backward(inputs, gain, grad):
    inverse = lax.rsqrt(jnp.mean(inputs * inputs, axis=0, keepdims=True) + EPSILON)
    scaled = gain * grad
    inner = jnp.mean(scaled * inputs, axis=0, keepdims=True)
    return (inverse * scaled - inputs * inverse**3 * inner, jnp.sum(grad * inputs * inverse, axis=1, keepdims=True))


def project(inputs, w_qkv, gains, tables):
    _, cosine, sine = tables
    length = inputs.shape[1]
    normed = norm_forward(inputs, gains[0])
    raw = dot(w_qkv, normed, (0, 0))
    heads = QUERY_HEADS + KEY_VALUE_HEADS
    pairs = raw[: heads * HEAD_SIZE].reshape(heads, 2, HALF, length)
    first, second = pairs[:, 0], pairs[:, 1]
    rotated = jnp.stack([first * cosine - second * sine, second * cosine + first * sine], axis=1)
    qkv = jnp.concatenate(
        [rotated.reshape(heads * HEAD_SIZE, length).astype(BF16), raw[heads * HEAD_SIZE :].astype(BF16)], axis=0
    )
    return (normed, qkv)


def project_out(inputs, w_out, mix):
    return inputs + dot(w_out, mix, (0, 0))


def attention_backward(kept, attn_grad, weights, tables):
    start, cosine, sine = tables
    _, _, qkv, logsum, mix = kept
    mix_grad = dot(weights[1], attn_grad, (1, 0)).astype(BF16)
    return attention_back(start, cosine, sine, qkv, mix, logsum, mix_grad)


def input_backward(kept, middle_grad, qkv_grad, weights, gains):
    normed_grad = dot(weights[0], qkv_grad, (1, 0))
    inputs_grad, gain_grad = norm_backward(kept[0], gains[0], normed_grad)
    return (inputs_grad + middle_grad, gain_grad)


def after(value, *earlier):
    return lax.optimization_barrier((value,) + earlier)[0]


def swap_fsdp(value):
    return lax.ppermute(value, "fsdp", [(0, 1), (1, 0)])


def swap_dp(value, bit, size=16):
    return lax.ppermute(value, "dp", [(i, i ^ bit) for i in range(size)])


def fetch(parts, axis, index, pieces):
    sent = [cut_piece(part, index, axis, pieces) for part in parts]
    sent = jnp.concatenate(sent, axis=1) if len(sent) > 1 else sent[0]
    return sent


def cut_piece(value, index, axis, pieces):
    count = value.shape[axis] // pieces
    return lax.dynamic_slice_in_dim(value, index * count, count, axis)


def join_kernel(own_count, shard_axis, piece_axis, index_at, places_ref, *refs):
    own, pieces, out_ref = refs[:own_count], refs[own_count:-1], refs[-1]
    rows, cols = out_ref.shape
    fsdp = places_ref[0]
    index = places_ref[index_at]
    if shard_axis == 0:
        half = pl.ds(pl.multiple_of(fsdp * (rows // 2), 16), rows // 2)
        at = 0
        for ref in own:
            out_ref[half, at : at + ref.shape[1]] = ref[...]
            at += ref.shape[1]
    else:
        out_ref[:, pl.ds(pl.multiple_of(fsdp * (cols // 2), 128), cols // 2)] = own[0][...]
    for flip, ref in enumerate(pieces):
        at = jnp.bitwise_xor(index, flip)
        count, width = ref.shape
        row = at * count if piece_axis == 0 else 0
        col = at * width if piece_axis == 1 else 0
        if shard_axis == 0:
            row = row + (1 - fsdp) * (rows // 2)
        else:
            col = col + (1 - fsdp) * (cols // 2)
        row_at = pl.ds(pl.multiple_of(row, 16), count)
        if shard_axis == 0 and piece_axis == 0:
            out_ref[row_at, :] = ref[...]
        else:
            out_ref[row_at, pl.ds(pl.multiple_of(col, 128), width)] = ref[...]


def join(places, own, pieces, shard_axis, piece_axis, index_at):
    rows, cols = own[0].shape[0], sum(part.shape[1] for part in own)
    shape = (2 * rows, cols) if shard_axis == 0 else (rows, 2 * cols)
    full = lambda shape: pl.BlockSpec(shape, lambda j, places: (0, 0))
    return pl.pallas_call(
        partial(join_kernel, len(own), shard_axis, piece_axis, index_at),
        grid_spec=pltpu.PrefetchScalarGridSpec(
            num_scalar_prefetch=1,
            grid=(1,),
            in_specs=[full(part.shape) for part in (*own, *pieces)],
            out_specs=full(shape),
        ),
        out_shape=jax.ShapeDtypeStruct(shape, BF16),
        compiler_params=pltpu.CompilerParams(vmem_limit_bytes=24 << 20),
        cost_estimate=pl.CostEstimate(flops=0, bytes_accessed=4 * shape[0] * shape[1], transcendentals=0),
        name="join",
    )(places, *own, *pieces)


def add(left, right):
    return (left.astype(F32) + right.astype(F32)).astype(BF16)


def add3(first, second, third):
    return ((first.astype(F32) + second.astype(F32)) + third.astype(F32)).astype(BF16)


def reduce_vector(values):
    total = values
    for bit in (1, 2, 4, 8):
        total = add(total, swap_dp(total, bit))
    total = add(total, swap_fsdp(total))
    count = values.shape[1] // 2
    return lax.dynamic_slice_in_dim(total, lax.axis_index("fsdp") * count, count, 1)


def gather_gains(gains):
    other = swap_fsdp(gains)
    first = lax.axis_index("fsdp") == 0
    return jnp.concatenate([jnp.where(first, gains, other), jnp.where(first, other, gains)], axis=1)


def cut(value, which, axis):
    count = value.shape[axis] // 2
    return lax.dynamic_slice_in_dim(value, which * count, count, axis)


class Reduction:
    def __init__(self, halves):
        self.keep, send = halves
        self.received = swap_dp(send, 1)
        place = lax.axis_index("dp")
        self.side, self.lane = (place // 2) % 2, (place // 4) % 2
        self.stage = 0

    def step(self, queue):
        gate = lambda value: after(value, *queue)
        self.stage += 1
        if self.stage == 1:
            mine = add(gate(self.keep)[1], self.received[1])
            self.incoming = swap_fsdp(mine)
        elif self.stage == 2:
            half = add3(gate(self.keep)[0], self.received[0], self.incoming)
            mine, self.own = cut(half, 1 - self.side, 0), cut(half, self.side, 0)
            self.incoming = swap_dp(mine, 2)
        elif self.stage == 3:
            part = add(gate(self.own), self.incoming)
            mine, self.own = cut(part, 1 - self.lane, 1), cut(part, self.lane, 1)
            self.incoming = swap_dp(mine, 4)
        elif self.stage in (4, 5):
            mine = self.own = add(gate(self.own), self.incoming)
            self.incoming = swap_dp(mine, 8 if self.stage == 4 else 4)
        elif self.stage == 6:
            own = gate(self.own)
            low = jnp.where(self.lane == 0, own, self.incoming)
            high = jnp.where(self.lane == 0, self.incoming, own)
            mine = self.own = jnp.concatenate([low, high], axis=1)
            self.across = swap_dp(mine, 2)
            self.beside = swap_dp(mine, 1)
        else:
            mine = gate(self.across)
            self.pieces = (self.own, mine, self.beside, swap_dp(mine, 1))
        queue[:] = [mine]
        return mine


def make_body(fsdp_size, dp_size):
    paired = fsdp_size == 2 and dp_size == 16

    def body(
        activations, doc_ids, w_query, key_projection, value_projection, w_out,
        gain_attn, gain_ffn, w_gate, w_up, w_down, cotangent,
    ):
        if paired:
            place = lax.axis_index("dp")
            core, side, lane = place % 2, (place // 2) % 2, (place // 4) % 2
            index_y, index_z = place % 4, core + 2 * lane
            places = jnp.stack([lax.axis_index("fsdp"), core, side, index_y, index_z]).astype(jnp.int32)
            qkv_own = (w_query, key_projection, value_projection)
            qkv_sent = fetch(qkv_own, 0, core, 2)
            out_sent = fetch((after(w_out, qkv_sent),), 0, core, 2)
            gate_sent = fetch((after(w_gate, out_sent),), 1, index_y, 4)
            up_sent = fetch((after(w_up, gate_sent),), 1, index_z, 4)
            down_sent = fetch((after(w_down.T, up_sent),), 0, index_y, 4)
            qkv_mine = swap_fsdp(qkv_sent)
            gains = gather_gains(after(jnp.stack([gain_attn, gain_ffn]), qkv_sent)).astype(F32)
            out_mine, gate_mine, up_mine, down_mine = [
                swap_fsdp(sent) for sent in (out_sent, gate_sent, up_sent, down_sent)
            ]
            w_qkv = join(places, qkv_own, (qkv_mine, swap_dp(qkv_mine, 1)), 0, 0, 1)
        else:
            collect = lambda shard, axis: lax.all_gather(shard, "fsdp", axis=axis, tiled=True)
            gains = collect(jnp.stack([gain_attn, gain_ffn]), 1).astype(F32)
            places = jnp.zeros((4,), jnp.int32)
            qkv_shard = jnp.concatenate([w_query, key_projection, value_projection], axis=1)
            weights = (
                collect(qkv_shard, 0), collect(w_out, 0), collect(w_gate, 0), collect(w_up, 0), collect(w_down, 0).T,
            )
        gains = (gains[0][:, None], gains[1][:, None])
        tables = doc_tables(doc_ids[0])
        start, cosine, sine = tables
        inputs = activations[0].T.astype(F32)

        if paired:
            normed, qkv = project(inputs, w_qkv, gains, tables)
            out_mine = after(out_mine, qkv)
            gate_mine = after(gate_mine, out_mine)
            out_beside = swap_dp(out_mine, 1)
            gate_across, gate_beside = swap_dp(gate_mine, 2), swap_dp(gate_mine, 1)
            mix, logsum = attention(start, qkv)
            up_mine = after(up_mine, mix)
            up_across, up_beside = swap_dp(up_mine, 4), swap_dp(up_mine, 1)
            gate_across = after(gate_across, up_mine)
            gate_corner = swap_dp(gate_across, 1)
            w_out_full = join(places, (w_out,), (out_mine, out_beside), 0, 0, 1)
            middle = project_out(inputs, w_out_full, mix)
            down_mine = after(down_mine, middle)
            down_across, down_beside = swap_dp(down_mine, 2), swap_dp(down_mine, 1)
            gate_pieces = (after(gate_mine, down_mine), gate_beside, gate_across, gate_corner)
            w_gate_full = join(places, (w_gate,), gate_pieces, 0, 1, 3)
            up_across = after(up_across, w_gate_full)
            w_up_full = join(places, (w_up,), (up_mine, up_beside, up_across, swap_dp(up_across, 1)), 0, 1, 4)
            first_normed, first_gate, first_up, first_hidden = ffn_up(middle, gains[1], w_gate_full, w_up_full)
            down_across = after(down_across, first_hidden)
            w_down_full = join(
                places, (w_down.T,), (down_mine, down_beside, down_across, swap_dp(down_across, 1)), 1, 0, 3
            )
            weights = (w_qkv, w_out_full, w_gate_full, w_up_full, w_down_full)
            ffn_weights = weights[2:]
        else:
            ffn_weights = weights[2:]
            normed, qkv = project(inputs, weights[0], gains, tables)
            mix, logsum = attention(start, qkv)
            middle = project_out(inputs, weights[1], mix)
            first_normed, first_gate, first_up, first_hidden = ffn_up(middle, gains[1], *ffn_weights[:2])
        first = (inputs, normed, qkv, logsum, mix)
        inputs2 = middle + dot(ffn_weights[2], first_hidden, (1, 1))
        normed2, qkv2 = project(inputs2, weights[0], gains, tables)
        mix2, logsum2 = attention(start, qkv2)
        middle2 = project_out(inputs2, weights[1], mix2)
        second = (inputs2, normed2, qkv2, logsum2, mix2)
        outputs, second_normed, second_gate, second_up, second_hidden = ffn(middle2, gains[1], *ffn_weights)

        grad = cotangent[0].T.astype(F32)
        grad, attn_grad2, gate_grad2, up_grad2, ffn_gain2, branch2 = ffn_back(
            grad, middle2, gains[1], second_gate, second_up, *ffn_weights
        )
        qkv_grad2 = attention_backward(second, attn_grad2, weights, tables)
        grad, attn_gain2 = input_backward(second, grad, qkv_grad2, weights, gains)

        down_halves = weight_grad(
            places, (branch2, second_hidden), (grad.astype(BF16), first_hidden), False
        )
        queue = []
        if paired:
            down = Reduction(down_halves)
            grad = after(grad, down.step(queue))
        else:
            grad = after(grad, *down_halves)
        grad, attn_grad, gate_grad, up_grad, ffn_gain, _ = ffn_back(
            grad, middle, gains[1], first_gate, first_up, *ffn_weights
        )
        if paired:
            down.step(queue)
            gate_grad = after(gate_grad, *queue)
        gate_halves = weight_grad(places, (second_normed, gate_grad2), (first_normed, gate_grad), True)
        mix_grad_in = after(attn_grad, *gate_halves)
        mix_grad = dot(weights[1], mix_grad_in, (1, 0)).astype(BF16)
        if paired:
            gate = Reduction(gate_halves)
            queue.append(mix_grad)
            gate.step(queue)
            up_grad = after(up_grad, *queue)
        up_halves = weight_grad(places, (second_normed, up_grad2), (first_normed, up_grad), True)
        if paired:
            queue.append(up_halves[0])
            up = Reduction(up_halves)
            down.step(queue)
            up.step(queue)
            mix_grad = after(mix_grad, *queue)
        qkv_grad = attention_back(start, cosine, sine, first[2], first[4], first[3], mix_grad)
        if paired:
            queue.append(qkv_grad)
            down.step(queue)
            gate.step(queue)
            qkv_grad = after(qkv_grad, *queue)
        mixed_halves = mixed_grad(
            places,
            ((second[4], attn_grad2), (second[1], qkv_grad2)),
            ((first[4], attn_grad), (first[1], qkv_grad)),
        )
        if paired:
            mixed = Reduction(mixed_halves)
            queue.append(mixed_halves[0])
            down.step(queue)
            gate.step(queue)
            up.step(queue)
            mixed.step(queue)
            grad = after(grad, *queue)
        grad, attn_gain = input_backward(first, grad, after(qkv_grad, *mixed_halves), weights, gains)
        gain_grads = jnp.concatenate([attn_gain + attn_gain2, ffn_gain + ffn_gain2], axis=1).T.astype(BF16)

        width = w_query.shape[1]
        key_end = width + key_projection.shape[1]
        value_end = key_end + value_projection.shape[1]
        cuts = ((0, width), (width, 2 * width), (2 * width, width + key_end), (width + key_end, width + value_end))
        if paired:
            queue.append(grad)
            for reduction in (
                down, gate, up, down, gate, up, mixed, gate, up, mixed, gate, up, mixed, mixed, up, mixed, mixed,
            ):
                reduction.step(queue)
            (grad_down,) = assemble(places, down.pieces, True)
            (grad_gate,) = assemble(places, gate.pieces, False)
            (grad_up,) = assemble(places, up.pieces, False)
            grad_out, grad_query, grad_key, grad_value = assemble(places, mixed.pieces, False, cuts)
            gain_grads = reduce_vector(gain_grads).astype(F32)
        else:

            def reduce(value, axis):
                part = lax.psum_scatter(value, "fsdp", scatter_dimension=axis, tiled=True)
                return lax.psum(part, "dp").astype(F32)

            rows = lambda halves: jnp.concatenate([h.reshape(-1, h.shape[2]) for h in halves], axis=1)
            cols = lambda halves: jnp.concatenate([jnp.concatenate([h[0], h[1]], axis=1) for h in halves])
            grad_down = reduce(cols(down_halves).T, 0).T
            grad_gate = reduce(rows(gate_halves), 0)
            grad_up = reduce(rows(up_halves), 0)
            mixed = reduce(rows(mixed_halves), 0)
            grad_out, grad_query, grad_key, grad_value = [mixed[:, low:high] for low, high in cuts]
            gain_grads = reduce(gain_grads, 1)
        return (
            outputs.T.astype(BF16)[None],
            grad.T.astype(BF16)[None],
            grad_query,
            grad_key,
            grad_value,
            grad_out,
            gain_grads[0],
            gain_grads[1],
            grad_gate,
            grad_up,
            grad_down.T,
        )

    return body


def solution(mesh):
    sequences = P(("dp", "fsdp"), None, None)
    rows = P("fsdp", None)
    vector = P("fsdp")
    in_specs = (
        sequences, P(("dp", "fsdp"), None), rows, rows, rows, rows, vector, vector, rows, rows, rows, sequences,
    )
    out_specs = (sequences, sequences, rows, rows, rows, rows, vector, vector, rows, rows, rows)
    body = make_body(mesh.shape["fsdp"], mesh.shape["dp"])
    return jax.shard_map(body, mesh=mesh, in_specs=in_specs, out_specs=out_specs, check_vma=False)
```

```python
from functools import partial

import jax
import jax.numpy as jnp
from jax import lax
from jax.experimental import pallas as pl
from jax.experimental.pallas import tpu as pltpu
from jax.sharding import PartitionSpec as P

QUERY_HEADS = 15
KEY_VALUE_HEADS = 5
GROUP = QUERY_HEADS // KEY_VALUE_HEADS
HEAD_SIZE = 64
HALF = HEAD_SIZE // 2
LONGEST_DOC = 384
EPSILON = 1e-05
ROPE_BASE = 10000.0
NEGATIVE = -1e30
SCALE = HEAD_SIZE ** (-0.5)
QUERY_BLOCK = 128
BF16 = jnp.bfloat16
F32 = jnp.float32
HBM = pltpu.HBM
FFN_GRANT = 24 << 20
BACK_GRANT = 40 << 20
GRAD_GRANT = 24 << 20
MIXED_GRANT = 36 << 20


def dot(left, right, contract):
    return lax.dot_general(left, right, ((contract[:1], contract[1:]), ((), ())), preferred_element_type=F32)


def key_window(block):
    return (max(0, block * QUERY_BLOCK - LONGEST_DOC), (block + 1) * QUERY_BLOCK)


def fill_mask(start_ref, mask_ref):
    for block in range(mask_ref.shape[0] // QUERY_BLOCK):
        low, high = key_window(block)
        cols = slice(block * QUERY_BLOCK, high)
        shape = (high - low, QUERY_BLOCK)
        key = low + lax.broadcasted_iota(jnp.int32, shape, 0)
        query = block * QUERY_BLOCK + lax.broadcasted_iota(jnp.int32, shape, 1)
        allowed = (key >= start_ref[:, cols]) & (key <= query)
        mask_ref[low:high, cols] = jnp.where(allowed, 0.0, NEGATIVE)


def side_by_side(ref, cols):
    return jnp.concatenate([ref[j * HEAD_SIZE : (j + 1) * HEAD_SIZE, cols] for j in range(GROUP)], axis=1)


def attention_kernel(start_ref, query_ref, key_ref, value_ref, mix_ref, logsum_ref, mask_ref, key_rows_ref):
    @pl.when(pl.program_id(0) == 0)
    def _():
        fill_mask(start_ref, mask_ref)

    key_rows_ref[...] = key_ref[...].T
    for block in range(query_ref.shape[1] // QUERY_BLOCK):
        low, high = key_window(block)
        cols = slice(block * QUERY_BLOCK, high)
        queries = side_by_side(query_ref, cols)
        mask = jnp.concatenate([mask_ref[low:high, cols]] * GROUP, axis=1)
        scores = dot(key_rows_ref[low:high, :], queries, (1, 0)) * SCALE + mask
        top = jnp.max(scores, axis=0, keepdims=True)
        weights = jnp.exp(scores - top)
        total = jnp.sum(weights, axis=0, keepdims=True)
        mix = dot(value_ref[:, low:high], weights.astype(BF16), (1, 0))
        mix = (mix / total).astype(BF16)
        logsum = top + jnp.log(total)
        for j in range(GROUP):
            part = slice(j * QUERY_BLOCK, (j + 1) * QUERY_BLOCK)
            mix_ref[j * HEAD_SIZE : (j + 1) * HEAD_SIZE, cols] = mix[:, part]
            logsum_ref[0, j : j + 1, cols] = logsum[:, part]


def attention(start, qkv):
    length = qkv.shape[1]
    rows = GROUP * HEAD_SIZE
    return pl.pallas_call(
        attention_kernel,
        grid=(KEY_VALUE_HEADS,),
        in_specs=[
            pl.BlockSpec((1, length), lambda g: (0, 0)),
            pl.BlockSpec((rows, length), lambda g: (g, 0)),
            pl.BlockSpec((HEAD_SIZE, length), lambda g: (QUERY_HEADS + g, 0)),
            pl.BlockSpec((HEAD_SIZE, length), lambda g: (QUERY_HEADS + KEY_VALUE_HEADS + g, 0)),
        ],
        out_specs=[
            pl.BlockSpec((rows, length), lambda g: (g, 0)),
            pl.BlockSpec((1, 8, length), lambda g: (g, 0, 0)),
        ],
        out_shape=[
            jax.ShapeDtypeStruct((QUERY_HEADS * HEAD_SIZE, length), BF16),
            jax.ShapeDtypeStruct((KEY_VALUE_HEADS, 8, length), F32),
        ],
        scratch_shapes=[pltpu.VMEM((length, length), F32), pltpu.VMEM((length, HEAD_SIZE), BF16)],
        compiler_params=pltpu.CompilerParams(vmem_limit_bytes=8 << 20),
        cost_estimate=pl.CostEstimate(flops=6_000_000_000, bytes_accessed=4_000_000, transcendentals=4_500_000),
        name="attention",
    )(start, qkv, qkv, qkv)


def unrotate(rows, cosine, sine):
    first = rows[:HALF]
    second = rows[HALF:]
    return (first * cosine + second * sine, second * cosine - first * sine)


def attention_back_kernel(
    start_ref, cosine_ref, sine_ref, query_ref, key_ref, value_ref, mix_ref, logsum_ref, mix_grad_ref,
    out_ref, mask_ref, key_rows_ref, value_rows_ref, key_grad_ref, value_grad_ref,
):
    group = pl.program_id(0)

    @pl.when(group == 0)
    def _():
        fill_mask(start_ref, mask_ref)

    key_rows_ref[...] = key_ref[...].T
    value_rows_ref[...] = value_ref[...].T
    key_grad_ref[...] = jnp.zeros_like(key_grad_ref)
    value_grad_ref[...] = jnp.zeros_like(value_grad_ref)
    for block in range(query_ref.shape[1] // QUERY_BLOCK):
        low, high = key_window(block)
        cols = slice(block * QUERY_BLOCK, high)
        queries = side_by_side(query_ref, cols)
        mix_grads = side_by_side(mix_grad_ref, cols)
        mixes = side_by_side(mix_ref, cols)
        inner = jnp.sum(mix_grads.astype(F32) * mixes.astype(F32), axis=0, keepdims=True)
        logsum = jnp.concatenate([logsum_ref[0, j : j + 1, cols] for j in range(GROUP)], axis=1)
        mask = jnp.concatenate([mask_ref[low:high, cols]] * GROUP, axis=1)
        scores = dot(key_rows_ref[low:high, :], queries, (1, 0)) * SCALE + mask
        weights = jnp.exp(scores - logsum)
        weight_grads = dot(value_rows_ref[low:high, :], mix_grads, (1, 0))
        score_grads = (weights * (weight_grads - inner)).astype(BF16)
        value_grad_ref[:, low:high] += dot(mix_grads, weights.astype(BF16), (1, 1))
        key_grad_ref[:, low:high] += dot(queries, score_grads, (1, 1))
        query_grads = dot(key_ref[:, low:high], score_grads, (1, 0)) * SCALE
        cosine = cosine_ref[:, cols]
        sine = sine_ref[:, cols]
        for j in range(GROUP):
            first, second = unrotate(query_grads[:, j * QUERY_BLOCK : (j + 1) * QUERY_BLOCK], cosine, sine)
            base = group * (GROUP * HEAD_SIZE) + j * HEAD_SIZE
            out_ref[pl.ds(pl.multiple_of(base, HALF), HALF), cols] = first.astype(BF16)
            out_ref[pl.ds(pl.multiple_of(base + HALF, HALF), HALF), cols] = second.astype(BF16)
    first, second = unrotate(key_grad_ref[...] * SCALE, cosine_ref[...], sine_ref[...])
    base = (QUERY_HEADS + group) * HEAD_SIZE
    out_ref[pl.ds(pl.multiple_of(base, HALF), HALF), :] = first.astype(BF16)
    out_ref[pl.ds(pl.multiple_of(base + HALF, HALF), HALF), :] = second.astype(BF16)
    base = (QUERY_HEADS + KEY_VALUE_HEADS + group) * HEAD_SIZE
    out_ref[pl.ds(pl.multiple_of(base, HEAD_SIZE), HEAD_SIZE), :] = value_grad_ref[...].astype(BF16)


def attention_back(start, cosine, sine, qkv, mix, logsum, mix_grad):
    length = qkv.shape[1]
    rows = GROUP * HEAD_SIZE
    return pl.pallas_call(
        attention_back_kernel,
        grid=(KEY_VALUE_HEADS,),
        in_specs=[
            pl.BlockSpec((1, length), lambda g: (0, 0)),
            pl.BlockSpec((HALF, length), lambda g: (0, 0)),
            pl.BlockSpec((HALF, length), lambda g: (0, 0)),
            pl.BlockSpec((rows, length), lambda g: (g, 0)),
            pl.BlockSpec((HEAD_SIZE, length), lambda g: (QUERY_HEADS + g, 0)),
            pl.BlockSpec((HEAD_SIZE, length), lambda g: (QUERY_HEADS + KEY_VALUE_HEADS + g, 0)),
            pl.BlockSpec((rows, length), lambda g: (g, 0)),
            pl.BlockSpec((1, 8, length), lambda g: (g, 0, 0)),
            pl.BlockSpec((rows, length), lambda g: (g, 0)),
        ],
        out_specs=pl.BlockSpec(qkv.shape, lambda g: (0, 0)),
        out_shape=jax.ShapeDtypeStruct(qkv.shape, BF16),
        scratch_shapes=[
            pltpu.VMEM((length, length), F32),
            pltpu.VMEM((length, HEAD_SIZE), BF16),
            pltpu.VMEM((length, HEAD_SIZE), BF16),
            pltpu.VMEM((HEAD_SIZE, length), F32),
            pltpu.VMEM((HEAD_SIZE, length), F32),
        ],
        compiler_params=pltpu.CompilerParams(vmem_limit_bytes=8 << 20),
        cost_estimate=pl.CostEstimate(flops=9_000_000_000, bytes_accessed=9_000_000, transcendentals=4_500_000),
        name="attention_back",
    )(start, cosine, sine, qkv, qkv, qkv, mix, logsum, mix_grad)


ROWS = 256
CHUNK = 512


def row_tiles(count):
    return [slice(row, row + ROWS) for row in range(0, count, ROWS)]


def whole(shape):
    return pl.BlockSpec(shape, lambda k: (0,) * len(shape))


def by_cols(rows):
    return pl.BlockSpec((rows, CHUNK), lambda k: (0, k))


def ffn_kernel(
    middle_ref, gain_ref, gate_w_ref, up_w_ref, down_w_ref,
    out_ref, normed_t_ref, gate_ref, up_ref, hidden_ref, normed_ref,
):
    tiles = row_tiles(middle_ref.shape[1])

    @pl.when(pl.program_id(0) == 0)
    def _():
        for cols in tiles:
            middle = middle_ref[:, cols]
            inverse = lax.rsqrt(jnp.mean(middle * middle, axis=0, keepdims=True) + EPSILON)
            normed = (middle * inverse * gain_ref[...]).astype(BF16)
            normed_t_ref[:, cols] = normed
            normed_ref[cols, :] = normed.T
            out_ref[:, cols] = middle

    for rows in tiles:
        normed = normed_ref[rows, :]
        gate = dot(normed, gate_w_ref[...], (1, 0))
        up = dot(normed, up_w_ref[...], (1, 0))
        gate_ref[rows, :] = gate.astype(BF16)
        up_ref[rows, :] = up.astype(BF16)
        hidden = (gate * jax.nn.sigmoid(gate) * up).astype(BF16)
        hidden_ref[rows, :] = hidden
    out_ref[...] += dot(down_w_ref[...], hidden_ref[...], (1, 1))


def ffn(middle, gain, w_gate, w_up, w_down_t):
    width, length = middle.shape
    hidden = w_gate.shape[1]
    return pl.pallas_call(
        ffn_kernel,
        grid=(hidden // CHUNK,),
        in_specs=[whole((width, length)), whole((width, 1)), by_cols(width), by_cols(width), by_cols(width)],
        out_specs=[whole((width, length)), whole((width, length)), by_cols(length), by_cols(length), by_cols(length)],
        out_shape=[
            jax.ShapeDtypeStruct((width, length), F32),
            HBM((width, length), BF16),
            HBM((length, hidden), BF16),
            HBM((length, hidden), BF16),
            HBM((length, hidden), BF16),
        ],
        scratch_shapes=[pltpu.VMEM((length, width), BF16)],
        compiler_params=pltpu.CompilerParams(vmem_limit_bytes=FFN_GRANT),
        cost_estimate=pl.CostEstimate(
            flops=6 * length * width * hidden, bytes_accessed=40_000_000, transcendentals=length * hidden
        ),
        name="ffn",
    )(middle, gain, w_gate, w_up, w_down_t)


def ffn_up_kernel(
    middle_ref, gain_ref, gate_w_ref, up_w_ref, normed_t_ref, gate_ref, up_ref, hidden_ref, normed_ref,
):
    tiles = row_tiles(middle_ref.shape[1])

    @pl.when(pl.program_id(0) == 0)
    def _():
        for cols in tiles:
            middle = middle_ref[:, cols]
            inverse = lax.rsqrt(jnp.mean(middle * middle, axis=0, keepdims=True) + EPSILON)
            normed = (middle * inverse * gain_ref[...]).astype(BF16)
            normed_t_ref[:, cols] = normed
            normed_ref[cols, :] = normed.T

    for rows in tiles:
        normed = normed_ref[rows, :]
        gate = dot(normed, gate_w_ref[...], (1, 0))
        up = dot(normed, up_w_ref[...], (1, 0))
        gate_ref[rows, :] = gate.astype(BF16)
        up_ref[rows, :] = up.astype(BF16)
        hidden_ref[rows, :] = (gate * jax.nn.sigmoid(gate) * up).astype(BF16)


def ffn_up(middle, gain, w_gate, w_up):
    width, length = middle.shape
    hidden = w_gate.shape[1]
    return pl.pallas_call(
        ffn_up_kernel,
        grid=(hidden // CHUNK,),
        in_specs=[whole((width, length)), whole((width, 1)), by_cols(width), by_cols(width)],
        out_specs=[whole((width, length)), by_cols(length), by_cols(length), by_cols(length)],
        out_shape=[HBM((width, length), BF16)] + [HBM((length, hidden), BF16)] * 3,
        scratch_shapes=[pltpu.VMEM((length, width), BF16)],
        compiler_params=pltpu.CompilerParams(vmem_limit_bytes=FFN_GRANT),
        cost_estimate=pl.CostEstimate(
            flops=4 * length * width * hidden, bytes_accessed=30_000_000, transcendentals=length * hidden
        ),
        name="ffn_up",
    )(middle, gain, w_gate, w_up)


def ffn_back_kernel(
    grad_ref, middle_ref, gain_ref, gate_ref, up_ref, gate_w_ref, up_w_ref, down_w_ref,
    out_ref, out_narrow_ref, gate_grad_ref, up_grad_ref, gain_grad_ref, branch_t_ref, total_ref, branch_ref,
):
    step = pl.program_id(0)
    tiles = row_tiles(middle_ref.shape[1])

    @pl.when(step == 0)
    def _():
        for cols in tiles:
            branch = grad_ref[:, cols].astype(BF16)
            branch_t_ref[:, cols] = branch
            branch_ref[cols, :] = branch.T

    for rows in tiles:
        hidden_grad = dot(branch_ref[rows, :], down_w_ref[...], (1, 0))
        gate = gate_ref[rows, :].astype(F32)
        up = up_ref[rows, :].astype(F32)
        sigmoid = jax.nn.sigmoid(gate)
        scaled = hidden_grad * sigmoid
        up_grad = (scaled * gate).astype(BF16)
        gate_grad = (scaled * up * (1.0 + gate * (1.0 - sigmoid))).astype(BF16)
        gate_grad_ref[rows, :] = gate_grad
        up_grad_ref[rows, :] = up_grad
    part = dot(gate_w_ref[...], gate_grad_ref[...], (1, 1)) + dot(up_w_ref[...], up_grad_ref[...], (1, 1))

    @pl.when(step == 0)
    def _():
        total_ref[...] = part

    @pl.when(step > 0)
    def _():
        total_ref[...] += part

    @pl.when(step == pl.num_programs(0) - 1)
    def _():
        gain_grad = jnp.zeros(gain_ref.shape, F32)
        for cols in tiles:
            middle = middle_ref[:, cols]
            normed_grad = total_ref[:, cols]
            inverse = lax.rsqrt(jnp.mean(middle * middle, axis=0, keepdims=True) + EPSILON)
            unit = middle * inverse
            gain_grad += jnp.sum(normed_grad * unit, axis=1, keepdims=True)
            scaled = gain_ref[...] * normed_grad
            inner = jnp.mean(scaled * unit, axis=0, keepdims=True)
            out = grad_ref[:, cols] + inverse * (scaled - unit * inner)
            out_ref[:, cols] = out
            out_narrow_ref[:, cols] = out.astype(BF16)
        gain_grad_ref[...] = gain_grad


def ffn_back(grad, middle, gain, gate, up, w_gate, w_up, w_down_t):
    width, length = middle.shape
    hidden = w_gate.shape[1]
    full = whole((width, length))
    return pl.pallas_call(
        ffn_back_kernel,
        grid=(hidden // CHUNK,),
        in_specs=[
            full, full, whole((width, 1)), by_cols(length), by_cols(length), by_cols(width), by_cols(width), by_cols(width),
        ],
        out_specs=[full, full, by_cols(length), by_cols(length), whole((width, 1)), full],
        out_shape=[
            HBM((width, length), F32),
            jax.ShapeDtypeStruct((width, length), BF16),
            HBM((length, hidden), BF16),
            HBM((length, hidden), BF16),
            jax.ShapeDtypeStruct((width, 1), F32),
            HBM((width, length), BF16),
        ],
        scratch_shapes=[pltpu.VMEM((width, length), F32), pltpu.VMEM((length, width), BF16)],
        compiler_params=pltpu.CompilerParams(vmem_limit_bytes=BACK_GRANT),
        cost_estimate=pl.CostEstimate(
            flops=6 * length * width * hidden, bytes_accessed=50_000_000, transcendentals=length * hidden
        ),
        name="ffn_back",
    )(grad, middle, gain, gate, up, w_gate, w_up, w_down_t)


def weight_grad_kernel(left_fsdp, transposed, places_ref, left_ref, right_ref, left2_ref, right2_ref, keep_ref, send_ref):
    step = pl.program_id(0)
    contract = (1, 1) if transposed else (1, 0)
    total = dot(left_ref[...], right_ref[...], contract) + dot(left2_ref[...], right2_ref[...], contract)
    total = total.astype(BF16)
    half = total.shape[0] // 2
    fsdp, core = places_ref[0], places_ref[1]
    if left_fsdp:
        for out_ref, here in ((keep_ref, step < 2), (send_ref, step >= 2)):

            @pl.when(here)
            def _():
                out_ref[fsdp] = total[:half]
                out_ref[1 - fsdp] = total[half:]

    else:
        for out_ref, first in ((keep_ref, core), (send_ref, 1 - core)):

            @pl.when(first == 0)
            def _():
                out_ref[0] = total[:half]

            @pl.when(first == 1)
            def _():
                out_ref[0] = total[half:]


def weight_grad(places, products, more_products, left_fsdp):
    left, right = products
    left2, right2 = more_products
    rows, length = left.shape
    cols = right.shape[1]
    block = cols // 4
    left_spec = pl.BlockSpec((rows, length), lambda j, places: (0, 0))
    if left_fsdp:
        right_spec = pl.BlockSpec((length, block), lambda j, places: (0, (2 * places[1] + j) % 4))
        keep_spec = pl.BlockSpec((2, rows // 2, block), lambda j, places: (0, 0, jnp.minimum(j, 1)))
        send_spec = pl.BlockSpec((2, rows // 2, block), lambda j, places: (0, 0, jnp.maximum(j - 2, 0)))
    else:
        right_spec = pl.BlockSpec((length, block), lambda j, places: (0, (2 * places[0] + j) % 4))
        keep_spec = pl.BlockSpec((1, rows // 2, block), lambda j, places: (j // 2, 0, j % 2))
        send_spec = keep_spec
    return pl.pallas_call(
        partial(weight_grad_kernel, left_fsdp, False),
        grid_spec=pltpu.PrefetchScalarGridSpec(
            num_scalar_prefetch=1,
            grid=(4,),
            in_specs=[left_spec, right_spec, left_spec, right_spec],
            out_specs=[keep_spec, send_spec],
        ),
        out_shape=[jax.ShapeDtypeStruct((2, rows // 2, cols // 2), BF16)] * 2,
        compiler_params=pltpu.CompilerParams(vmem_limit_bytes=GRAD_GRANT),
        cost_estimate=pl.CostEstimate(
            flops=4 * rows * length * cols, bytes_accessed=10 * rows * cols, transcendentals=0
        ),
        name="weight_grad",
    )(places, left, right, left2, right2)


def mixed_grad_kernel(
    places_ref, mix_ref, branch_ref, normed_ref, qkv_ref, mix2_ref, branch2_ref, normed2_ref, qkv2_ref,
    keep_ref, send_ref,
):
    width = branch_ref.shape[0]
    half_cols = keep_ref.shape[2]
    out_part = dot(mix_ref[...], branch_ref[...], (1, 1)) + dot(mix2_ref[...], branch2_ref[...], (1, 1))
    qkv_part = dot(normed_ref[...], qkv_ref[...], (1, 1)) + dot(normed2_ref[...], qkv2_ref[...], (1, 1))
    out_part = out_part.astype(BF16)
    qkv_part = qkv_part.astype(BF16)
    first = half_cols - width
    core = places_ref[1]
    for low_ref, high_ref, here in ((keep_ref, send_ref, core == 0), (send_ref, keep_ref, core == 1)):

        @pl.when(here)
        def _():
            low_ref[0, :, :width] = out_part
            low_ref[0, :, width:] = qkv_part[:, :first]
            high_ref[0] = qkv_part[:, first:]


def mixed_grad(places, products, more_products):
    (mix, branch), (normed, qkv) = products
    (mix2, branch2), (normed2, qkv2) = more_products
    rows, length = mix.shape
    cols = branch.shape[0] + qkv.shape[0]
    left = pl.BlockSpec((rows // 2, length), lambda j, places: ((places[0] + j) % 2, 0))
    fixed = lambda shape: pl.BlockSpec(shape, lambda j, places: (0, 0))
    specs = [left, fixed(branch.shape), left, fixed(qkv.shape)]
    return pl.pallas_call(
        mixed_grad_kernel,
        grid_spec=pltpu.PrefetchScalarGridSpec(
            num_scalar_prefetch=1,
            grid=(2,),
            in_specs=specs + specs,
            out_specs=[pl.BlockSpec((1, rows // 2, cols // 2), lambda j, places: (j, 0, 0))] * 2,
        ),
        out_shape=[jax.ShapeDtypeStruct((2, rows // 2, cols // 2), BF16)] * 2,
        compiler_params=pltpu.CompilerParams(vmem_limit_bytes=MIXED_GRANT),
        cost_estimate=pl.CostEstimate(
            flops=4 * rows * length * cols, bytes_accessed=10 * rows * cols, transcendentals=0
        ),
        name="mixed_grad",
    )(places, mix, branch, normed, qkv, mix2, branch2, normed2, qkv2)


def assemble_kernel(stack_cores, cuts, places_ref, *refs):
    core, side = places_ref[1], places_ref[2]
    inputs, outputs = refs[:4], refs[4:]
    count, cols = inputs[0].shape
    whole_ref = outputs[-1]
    for k, piece_ref in enumerate(inputs):
        at_side = jnp.bitwise_xor(side, k % 2)
        at_core = jnp.bitwise_xor(core, k // 2)
        row = at_side * count + (at_core * (2 * count) if stack_cores else 0)
        rows = pl.ds(pl.multiple_of(row, 8), count)
        value = piece_ref[...].astype(F32)
        if stack_cores:
            whole_ref[rows, :] = value
        else:
            whole_ref[rows, pl.ds(pl.multiple_of(at_core * cols, 128), cols)] = value
    for out_ref, (low, high) in zip(outputs[:-1], cuts):
        value = whole_ref[:, low:high]
        out_ref[...] = value.T if out_ref.shape[0] == high - low else value


def assemble(places, pieces, stack_cores, cuts=()):
    count, cols = pieces[0].shape
    shape = (4 * count, cols) if stack_cores else (2 * count, 2 * cols)
    out_shape = [
        jax.ShapeDtypeStruct((high - low, shape[0]) if high - low < shape[0] else (shape[0], high - low), F32)
        for low, high in cuts
    ]
    out_shape = out_shape or [jax.ShapeDtypeStruct(shape, F32)]
    return pl.pallas_call(
        partial(assemble_kernel, stack_cores, cuts),
        grid_spec=pltpu.PrefetchScalarGridSpec(
            num_scalar_prefetch=1,
            grid=(1,),
            in_specs=[pl.BlockSpec((count, cols), lambda j, places: (0, 0))] * 4,
            out_specs=[pl.BlockSpec(out.shape, lambda j, places: (0, 0)) for out in out_shape],
            scratch_shapes=[pltpu.VMEM(shape, F32)] if cuts else [],
        ),
        out_shape=out_shape,
        compiler_params=pltpu.CompilerParams(vmem_limit_bytes=24 << 20),
        cost_estimate=pl.CostEstimate(flops=0, bytes_accessed=24 * count * cols, transcendentals=0),
        name="assemble",
    )(places, *pieces)


def doc_tables(doc_row):
    token_index = jnp.arange(doc_row.shape[0])
    start = jnp.sum((doc_row[:, None] < doc_row[None, :]).astype(jnp.int32), axis=0)
    places = (token_index - start).astype(F32)
    frequency = ROPE_BASE ** (-2.0 * jnp.arange(HALF, dtype=F32) / HEAD_SIZE)
    angles = frequency[:, None] * places[None, :]
    return (start[None, :], jnp.cos(angles), jnp.sin(angles))


def norm_forward(inputs, gain):
    inverse = lax.rsqrt(jnp.mean(inputs * inputs, axis=0, keepdims=True) + EPSILON)
    return (inputs * inverse * gain).astype(BF16)


def norm_backward(inputs, gain, grad):
    inverse = lax.rsqrt(jnp.mean(inputs * inputs, axis=0, keepdims=True) + EPSILON)
    scaled = gain * grad
    inner = jnp.mean(scaled * inputs, axis=0, keepdims=True)
    return (inverse * scaled - inputs * inverse**3 * inner, jnp.sum(grad * inputs * inverse, axis=1, keepdims=True))


def project(inputs, w_qkv, gains, tables):
    _, cosine, sine = tables
    length = inputs.shape[1]
    normed = norm_forward(inputs, gains[0])
    raw = dot(w_qkv, normed, (0, 0))
    heads = QUERY_HEADS + KEY_VALUE_HEADS
    pairs = raw[: heads * HEAD_SIZE].reshape(heads, 2, HALF, length)
    first, second = pairs[:, 0], pairs[:, 1]
    rotated = jnp.stack([first * cosine - second * sine, second * cosine + first * sine], axis=1)
    qkv = jnp.concatenate(
        [rotated.reshape(heads * HEAD_SIZE, length).astype(BF16), raw[heads * HEAD_SIZE :].astype(BF16)], axis=0
    )
    return (normed, qkv)


def project_out(inputs, w_out, mix):
    return inputs + dot(w_out, mix, (0, 0))


def attention_backward(kept, attn_grad, weights, tables):
    start, cosine, sine = tables
    _, _, qkv, logsum, mix = kept
    mix_grad = dot(weights[1], attn_grad, (1, 0)).astype(BF16)
    return attention_back(start, cosine, sine, qkv, mix, logsum, mix_grad)


def input_backward(kept, middle_grad, qkv_grad, weights, gains):
    normed_grad = dot(weights[0], qkv_grad, (1, 0))
    inputs_grad, gain_grad = norm_backward(kept[0], gains[0], normed_grad)
    return (inputs_grad + middle_grad, gain_grad)


def after(value, *earlier):
    return lax.optimization_barrier((value,) + earlier)[0]


def swap_fsdp(value):
    return lax.ppermute(value, "fsdp", [(0, 1), (1, 0)])


def swap_dp(value, bit, size=16):
    return lax.ppermute(value, "dp", [(i, i ^ bit) for i in range(size)])


def fetch(parts, axis, index, pieces):
    sent = [cut_piece(part, index, axis, pieces) for part in parts]
    sent = jnp.concatenate(sent, axis=1) if len(sent) > 1 else sent[0]
    return sent


def cut_piece(value, index, axis, pieces):
    count = value.shape[axis] // pieces
    return lax.dynamic_slice_in_dim(value, index * count, count, axis)


def join_kernel(own_count, shard_axis, piece_axis, index_at, places_ref, *refs):
    own, pieces, out_ref = refs[:own_count], refs[own_count:-1], refs[-1]
    rows, cols = out_ref.shape
    fsdp = places_ref[0]
    index = places_ref[index_at]
    if shard_axis == 0:
        half = pl.ds(pl.multiple_of(fsdp * (rows // 2), 16), rows // 2)
        at = 0
        for ref in own:
            out_ref[half, at : at + ref.shape[1]] = ref[...]
            at += ref.shape[1]
    else:
        out_ref[:, pl.ds(pl.multiple_of(fsdp * (cols // 2), 128), cols // 2)] = own[0][...]
    for flip, ref in enumerate(pieces):
        at = jnp.bitwise_xor(index, flip)
        count, width = ref.shape
        row = at * count if piece_axis == 0 else 0
        col = at * width if piece_axis == 1 else 0
        if shard_axis == 0:
            row = row + (1 - fsdp) * (rows // 2)
        else:
            col = col + (1 - fsdp) * (cols // 2)
        row_at = pl.ds(pl.multiple_of(row, 16), count)
        if shard_axis == 0 and piece_axis == 0:
            out_ref[row_at, :] = ref[...]
        else:
            out_ref[row_at, pl.ds(pl.multiple_of(col, 128), width)] = ref[...]


def join(places, own, pieces, shard_axis, piece_axis, index_at):
    rows, cols = own[0].shape[0], sum(part.shape[1] for part in own)
    shape = (2 * rows, cols) if shard_axis == 0 else (rows, 2 * cols)
    full = lambda shape: pl.BlockSpec(shape, lambda j, places: (0, 0))
    return pl.pallas_call(
        partial(join_kernel, len(own), shard_axis, piece_axis, index_at),
        grid_spec=pltpu.PrefetchScalarGridSpec(
            num_scalar_prefetch=1,
            grid=(1,),
            in_specs=[full(part.shape) for part in (*own, *pieces)],
            out_specs=full(shape),
        ),
        out_shape=jax.ShapeDtypeStruct(shape, BF16),
        compiler_params=pltpu.CompilerParams(vmem_limit_bytes=24 << 20),
        cost_estimate=pl.CostEstimate(flops=0, bytes_accessed=4 * shape[0] * shape[1], transcendentals=0),
        name="join",
    )(places, *own, *pieces)


def add(left, right):
    return (left.astype(F32) + right.astype(F32)).astype(BF16)


def add3(first, second, third):
    return ((first.astype(F32) + second.astype(F32)) + third.astype(F32)).astype(BF16)


def reduce_vector(values):
    total = values
    for bit in (1, 2, 4, 8):
        total = add(total, swap_dp(total, bit))
    total = add(total, swap_fsdp(total))
    count = values.shape[1] // 2
    return lax.dynamic_slice_in_dim(total, lax.axis_index("fsdp") * count, count, 1)


def gather_gains(gains):
    other = swap_fsdp(gains)
    first = lax.axis_index("fsdp") == 0
    return jnp.concatenate([jnp.where(first, gains, other), jnp.where(first, other, gains)], axis=1)


def cut(value, which, axis):
    count = value.shape[axis] // 2
    return lax.dynamic_slice_in_dim(value, which * count, count, axis)


def sides():
    place = lax.axis_index("dp")
    return ((place // 2) % 2, (place // 4) % 2, (place // 8) % 2)


class Reduction:
    def __init__(self, halves, queue=()):
        self.keep, send = halves
        self.received = swap_dp(after(send, *queue), 1)
        self.side, self.lane, _ = sides()
        self.plan = iter((self.fsdp, self.y, self.z_near, self.z_far, self.z_back, self.y_back, self.finish))

    def step(self, queue):
        mine = next(self.plan)(lambda value: after(value, *queue))
        queue[:] = [mine]

    def split(self, value, which, axis, bit):
        mine, self.own = cut(value, 1 - which, axis), cut(value, which, axis)
        self.incoming = swap_dp(mine, bit)
        return mine

    def fsdp(self, gate):
        mine = add(gate(self.keep)[1], self.received[1])
        self.incoming = swap_fsdp(mine)
        return mine

    def fsdp_sum(self, gate):
        return add3(gate(self.keep)[0], self.received[0], self.incoming)

    def y(self, gate):
        return self.split(self.fsdp_sum(gate), self.side, 0, 2)

    def z_near(self, gate):
        return self.split(add(gate(self.own), self.incoming), self.lane, 1, 4)

    def z_far(self, gate):
        self.own = add(gate(self.own), self.incoming)
        self.incoming = swap_dp(self.own, 8)
        return self.own

    def z_back(self, gate):
        self.own = add(gate(self.own), self.incoming)
        self.incoming = swap_dp(self.own, 4)
        return self.own

    def y_back(self, gate):
        mine = self.own = put_together(gate(self.own), self.incoming, self.lane, 1)
        self.across = swap_dp(mine, 2)
        self.beside = swap_dp(mine, 1)
        return mine

    def finish(self, gate):
        mine = gate(self.across)
        self.pieces = (self.own, mine, self.beside, swap_dp(mine, 1))
        return mine


class ReductionOverZ(Reduction):
    def __init__(self, halves, queue=()):
        super().__init__(halves, queue)
        self.far = sides()[2]
        self.plan = iter((self.fsdp, self.first, self.second, self.over_y, self.back_far, self.back_near, self.done))

    def first(self, gate):
        return self.split(self.fsdp_sum(gate), self.lane, 0, 4)

    def second(self, gate):
        return self.split(add(gate(self.own), self.incoming), self.far, 0, 8)

    def over_y(self, gate):
        self.own = add(gate(self.own), self.incoming)
        self.incoming = swap_dp(self.own, 2)
        return self.own

    def back_far(self, gate):
        self.own = add(gate(self.own), self.incoming)
        self.incoming = swap_dp(self.own, 8)
        return self.own

    def back_near(self, gate):
        mine = self.own = put_together(gate(self.own), self.incoming, self.far, 0)
        self.across = swap_dp(mine, 4)
        self.beside = swap_dp(mine, 1)
        return mine

    def done(self, gate):
        mine = gate(self.across)
        self.pieces = (self.own, mine, self.beside, swap_dp(mine, 1))
        return mine


class ReductionBothWays(Reduction):
    def __init__(self, halves, queue=()):
        super().__init__(halves, queue)
        self.plan = iter((self.one, self.two, self.three, self.z_far, self.z_back, self.y_back, self.finish))

    def one(self, gate):
        keep = gate(self.keep)
        half = keep.shape[2] // 2
        theirs = add(keep[1, :, :half], self.received[1, :, :half])
        self.over_x = swap_fsdp(theirs)
        both = add(keep[:, :, half:], self.received[:, :, half:])
        mine, self.both = cut(both, 1 - self.side, 1), cut(both, self.side, 1)
        self.over_y = swap_dp(mine, 2)
        return mine

    def two(self, gate):
        half = self.keep.shape[2] // 2
        first = add3(gate(self.keep)[0, :, :half], self.received[0, :, :half], self.over_x)
        mine, self.first = cut(first, 1 - self.side, 0), cut(first, self.side, 0)
        self.over_y_too = swap_dp(mine, 2)
        theirs = add(gate(self.both)[1], self.over_y[1])
        self.over_x_too = swap_fsdp(theirs)
        return theirs

    def three(self, gate):
        first = add(gate(self.first), self.over_y_too)
        second = add3(gate(self.both)[0], self.over_y[0], self.over_x_too)
        mine = jnp.where(self.lane == 0, second, first)
        self.own = jnp.where(self.lane == 0, first, second)
        self.incoming = swap_dp(mine, 4)
        return mine


def put_together(own, other, which, axis):
    low = jnp.where(which == 0, own, other)
    high = jnp.where(which == 0, other, own)
    return jnp.concatenate([low, high], axis=axis)


def make_body(fsdp_size, dp_size):
    paired = fsdp_size == 2 and dp_size == 16

    def body(
        activations, doc_ids, w_query, key_projection, value_projection, w_out,
        gain_attn, gain_ffn, w_gate, w_up, w_down, cotangent,
    ):
        if paired:
            place = lax.axis_index("dp")
            core, side, lane = place % 2, (place // 2) % 2, (place // 4) % 2
            index_y, index_z = place % 4, core + 2 * lane
            places = jnp.stack([lax.axis_index("fsdp"), core, side, index_y, index_z]).astype(jnp.int32)
            qkv_own = (w_query, key_projection, value_projection)
            qkv_sent = fetch(qkv_own, 0, core, 2)
            out_sent = fetch((after(w_out, qkv_sent),), 0, core, 2)
            gate_sent = fetch((after(w_gate, out_sent),), 1, index_y, 4)
            up_sent = fetch((after(w_up, gate_sent),), 1, index_z, 4)
            down_sent = fetch((after(w_down.T, up_sent),), 0, index_y, 4)
            qkv_mine = swap_fsdp(qkv_sent)
            gains = gather_gains(after(jnp.stack([gain_attn, gain_ffn]), qkv_sent)).astype(F32)
            out_mine, gate_mine, up_mine, down_mine = [
                swap_fsdp(sent) for sent in (out_sent, gate_sent, up_sent, down_sent)
            ]
            w_qkv = join(places, qkv_own, (qkv_mine, swap_dp(qkv_mine, 1)), 0, 0, 1)
        else:
            collect = lambda shard, axis: lax.all_gather(shard, "fsdp", axis=axis, tiled=True)
            gains = collect(jnp.stack([gain_attn, gain_ffn]), 1).astype(F32)
            places = jnp.zeros((4,), jnp.int32)
            qkv_shard = jnp.concatenate([w_query, key_projection, value_projection], axis=1)
            weights = (
                collect(qkv_shard, 0), collect(w_out, 0), collect(w_gate, 0), collect(w_up, 0), collect(w_down, 0).T,
            )
        gains = (gains[0][:, None], gains[1][:, None])
        tables = doc_tables(doc_ids[0])
        start, cosine, sine = tables
        inputs = activations[0].T.astype(F32)

        if paired:
            normed, qkv = project(inputs, w_qkv, gains, tables)
            out_mine = after(out_mine, qkv)
            gate_mine = after(gate_mine, out_mine)
            out_beside = swap_dp(out_mine, 1)
            gate_across, gate_beside = swap_dp(gate_mine, 2), swap_dp(gate_mine, 1)
            mix, logsum = attention(start, qkv)
            up_mine = after(up_mine, mix)
            up_across, up_beside = swap_dp(up_mine, 4), swap_dp(up_mine, 1)
            gate_across = after(gate_across, up_mine)
            gate_corner = swap_dp(gate_across, 1)
            w_out_full = join(places, (w_out,), (out_mine, out_beside), 0, 0, 1)
            middle = project_out(inputs, w_out_full, mix)
            down_mine = after(down_mine, middle)
            down_across, down_beside = swap_dp(down_mine, 2), swap_dp(down_mine, 1)
            gate_pieces = (after(gate_mine, down_mine), gate_beside, gate_across, gate_corner)
            w_gate_full = join(places, (w_gate,), gate_pieces, 0, 1, 3)
            up_across = after(up_across, w_gate_full)
            w_up_full = join(places, (w_up,), (up_mine, up_beside, up_across, swap_dp(up_across, 1)), 0, 1, 4)
            first_normed, first_gate, first_up, first_hidden = ffn_up(middle, gains[1], w_gate_full, w_up_full)
            down_across = after(down_across, first_hidden)
            w_down_full = join(
                places, (w_down.T,), (down_mine, down_beside, down_across, swap_dp(down_across, 1)), 1, 0, 3
            )
            weights = (w_qkv, w_out_full, w_gate_full, w_up_full, w_down_full)
            ffn_weights = weights[2:]
        else:
            ffn_weights = weights[2:]
            normed, qkv = project(inputs, weights[0], gains, tables)
            mix, logsum = attention(start, qkv)
            middle = project_out(inputs, weights[1], mix)
            first_normed, first_gate, first_up, first_hidden = ffn_up(middle, gains[1], *ffn_weights[:2])
        first = (inputs, normed, qkv, logsum, mix)
        inputs2 = middle + dot(ffn_weights[2], first_hidden, (1, 1))
        normed2, qkv2 = project(inputs2, weights[0], gains, tables)
        mix2, logsum2 = attention(start, qkv2)
        middle2 = project_out(inputs2, weights[1], mix2)
        second = (inputs2, normed2, qkv2, logsum2, mix2)
        outputs, second_normed, second_gate, second_up, second_hidden = ffn(middle2, gains[1], *ffn_weights)

        grad = cotangent[0].T.astype(F32)
        grad, attn_grad2, gate_grad2, up_grad2, ffn_gain2, branch2 = ffn_back(
            grad, middle2, gains[1], second_gate, second_up, *ffn_weights
        )
        qkv_grad2 = attention_backward(second, attn_grad2, weights, tables)
        grad, attn_gain2 = input_backward(second, grad, qkv_grad2, weights, gains)

        down_halves = weight_grad(
            places, (branch2, second_hidden), (grad.astype(BF16), first_hidden), False
        )
        queue = []
        if paired:
            down = Reduction(down_halves)
            down.step(queue)
            grad = after(grad, *queue)
        else:
            grad = after(grad, *down_halves)
        grad, attn_grad, gate_grad, up_grad, ffn_gain, _ = ffn_back(
            grad, middle, gains[1], first_gate, first_up, *ffn_weights
        )
        if paired:
            down.step(queue)
            gate_grad = after(gate_grad, *queue)
        gate_halves = weight_grad(places, (second_normed, gate_grad2), (first_normed, gate_grad), True)
        if paired:
            queue.append(gate_halves[0])
            down.step(queue)
            gate = Reduction(gate_halves, queue)
        mix_grad_in = after(attn_grad, *gate_halves)
        mix_grad = dot(weights[1], mix_grad_in, (1, 0)).astype(BF16)
        if paired:
            queue.append(mix_grad)
            gate.step(queue)
            up_grad = after(up_grad, *queue)
        up_halves = weight_grad(places, (second_normed, up_grad2), (first_normed, up_grad), True)
        if paired:
            queue.append(up_halves[0])
            down.step(queue)
            up = Reduction(up_halves, queue)
            up.step(queue)
            mix_grad = after(mix_grad, *queue)
        qkv_grad = attention_back(start, cosine, sine, first[2], first[4], first[3], mix_grad)
        if paired:
            queue.append(qkv_grad)
            down.step(queue)
            gate.step(queue)
            qkv_grad = after(qkv_grad, *queue)
        mixed_halves = mixed_grad(
            places,
            ((second[4], attn_grad2), (second[1], qkv_grad2)),
            ((first[4], attn_grad), (first[1], qkv_grad)),
        )
        if paired:
            mixed = Reduction(mixed_halves)
            queue.append(mixed_halves[0])
            down.step(queue)
            gate.step(queue)
            up.step(queue)
            mixed.step(queue)
            grad = after(grad, *queue)
        grad, attn_gain = input_backward(first, grad, after(qkv_grad, *mixed_halves), weights, gains)
        gain_grads = jnp.concatenate([attn_gain + attn_gain2, ffn_gain + ffn_gain2], axis=1).T.astype(BF16)

        width = w_query.shape[1]
        key_end = width + key_projection.shape[1]
        value_end = key_end + value_projection.shape[1]
        cuts = ((0, width), (width, 2 * width), (2 * width, width + key_end), (width + key_end, width + value_end))
        if paired:
            queue.append(grad)
            down.step(queue)
            gate.step(queue)
            up.step(queue)
            mixed.step(queue)
            gate.step(queue)
            up.step(queue)
            gate.step(queue)
            mixed.step(queue)
            (grad_down,) = assemble(places, [after(down.pieces[0], *queue), *down.pieces[1:]], True)
            queue.append(grad_down)
            up.step(queue)
            mixed.step(queue)
            up.step(queue)
            mixed.step(queue)
            gate.step(queue)
            (grad_gate,) = assemble(places, [after(gate.pieces[0], *queue), *gate.pieces[1:]], False)
            queue.append(grad_gate)
            mixed.step(queue)
            up.step(queue)
            mixed.step(queue)
            (grad_up,) = assemble(places, [after(up.pieces[0], *queue), *up.pieces[1:]], False)
            queue.append(grad_up)
            grad_out, grad_query, grad_key, grad_value = assemble(places, mixed.pieces, False, cuts)
            grad_key, grad_value = grad_key.T, grad_value.T
            gain_grads = reduce_vector(gain_grads).astype(F32)
        else:

            def reduce(value, axis):
                part = lax.psum_scatter(value, "fsdp", scatter_dimension=axis, tiled=True)
                return lax.psum(part, "dp").astype(F32)

            rows = lambda halves: jnp.concatenate([h.reshape(-1, h.shape[2]) for h in halves], axis=1)
            cols = lambda halves: jnp.concatenate([jnp.concatenate([h[0], h[1]], axis=1) for h in halves])
            grad_down = reduce(cols(down_halves).T, 0).T
            grad_gate = reduce(rows(gate_halves), 0)
            grad_up = reduce(rows(up_halves), 0)
            mixed = reduce(rows(mixed_halves), 0)
            grad_out, grad_query, grad_key, grad_value = [mixed[:, low:high] for low, high in cuts]
            gain_grads = reduce(gain_grads, 1)
        return (
            outputs.T.astype(BF16)[None],
            grad.T.astype(BF16)[None],
            grad_query,
            grad_key,
            grad_value,
            grad_out,
            gain_grads[0],
            gain_grads[1],
            grad_gate,
            grad_up,
            grad_down.T,
        )

    return body


def solution(mesh):
    sequences = P(("dp", "fsdp"), None, None)
    rows = P("fsdp", None)
    vector = P("fsdp")
    in_specs = (
        sequences, P(("dp", "fsdp"), None), rows, rows, rows, rows, vector, vector, rows, rows, rows, sequences,
    )
    out_specs = (sequences, sequences, rows, rows, rows, rows, vector, vector, rows, rows, rows)
    body = make_body(mesh.shape["fsdp"], mesh.shape["dp"])
    return jax.shard_map(body, mesh=mesh, in_specs=in_specs, out_specs=out_specs, check_vma=False)
```

```python
from functools import partial

import jax
import jax.numpy as jnp
from jax import lax
from jax.experimental import pallas as pl
from jax.experimental.pallas import tpu as pltpu
from jax.sharding import PartitionSpec as P

QUERY_HEADS = 15
KEY_VALUE_HEADS = 5
GROUP = QUERY_HEADS // KEY_VALUE_HEADS
HEAD_SIZE = 64
HALF = HEAD_SIZE // 2
LONGEST_DOC = 384
EPSILON = 1e-05
ROPE_BASE = 10000.0
NEGATIVE = -1e30
SCALE = HEAD_SIZE ** (-0.5)
QUERY_BLOCK = 128
BF16 = jnp.bfloat16
F32 = jnp.float32
HBM = pltpu.HBM
FFN_GRANT = 24 << 20
BACK_GRANT = 40 << 20
GRAD_GRANT = 24 << 20
MIXED_GRANT = 36 << 20


def dot(left, right, contract):
    return lax.dot_general(left, right, ((contract[:1], contract[1:]), ((), ())), preferred_element_type=F32)


def key_window(block):
    return (max(0, block * QUERY_BLOCK - LONGEST_DOC), (block + 1) * QUERY_BLOCK)


def fill_mask(start_ref, mask_ref):
    for block in range(mask_ref.shape[0] // QUERY_BLOCK):
        low, high = key_window(block)
        cols = slice(block * QUERY_BLOCK, high)
        shape = (high - low, QUERY_BLOCK)
        key = low + lax.broadcasted_iota(jnp.int32, shape, 0)
        query = block * QUERY_BLOCK + lax.broadcasted_iota(jnp.int32, shape, 1)
        allowed = (key >= start_ref[:, cols]) & (key <= query)
        mask_ref[low:high, cols] = jnp.where(allowed, 0.0, NEGATIVE)


def side_by_side(ref, cols):
    return jnp.concatenate([ref[j * HEAD_SIZE : (j + 1) * HEAD_SIZE, cols] for j in range(GROUP)], axis=1)


def attention_kernel(start_ref, query_ref, key_ref, value_ref, mix_ref, logsum_ref, mask_ref, key_rows_ref):
    @pl.when(pl.program_id(0) == 0)
    def _():
        fill_mask(start_ref, mask_ref)

    key_rows_ref[...] = key_ref[...].T
    for block in range(query_ref.shape[1] // QUERY_BLOCK):
        low, high = key_window(block)
        cols = slice(block * QUERY_BLOCK, high)
        queries = side_by_side(query_ref, cols)
        mask = jnp.concatenate([mask_ref[low:high, cols]] * GROUP, axis=1)
        scores = dot(key_rows_ref[low:high, :], queries, (1, 0)) * SCALE + mask
        top = jnp.max(scores, axis=0, keepdims=True)
        weights = jnp.exp(scores - top)
        total = jnp.sum(weights, axis=0, keepdims=True)
        mix = dot(value_ref[:, low:high], weights.astype(BF16), (1, 0))
        mix = (mix / total).astype(BF16)
        logsum = top + jnp.log(total)
        for j in range(GROUP):
            part = slice(j * QUERY_BLOCK, (j + 1) * QUERY_BLOCK)
            mix_ref[j * HEAD_SIZE : (j + 1) * HEAD_SIZE, cols] = mix[:, part]
            logsum_ref[0, j : j + 1, cols] = logsum[:, part]


def attention(start, qkv):
    length = qkv.shape[1]
    rows = GROUP * HEAD_SIZE
    return pl.pallas_call(
        attention_kernel,
        grid=(KEY_VALUE_HEADS,),
        in_specs=[
            pl.BlockSpec((1, length), lambda g: (0, 0)),
            pl.BlockSpec((rows, length), lambda g: (g, 0)),
            pl.BlockSpec((HEAD_SIZE, length), lambda g: (QUERY_HEADS + g, 0)),
            pl.BlockSpec((HEAD_SIZE, length), lambda g: (QUERY_HEADS + KEY_VALUE_HEADS + g, 0)),
        ],
        out_specs=[
            pl.BlockSpec((rows, length), lambda g: (g, 0)),
            pl.BlockSpec((1, 8, length), lambda g: (g, 0, 0)),
        ],
        out_shape=[
            jax.ShapeDtypeStruct((QUERY_HEADS * HEAD_SIZE, length), BF16),
            jax.ShapeDtypeStruct((KEY_VALUE_HEADS, 8, length), F32),
        ],
        scratch_shapes=[pltpu.VMEM((length, length), F32), pltpu.VMEM((length, HEAD_SIZE), BF16)],
        compiler_params=pltpu.CompilerParams(vmem_limit_bytes=8 << 20),
        cost_estimate=pl.CostEstimate(flops=6_000_000_000, bytes_accessed=4_000_000, transcendentals=4_500_000),
        name="attention",
    )(start, qkv, qkv, qkv)


def unrotate(rows, cosine, sine):
    first = rows[:HALF]
    second = rows[HALF:]
    return (first * cosine + second * sine, second * cosine - first * sine)


def attention_back_kernel(
    start_ref, cosine_ref, sine_ref, query_ref, key_ref, value_ref, mix_ref, logsum_ref, mix_grad_ref,
    out_ref, mask_ref, key_rows_ref, value_rows_ref, key_grad_ref, value_grad_ref,
):
    group = pl.program_id(0)

    @pl.when(group == 0)
    def _():
        fill_mask(start_ref, mask_ref)

    key_rows_ref[...] = key_ref[...].T
    value_rows_ref[...] = value_ref[...].T
    key_grad_ref[...] = jnp.zeros_like(key_grad_ref)
    value_grad_ref[...] = jnp.zeros_like(value_grad_ref)
    for block in range(query_ref.shape[1] // QUERY_BLOCK):
        low, high = key_window(block)
        cols = slice(block * QUERY_BLOCK, high)
        queries = side_by_side(query_ref, cols)
        mix_grads = side_by_side(mix_grad_ref, cols)
        mixes = side_by_side(mix_ref, cols)
        inner = jnp.sum(mix_grads.astype(F32) * mixes.astype(F32), axis=0, keepdims=True)
        logsum = jnp.concatenate([logsum_ref[0, j : j + 1, cols] for j in range(GROUP)], axis=1)
        mask = jnp.concatenate([mask_ref[low:high, cols]] * GROUP, axis=1)
        scores = dot(key_rows_ref[low:high, :], queries, (1, 0)) * SCALE + mask
        weights = jnp.exp(scores - logsum)
        weight_grads = dot(value_rows_ref[low:high, :], mix_grads, (1, 0))
        score_grads = (weights * (weight_grads - inner)).astype(BF16)
        value_grad_ref[:, low:high] += dot(mix_grads, weights.astype(BF16), (1, 1))
        key_grad_ref[:, low:high] += dot(queries, score_grads, (1, 1))
        query_grads = dot(key_ref[:, low:high], score_grads, (1, 0)) * SCALE
        cosine = cosine_ref[:, cols]
        sine = sine_ref[:, cols]
        for j in range(GROUP):
            first, second = unrotate(query_grads[:, j * QUERY_BLOCK : (j + 1) * QUERY_BLOCK], cosine, sine)
            base = group * (GROUP * HEAD_SIZE) + j * HEAD_SIZE
            out_ref[pl.ds(pl.multiple_of(base, HALF), HALF), cols] = first.astype(BF16)
            out_ref[pl.ds(pl.multiple_of(base + HALF, HALF), HALF), cols] = second.astype(BF16)
    first, second = unrotate(key_grad_ref[...] * SCALE, cosine_ref[...], sine_ref[...])
    base = (QUERY_HEADS + group) * HEAD_SIZE
    out_ref[pl.ds(pl.multiple_of(base, HALF), HALF), :] = first.astype(BF16)
    out_ref[pl.ds(pl.multiple_of(base + HALF, HALF), HALF), :] = second.astype(BF16)
    base = (QUERY_HEADS + KEY_VALUE_HEADS + group) * HEAD_SIZE
    out_ref[pl.ds(pl.multiple_of(base, HEAD_SIZE), HEAD_SIZE), :] = value_grad_ref[...].astype(BF16)


def attention_back(start, cosine, sine, qkv, mix, logsum, mix_grad):
    length = qkv.shape[1]
    rows = GROUP * HEAD_SIZE
    return pl.pallas_call(
        attention_back_kernel,
        grid=(KEY_VALUE_HEADS,),
        in_specs=[
            pl.BlockSpec((1, length), lambda g: (0, 0)),
            pl.BlockSpec((HALF, length), lambda g: (0, 0)),
            pl.BlockSpec((HALF, length), lambda g: (0, 0)),
            pl.BlockSpec((rows, length), lambda g: (g, 0)),
            pl.BlockSpec((HEAD_SIZE, length), lambda g: (QUERY_HEADS + g, 0)),
            pl.BlockSpec((HEAD_SIZE, length), lambda g: (QUERY_HEADS + KEY_VALUE_HEADS + g, 0)),
            pl.BlockSpec((rows, length), lambda g: (g, 0)),
            pl.BlockSpec((1, 8, length), lambda g: (g, 0, 0)),
            pl.BlockSpec((rows, length), lambda g: (g, 0)),
        ],
        out_specs=pl.BlockSpec(qkv.shape, lambda g: (0, 0)),
        out_shape=jax.ShapeDtypeStruct(qkv.shape, BF16),
        scratch_shapes=[
            pltpu.VMEM((length, length), F32),
            pltpu.VMEM((length, HEAD_SIZE), BF16),
            pltpu.VMEM((length, HEAD_SIZE), BF16),
            pltpu.VMEM((HEAD_SIZE, length), F32),
            pltpu.VMEM((HEAD_SIZE, length), F32),
        ],
        compiler_params=pltpu.CompilerParams(vmem_limit_bytes=8 << 20),
        cost_estimate=pl.CostEstimate(flops=9_000_000_000, bytes_accessed=9_000_000, transcendentals=4_500_000),
        name="attention_back",
    )(start, cosine, sine, qkv, qkv, qkv, mix, logsum, mix_grad)


ROWS = 256
CHUNK = 512


def row_tiles(count):
    return [slice(row, row + ROWS) for row in range(0, count, ROWS)]


def whole(shape):
    return pl.BlockSpec(shape, lambda k: (0,) * len(shape))


def by_cols(rows):
    return pl.BlockSpec((rows, CHUNK), lambda k: (0, k))


def ffn_kernel(
    middle_ref, gain_ref, gate_w_ref, up_w_ref, down_w_ref,
    out_ref, normed_t_ref, gate_ref, up_ref, hidden_ref, normed_ref,
):
    tiles = row_tiles(middle_ref.shape[1])

    @pl.when(pl.program_id(0) == 0)
    def _():
        for cols in tiles:
            middle = middle_ref[:, cols]
            inverse = lax.rsqrt(jnp.mean(middle * middle, axis=0, keepdims=True) + EPSILON)
            normed = (middle * inverse * gain_ref[...]).astype(BF16)
            normed_t_ref[:, cols] = normed
            normed_ref[cols, :] = normed.T
            out_ref[:, cols] = middle

    for rows in tiles:
        normed = normed_ref[rows, :]
        gate = dot(normed, gate_w_ref[...], (1, 0))
        up = dot(normed, up_w_ref[...], (1, 0))
        gate_ref[rows, :] = gate.astype(BF16)
        up_ref[rows, :] = up.astype(BF16)
        hidden = (gate * jax.nn.sigmoid(gate) * up).astype(BF16)
        hidden_ref[rows, :] = hidden
    out_ref[...] += dot(down_w_ref[...], hidden_ref[...], (1, 1))


def ffn(middle, gain, w_gate, w_up, w_down_t):
    width, length = middle.shape
    hidden = w_gate.shape[1]
    return pl.pallas_call(
        ffn_kernel,
        grid=(hidden // CHUNK,),
        in_specs=[whole((width, length)), whole((width, 1)), by_cols(width), by_cols(width), by_cols(width)],
        out_specs=[whole((width, length)), whole((width, length)), by_cols(length), by_cols(length), by_cols(length)],
        out_shape=[
            jax.ShapeDtypeStruct((width, length), F32),
            HBM((width, length), BF16),
            HBM((length, hidden), BF16),
            HBM((length, hidden), BF16),
            HBM((length, hidden), BF16),
        ],
        scratch_shapes=[pltpu.VMEM((length, width), BF16)],
        compiler_params=pltpu.CompilerParams(vmem_limit_bytes=FFN_GRANT),
        cost_estimate=pl.CostEstimate(
            flops=6 * length * width * hidden, bytes_accessed=40_000_000, transcendentals=length * hidden
        ),
        name="ffn",
    )(middle, gain, w_gate, w_up, w_down_t)


def ffn_up_kernel(
    middle_ref, gain_ref, gate_w_ref, up_w_ref, normed_t_ref, gate_ref, up_ref, hidden_ref, normed_ref,
):
    tiles = row_tiles(middle_ref.shape[1])

    @pl.when(pl.program_id(0) == 0)
    def _():
        for cols in tiles:
            middle = middle_ref[:, cols]
            inverse = lax.rsqrt(jnp.mean(middle * middle, axis=0, keepdims=True) + EPSILON)
            normed = (middle * inverse * gain_ref[...]).astype(BF16)
            normed_t_ref[:, cols] = normed
            normed_ref[cols, :] = normed.T

    for rows in tiles:
        normed = normed_ref[rows, :]
        gate = dot(normed, gate_w_ref[...], (1, 0))
        up = dot(normed, up_w_ref[...], (1, 0))
        gate_ref[rows, :] = gate.astype(BF16)
        up_ref[rows, :] = up.astype(BF16)
        hidden_ref[rows, :] = (gate * jax.nn.sigmoid(gate) * up).astype(BF16)


def ffn_up(middle, gain, w_gate, w_up):
    width, length = middle.shape
    hidden = w_gate.shape[1]
    return pl.pallas_call(
        ffn_up_kernel,
        grid=(hidden // CHUNK,),
        in_specs=[whole((width, length)), whole((width, 1)), by_cols(width), by_cols(width)],
        out_specs=[whole((width, length)), by_cols(length), by_cols(length), by_cols(length)],
        out_shape=[HBM((width, length), BF16)] + [HBM((length, hidden), BF16)] * 3,
        scratch_shapes=[pltpu.VMEM((length, width), BF16)],
        compiler_params=pltpu.CompilerParams(vmem_limit_bytes=FFN_GRANT),
        cost_estimate=pl.CostEstimate(
            flops=4 * length * width * hidden, bytes_accessed=30_000_000, transcendentals=length * hidden
        ),
        name="ffn_up",
    )(middle, gain, w_gate, w_up)


def ffn_back_kernel(
    grad_ref, middle_ref, gain_ref, gate_ref, up_ref, gate_w_ref, up_w_ref, down_w_ref,
    out_ref, out_narrow_ref, gate_grad_ref, up_grad_ref, gain_grad_ref, branch_t_ref, total_ref, branch_ref,
):
    step = pl.program_id(0)
    tiles = row_tiles(middle_ref.shape[1])

    @pl.when(step == 0)
    def _():
        for cols in tiles:
            branch = grad_ref[:, cols].astype(BF16)
            branch_t_ref[:, cols] = branch
            branch_ref[cols, :] = branch.T

    for rows in tiles:
        hidden_grad = dot(branch_ref[rows, :], down_w_ref[...], (1, 0))
        gate = gate_ref[rows, :].astype(F32)
        up = up_ref[rows, :].astype(F32)
        sigmoid = jax.nn.sigmoid(gate)
        scaled = hidden_grad * sigmoid
        up_grad = (scaled * gate).astype(BF16)
        gate_grad = (scaled * up * (1.0 + gate * (1.0 - sigmoid))).astype(BF16)
        gate_grad_ref[rows, :] = gate_grad
        up_grad_ref[rows, :] = up_grad
    part = dot(gate_w_ref[...], gate_grad_ref[...], (1, 1)) + dot(up_w_ref[...], up_grad_ref[...], (1, 1))

    @pl.when(step == 0)
    def _():
        total_ref[...] = part

    @pl.when(step > 0)
    def _():
        total_ref[...] += part

    @pl.when(step == pl.num_programs(0) - 1)
    def _():
        gain_grad = jnp.zeros(gain_ref.shape, F32)
        for cols in tiles:
            middle = middle_ref[:, cols]
            normed_grad = total_ref[:, cols]
            inverse = lax.rsqrt(jnp.mean(middle * middle, axis=0, keepdims=True) + EPSILON)
            unit = middle * inverse
            gain_grad += jnp.sum(normed_grad * unit, axis=1, keepdims=True)
            scaled = gain_ref[...] * normed_grad
            inner = jnp.mean(scaled * unit, axis=0, keepdims=True)
            out = grad_ref[:, cols] + inverse * (scaled - unit * inner)
            out_ref[:, cols] = out
            out_narrow_ref[:, cols] = out.astype(BF16)
        gain_grad_ref[...] = gain_grad


def ffn_back(grad, middle, gain, gate, up, w_gate, w_up, w_down_t):
    width, length = middle.shape
    hidden = w_gate.shape[1]
    full = whole((width, length))
    return pl.pallas_call(
        ffn_back_kernel,
        grid=(hidden // CHUNK,),
        in_specs=[
            full, full, whole((width, 1)), by_cols(length), by_cols(length), by_cols(width), by_cols(width), by_cols(width),
        ],
        out_specs=[full, full, by_cols(length), by_cols(length), whole((width, 1)), full],
        out_shape=[
            HBM((width, length), F32),
            jax.ShapeDtypeStruct((width, length), BF16),
            HBM((length, hidden), BF16),
            HBM((length, hidden), BF16),
            jax.ShapeDtypeStruct((width, 1), F32),
            HBM((width, length), BF16),
        ],
        scratch_shapes=[pltpu.VMEM((width, length), F32), pltpu.VMEM((length, width), BF16)],
        compiler_params=pltpu.CompilerParams(vmem_limit_bytes=BACK_GRANT),
        cost_estimate=pl.CostEstimate(
            flops=6 * length * width * hidden, bytes_accessed=50_000_000, transcendentals=length * hidden
        ),
        name="ffn_back",
    )(grad, middle, gain, gate, up, w_gate, w_up, w_down_t)


def weight_grad_kernel(left_fsdp, transposed, places_ref, left_ref, right_ref, left2_ref, right2_ref, keep_ref, send_ref):
    step = pl.program_id(0)
    contract = (1, 1) if transposed else (1, 0)
    total = dot(left_ref[...], right_ref[...], contract) + dot(left2_ref[...], right2_ref[...], contract)
    total = total.astype(BF16)
    half = total.shape[0] // 2
    fsdp, core = places_ref[0], places_ref[1]
    if left_fsdp:
        for out_ref, here in ((keep_ref, step < 2), (send_ref, step >= 2)):

            @pl.when(here)
            def _():
                out_ref[fsdp] = total[:half]
                out_ref[1 - fsdp] = total[half:]

    else:
        for out_ref, first in ((keep_ref, core), (send_ref, 1 - core)):

            @pl.when(first == 0)
            def _():
                out_ref[0] = total[:half]

            @pl.when(first == 1)
            def _():
                out_ref[0] = total[half:]


def weight_grad(places, products, more_products, left_fsdp):
    left, right = products
    left2, right2 = more_products
    rows, length = left.shape
    cols = right.shape[1]
    block = cols // 4
    left_spec = pl.BlockSpec((rows, length), lambda j, places: (0, 0))
    if left_fsdp:
        right_spec = pl.BlockSpec((length, block), lambda j, places: (0, (2 * places[1] + j) % 4))
        keep_spec = pl.BlockSpec((2, rows // 2, block), lambda j, places: (0, 0, jnp.minimum(j, 1)))
        send_spec = pl.BlockSpec((2, rows // 2, block), lambda j, places: (0, 0, jnp.maximum(j - 2, 0)))
    else:
        right_spec = pl.BlockSpec((length, block), lambda j, places: (0, (2 * places[0] + j) % 4))
        keep_spec = pl.BlockSpec((1, rows // 2, block), lambda j, places: (j // 2, 0, j % 2))
        send_spec = keep_spec
    return pl.pallas_call(
        partial(weight_grad_kernel, left_fsdp, False),
        grid_spec=pltpu.PrefetchScalarGridSpec(
            num_scalar_prefetch=1,
            grid=(4,),
            in_specs=[left_spec, right_spec, left_spec, right_spec],
            out_specs=[keep_spec, send_spec],
        ),
        out_shape=[jax.ShapeDtypeStruct((2, rows // 2, cols // 2), BF16)] * 2,
        compiler_params=pltpu.CompilerParams(vmem_limit_bytes=GRAD_GRANT),
        cost_estimate=pl.CostEstimate(
            flops=4 * rows * length * cols, bytes_accessed=10 * rows * cols, transcendentals=0
        ),
        name="weight_grad",
    )(places, left, right, left2, right2)


def mixed_grad_kernel(
    places_ref, mix_ref, branch_ref, normed_ref, qkv_ref, mix2_ref, branch2_ref, normed2_ref, qkv2_ref,
    keep_ref, send_ref,
):
    width = branch_ref.shape[0]
    half_cols = keep_ref.shape[2]
    out_part = dot(mix_ref[...], branch_ref[...], (1, 1)) + dot(mix2_ref[...], branch2_ref[...], (1, 1))
    qkv_part = dot(normed_ref[...], qkv_ref[...], (1, 1)) + dot(normed2_ref[...], qkv2_ref[...], (1, 1))
    out_part = out_part.astype(BF16)
    qkv_part = qkv_part.astype(BF16)
    first = half_cols - width
    core = places_ref[1]
    for low_ref, high_ref, here in ((keep_ref, send_ref, core == 0), (send_ref, keep_ref, core == 1)):

        @pl.when(here)
        def _():
            low_ref[0, :, :width] = out_part
            low_ref[0, :, width:] = qkv_part[:, :first]
            high_ref[0] = qkv_part[:, first:]


def mixed_grad(places, products, more_products):
    (mix, branch), (normed, qkv) = products
    (mix2, branch2), (normed2, qkv2) = more_products
    rows, length = mix.shape
    cols = branch.shape[0] + qkv.shape[0]
    left = pl.BlockSpec((rows // 2, length), lambda j, places: ((places[0] + j) % 2, 0))
    fixed = lambda shape: pl.BlockSpec(shape, lambda j, places: (0, 0))
    specs = [left, fixed(branch.shape), left, fixed(qkv.shape)]
    return pl.pallas_call(
        mixed_grad_kernel,
        grid_spec=pltpu.PrefetchScalarGridSpec(
            num_scalar_prefetch=1,
            grid=(2,),
            in_specs=specs + specs,
            out_specs=[pl.BlockSpec((1, rows // 2, cols // 2), lambda j, places: (j, 0, 0))] * 2,
        ),
        out_shape=[jax.ShapeDtypeStruct((2, rows // 2, cols // 2), BF16)] * 2,
        compiler_params=pltpu.CompilerParams(vmem_limit_bytes=MIXED_GRANT),
        cost_estimate=pl.CostEstimate(
            flops=4 * rows * length * cols, bytes_accessed=10 * rows * cols, transcendentals=0
        ),
        name="mixed_grad",
    )(places, mix, branch, normed, qkv, mix2, branch2, normed2, qkv2)


def assemble_kernel(stack_cores, cuts, places_ref, *refs):
    core, side = places_ref[1], places_ref[2]
    inputs, outputs = refs[:4], refs[4:]
    count, cols = inputs[0].shape
    whole_ref = outputs[-1]
    for k, piece_ref in enumerate(inputs):
        at_side = jnp.bitwise_xor(side, k % 2)
        at_core = jnp.bitwise_xor(core, k // 2)
        row = at_side * count + (at_core * (2 * count) if stack_cores else 0)
        rows = pl.ds(pl.multiple_of(row, 8), count)
        value = piece_ref[...].astype(F32)
        if stack_cores:
            whole_ref[rows, :] = value
        else:
            whole_ref[rows, pl.ds(pl.multiple_of(at_core * cols, 128), cols)] = value
    for out_ref, (low, high) in zip(outputs[:-1], cuts):
        value = whole_ref[:, low:high]
        out_ref[...] = value.T if out_ref.shape[0] == high - low else value


def assemble(places, pieces, stack_cores, cuts=()):
    count, cols = pieces[0].shape
    shape = (4 * count, cols) if stack_cores else (2 * count, 2 * cols)
    out_shape = [
        jax.ShapeDtypeStruct((high - low, shape[0]) if high - low < shape[0] else (shape[0], high - low), F32)
        for low, high in cuts
    ]
    out_shape = out_shape or [jax.ShapeDtypeStruct(shape, F32)]
    return pl.pallas_call(
        partial(assemble_kernel, stack_cores, cuts),
        grid_spec=pltpu.PrefetchScalarGridSpec(
            num_scalar_prefetch=1,
            grid=(1,),
            in_specs=[pl.BlockSpec((count, cols), lambda j, places: (0, 0))] * 4,
            out_specs=[pl.BlockSpec(out.shape, lambda j, places: (0, 0)) for out in out_shape],
            scratch_shapes=[pltpu.VMEM(shape, F32)] if cuts else [],
        ),
        out_shape=out_shape,
        compiler_params=pltpu.CompilerParams(vmem_limit_bytes=24 << 20),
        cost_estimate=pl.CostEstimate(flops=0, bytes_accessed=24 * count * cols, transcendentals=0),
        name="assemble",
    )(places, *pieces)


def doc_tables(doc_row):
    token_index = jnp.arange(doc_row.shape[0])
    start = jnp.sum((doc_row[:, None] < doc_row[None, :]).astype(jnp.int32), axis=0)
    places = (token_index - start).astype(F32)
    frequency = ROPE_BASE ** (-2.0 * jnp.arange(HALF, dtype=F32) / HEAD_SIZE)
    angles = frequency[:, None] * places[None, :]
    return (start[None, :], jnp.cos(angles), jnp.sin(angles))


def norm_forward(inputs, gain):
    inverse = lax.rsqrt(jnp.mean(inputs * inputs, axis=0, keepdims=True) + EPSILON)
    return (inputs * inverse * gain).astype(BF16)


def norm_backward(inputs, gain, grad):
    inverse = lax.rsqrt(jnp.mean(inputs * inputs, axis=0, keepdims=True) + EPSILON)
    scaled = gain * grad
    inner = jnp.mean(scaled * inputs, axis=0, keepdims=True)
    return (inverse * scaled - inputs * inverse**3 * inner, jnp.sum(grad * inputs * inverse, axis=1, keepdims=True))


def project(inputs, w_qkv, gains, tables):
    _, cosine, sine = tables
    length = inputs.shape[1]
    normed = norm_forward(inputs, gains[0])
    raw = dot(w_qkv, normed, (0, 0))
    heads = QUERY_HEADS + KEY_VALUE_HEADS
    pairs = raw[: heads * HEAD_SIZE].reshape(heads, 2, HALF, length)
    first, second = pairs[:, 0], pairs[:, 1]
    rotated = jnp.stack([first * cosine - second * sine, second * cosine + first * sine], axis=1)
    qkv = jnp.concatenate(
        [rotated.reshape(heads * HEAD_SIZE, length).astype(BF16), raw[heads * HEAD_SIZE :].astype(BF16)], axis=0
    )
    return (normed, qkv)


def project_out(inputs, w_out, mix):
    return inputs + dot(w_out, mix, (0, 0))


def attention_backward(kept, attn_grad, weights, tables):
    start, cosine, sine = tables
    _, _, qkv, logsum, mix = kept
    mix_grad = dot(weights[1], attn_grad, (1, 0)).astype(BF16)
    return attention_back(start, cosine, sine, qkv, mix, logsum, mix_grad)


def input_backward(kept, middle_grad, qkv_grad, weights, gains):
    normed_grad = dot(weights[0], qkv_grad, (1, 0))
    inputs_grad, gain_grad = norm_backward(kept[0], gains[0], normed_grad)
    return (inputs_grad + middle_grad, gain_grad)


def after(value, *earlier):
    return lax.optimization_barrier((value,) + earlier)[0]


def swap_fsdp(value):
    return lax.ppermute(value, "fsdp", [(0, 1), (1, 0)])


def swap_dp(value, bit, size=16):
    return lax.ppermute(value, "dp", [(i, i ^ bit) for i in range(size)])


def fetch(parts, axis, index, pieces):
    sent = [cut_piece(part, index, axis, pieces) for part in parts]
    sent = jnp.concatenate(sent, axis=1) if len(sent) > 1 else sent[0]
    return sent


def cut_piece(value, index, axis, pieces):
    count = value.shape[axis] // pieces
    return lax.dynamic_slice_in_dim(value, index * count, count, axis)


def join_kernel(own_count, shard_axis, piece_axis, index_at, places_ref, *refs):
    own, pieces, out_ref = refs[:own_count], refs[own_count:-1], refs[-1]
    rows, cols = out_ref.shape
    fsdp = places_ref[0]
    index = places_ref[index_at]
    if shard_axis == 0:
        half = pl.ds(pl.multiple_of(fsdp * (rows // 2), 16), rows // 2)
        at = 0
        for ref in own:
            out_ref[half, at : at + ref.shape[1]] = ref[...]
            at += ref.shape[1]
    else:
        out_ref[:, pl.ds(pl.multiple_of(fsdp * (cols // 2), 128), cols // 2)] = own[0][...]
    for flip, ref in enumerate(pieces):
        at = jnp.bitwise_xor(index, flip)
        count, width = ref.shape
        row = at * count if piece_axis == 0 else 0
        col = at * width if piece_axis == 1 else 0
        if shard_axis == 0:
            row = row + (1 - fsdp) * (rows // 2)
        else:
            col = col + (1 - fsdp) * (cols // 2)
        row_at = pl.ds(pl.multiple_of(row, 16), count)
        if shard_axis == 0 and piece_axis == 0:
            out_ref[row_at, :] = ref[...]
        else:
            out_ref[row_at, pl.ds(pl.multiple_of(col, 128), width)] = ref[...]


def join(places, own, pieces, shard_axis, piece_axis, index_at):
    rows, cols = own[0].shape[0], sum(part.shape[1] for part in own)
    shape = (2 * rows, cols) if shard_axis == 0 else (rows, 2 * cols)
    full = lambda shape: pl.BlockSpec(shape, lambda j, places: (0, 0))
    return pl.pallas_call(
        partial(join_kernel, len(own), shard_axis, piece_axis, index_at),
        grid_spec=pltpu.PrefetchScalarGridSpec(
            num_scalar_prefetch=1,
            grid=(1,),
            in_specs=[full(part.shape) for part in (*own, *pieces)],
            out_specs=full(shape),
        ),
        out_shape=jax.ShapeDtypeStruct(shape, BF16),
        compiler_params=pltpu.CompilerParams(vmem_limit_bytes=24 << 20),
        cost_estimate=pl.CostEstimate(flops=0, bytes_accessed=4 * shape[0] * shape[1], transcendentals=0),
        name="join",
    )(places, *own, *pieces)


def add(left, right):
    return (left.astype(F32) + right.astype(F32)).astype(BF16)


def add3(first, second, third):
    return ((first.astype(F32) + second.astype(F32)) + third.astype(F32)).astype(BF16)


def reduce_vector(values):
    total = values
    for bit in (1, 2, 4, 8):
        total = add(total, swap_dp(total, bit))
    total = add(total, swap_fsdp(total))
    count = values.shape[1] // 2
    return lax.dynamic_slice_in_dim(total, lax.axis_index("fsdp") * count, count, 1)


def gather_gains(gains):
    other = swap_fsdp(gains)
    first = lax.axis_index("fsdp") == 0
    return jnp.concatenate([jnp.where(first, gains, other), jnp.where(first, other, gains)], axis=1)


def cut(value, which, axis):
    count = value.shape[axis] // 2
    return lax.dynamic_slice_in_dim(value, which * count, count, axis)


def sides():
    place = lax.axis_index("dp")
    return ((place // 2) % 2, (place // 4) % 2, (place // 8) % 2)


class Reduction:
    def __init__(self, halves, queue=()):
        self.keep, send = halves
        self.received = swap_dp(after(send, *queue), 1)
        self.side, self.lane, _ = sides()
        self.plan = iter((self.fsdp, self.y, self.z_near, self.z_far, self.z_back, self.y_back, self.finish))

    def step(self, queue):
        mine = next(self.plan)(lambda value: after(value, *queue))
        queue[:] = [mine]

    def split(self, value, which, axis, bit):
        mine, self.own = cut(value, 1 - which, axis), cut(value, which, axis)
        self.incoming = swap_dp(mine, bit)
        return mine

    def fsdp(self, gate):
        mine = add(gate(self.keep)[1], self.received[1])
        self.incoming = swap_fsdp(mine)
        return mine

    def fsdp_sum(self, gate):
        return add3(gate(self.keep)[0], self.received[0], self.incoming)

    def y(self, gate):
        return self.split(self.fsdp_sum(gate), self.side, 0, 2)

    def z_near(self, gate):
        return self.split(add(gate(self.own), self.incoming), self.lane, 1, 4)

    def z_far(self, gate):
        self.own = add(gate(self.own), self.incoming)
        self.incoming = swap_dp(self.own, 8)
        return self.own

    def z_back(self, gate):
        self.own = add(gate(self.own), self.incoming)
        self.incoming = swap_dp(self.own, 4)
        return self.own

    def y_back(self, gate):
        mine = self.own = put_together(gate(self.own), self.incoming, self.lane, 1)
        self.across = swap_dp(mine, 2)
        self.beside = swap_dp(mine, 1)
        return mine

    def finish(self, gate):
        mine = gate(self.across)
        self.pieces = (self.own, mine, self.beside, swap_dp(mine, 1))
        return mine


class ReductionOverZ(Reduction):
    def __init__(self, halves, queue=()):
        super().__init__(halves, queue)
        self.far = sides()[2]
        self.plan = iter((self.fsdp, self.first, self.second, self.over_y, self.back_far, self.back_near, self.done))

    def first(self, gate):
        return self.split(self.fsdp_sum(gate), self.lane, 0, 4)

    def second(self, gate):
        return self.split(add(gate(self.own), self.incoming), self.far, 0, 8)

    def over_y(self, gate):
        self.own = add(gate(self.own), self.incoming)
        self.incoming = swap_dp(self.own, 2)
        return self.own

    def back_far(self, gate):
        self.own = add(gate(self.own), self.incoming)
        self.incoming = swap_dp(self.own, 8)
        return self.own

    def back_near(self, gate):
        mine = self.own = put_together(gate(self.own), self.incoming, self.far, 0)
        self.across = swap_dp(mine, 4)
        self.beside = swap_dp(mine, 1)
        return mine

    def done(self, gate):
        mine = gate(self.across)
        self.pieces = (self.own, mine, self.beside, swap_dp(mine, 1))
        return mine


class ReductionBothWays(Reduction):
    def __init__(self, halves, queue=()):
        super().__init__(halves, queue)
        self.plan = iter((self.one, self.two, self.three, self.z_far, self.z_back, self.y_back, self.finish))

    def one(self, gate):
        keep = gate(self.keep)
        half = keep.shape[2] // 2
        theirs = add(keep[1, :, :half], self.received[1, :, :half])
        self.over_x = swap_fsdp(theirs)
        both = add(keep[:, :, half:], self.received[:, :, half:])
        mine, self.both = cut(both, 1 - self.side, 1), cut(both, self.side, 1)
        self.over_y = swap_dp(mine, 2)
        return mine

    def two(self, gate):
        half = self.keep.shape[2] // 2
        first = add3(gate(self.keep)[0, :, :half], self.received[0, :, :half], self.over_x)
        mine, self.first = cut(first, 1 - self.side, 0), cut(first, self.side, 0)
        self.over_y_too = swap_dp(mine, 2)
        theirs = add(gate(self.both)[1], self.over_y[1])
        self.over_x_too = swap_fsdp(theirs)
        return theirs

    def three(self, gate):
        first = add(gate(self.first), self.over_y_too)
        second = add3(gate(self.both)[0], self.over_y[0], self.over_x_too)
        mine = jnp.where(self.lane == 0, second, first)
        self.own = jnp.where(self.lane == 0, first, second)
        self.incoming = swap_dp(mine, 4)
        return mine


def put_together(own, other, which, axis):
    low = jnp.where(which == 0, own, other)
    high = jnp.where(which == 0, other, own)
    return jnp.concatenate([low, high], axis=axis)


def make_body(fsdp_size, dp_size):
    paired = fsdp_size == 2 and dp_size == 16

    def body(
        activations, doc_ids, w_query, key_projection, value_projection, w_out,
        gain_attn, gain_ffn, w_gate, w_up, w_down, cotangent,
    ):
        if paired:
            place = lax.axis_index("dp")
            core, side, lane = place % 2, (place // 2) % 2, (place // 4) % 2
            index_y, index_z = place % 4, core + 2 * lane
            places = jnp.stack([lax.axis_index("fsdp"), core, side, index_y, index_z]).astype(jnp.int32)
            qkv_own = (w_query, key_projection, value_projection)
            qkv_sent = fetch(qkv_own, 0, core, 2)
            out_sent = fetch((after(w_out, qkv_sent),), 0, core, 2)
            gate_sent = fetch((after(w_gate, out_sent),), 1, index_y, 4)
            up_sent = fetch((after(w_up, gate_sent),), 1, index_z, 4)
            down_sent = fetch((after(w_down.T, up_sent),), 0, index_y, 4)
            qkv_mine = swap_fsdp(qkv_sent)
            gains = gather_gains(after(jnp.stack([gain_attn, gain_ffn]), qkv_sent)).astype(F32)
            out_mine, gate_mine, up_mine, down_mine = [
                swap_fsdp(sent) for sent in (out_sent, gate_sent, up_sent, down_sent)
            ]
            w_qkv = join(places, qkv_own, (qkv_mine, swap_dp(qkv_mine, 1)), 0, 0, 1)
        else:
            collect = lambda shard, axis: lax.all_gather(shard, "fsdp", axis=axis, tiled=True)
            gains = collect(jnp.stack([gain_attn, gain_ffn]), 1).astype(F32)
            places = jnp.zeros((4,), jnp.int32)
            qkv_shard = jnp.concatenate([w_query, key_projection, value_projection], axis=1)
            weights = (
                collect(qkv_shard, 0), collect(w_out, 0), collect(w_gate, 0), collect(w_up, 0), collect(w_down, 0).T,
            )
        gains = (gains[0][:, None], gains[1][:, None])
        tables = doc_tables(doc_ids[0])
        start, cosine, sine = tables
        inputs = activations[0].T.astype(F32)

        if paired:
            normed, qkv = project(inputs, w_qkv, gains, tables)
            out_mine = after(out_mine, qkv)
            gate_mine = after(gate_mine, out_mine)
            out_beside = swap_dp(out_mine, 1)
            gate_across, gate_beside = swap_dp(gate_mine, 2), swap_dp(gate_mine, 1)
            mix, logsum = attention(start, qkv)
            up_mine = after(up_mine, mix)
            up_across, up_beside = swap_dp(up_mine, 4), swap_dp(up_mine, 1)
            gate_across = after(gate_across, up_mine)
            gate_corner = swap_dp(gate_across, 1)
            w_out_full = join(places, (w_out,), (out_mine, out_beside), 0, 0, 1)
            middle = project_out(inputs, w_out_full, mix)
            down_mine = after(down_mine, middle)
            down_across, down_beside = swap_dp(down_mine, 2), swap_dp(down_mine, 1)
            gate_pieces = (after(gate_mine, down_mine), gate_beside, gate_across, gate_corner)
            w_gate_full = join(places, (w_gate,), gate_pieces, 0, 1, 3)
            up_across = after(up_across, w_gate_full)
            w_up_full = join(places, (w_up,), (up_mine, up_beside, up_across, swap_dp(up_across, 1)), 0, 1, 4)
            first_normed, first_gate, first_up, first_hidden = ffn_up(middle, gains[1], w_gate_full, w_up_full)
            down_across = after(down_across, first_hidden)
            w_down_full = join(
                places, (w_down.T,), (down_mine, down_beside, down_across, swap_dp(down_across, 1)), 1, 0, 3
            )
            weights = (w_qkv, w_out_full, w_gate_full, w_up_full, w_down_full)
            ffn_weights = weights[2:]
        else:
            ffn_weights = weights[2:]
            normed, qkv = project(inputs, weights[0], gains, tables)
            mix, logsum = attention(start, qkv)
            middle = project_out(inputs, weights[1], mix)
            first_normed, first_gate, first_up, first_hidden = ffn_up(middle, gains[1], *ffn_weights[:2])
        first = (inputs, normed, qkv, logsum, mix)
        inputs2 = middle + dot(ffn_weights[2], first_hidden, (1, 1))
        normed2, qkv2 = project(inputs2, weights[0], gains, tables)
        mix2, logsum2 = attention(start, qkv2)
        middle2 = project_out(inputs2, weights[1], mix2)
        second = (inputs2, normed2, qkv2, logsum2, mix2)
        outputs, second_normed, second_gate, second_up, second_hidden = ffn(middle2, gains[1], *ffn_weights)

        grad = cotangent[0].T.astype(F32)
        grad, attn_grad2, gate_grad2, up_grad2, ffn_gain2, branch2 = ffn_back(
            grad, middle2, gains[1], second_gate, second_up, *ffn_weights
        )
        qkv_grad2 = attention_backward(second, attn_grad2, weights, tables)
        grad, attn_gain2 = input_backward(second, grad, qkv_grad2, weights, gains)

        down_halves = weight_grad(
            places, (branch2, second_hidden), (grad.astype(BF16), first_hidden), False
        )
        queue = []
        if paired:
            down = Reduction(down_halves)
            down.step(queue)
            grad = after(grad, *queue)
        else:
            grad = after(grad, *down_halves)
        grad, attn_grad, gate_grad, up_grad, ffn_gain, _ = ffn_back(
            grad, middle, gains[1], first_gate, first_up, *ffn_weights
        )
        if paired:
            down.step(queue)
            gate_grad = after(gate_grad, *queue)
        gate_halves = weight_grad(places, (second_normed, gate_grad2), (first_normed, gate_grad), True)
        if paired:
            queue.append(gate_halves[0])
            down.step(queue)
            gate = Reduction(gate_halves, queue)
        mix_grad_in = after(attn_grad, *gate_halves)
        mix_grad = dot(weights[1], mix_grad_in, (1, 0)).astype(BF16)
        if paired:
            queue.append(mix_grad)
            gate.step(queue)
            up_grad = after(up_grad, *queue)
        up_halves = weight_grad(places, (second_normed, up_grad2), (first_normed, up_grad), True)
        if paired:
            queue.append(up_halves[0])
            down.step(queue)
            up = Reduction(up_halves, queue)
            up.step(queue)
            mix_grad = after(mix_grad, *queue)
        qkv_grad = attention_back(start, cosine, sine, first[2], first[4], first[3], mix_grad)
        if paired:
            queue.append(qkv_grad)
            down.step(queue)
            gate.step(queue)
            qkv_grad = after(qkv_grad, *queue)
        mixed_halves = mixed_grad(
            places,
            ((second[4], attn_grad2), (second[1], qkv_grad2)),
            ((first[4], attn_grad), (first[1], qkv_grad)),
        )
        if paired:
            mixed = Reduction(mixed_halves)
            queue.append(mixed_halves[0])
            down.step(queue)
            gate.step(queue)
            up.step(queue)
            mixed.step(queue)
            grad = after(grad, *queue)
        grad, attn_gain = input_backward(first, grad, after(qkv_grad, *mixed_halves), weights, gains)
        gain_grads = jnp.concatenate([attn_gain + attn_gain2, ffn_gain + ffn_gain2], axis=1).T.astype(BF16)

        width = w_query.shape[1]
        key_end = width + key_projection.shape[1]
        value_end = key_end + value_projection.shape[1]
        cuts = ((0, width), (width, 2 * width), (2 * width, width + key_end), (width + key_end, width + value_end))
        if paired:
            grad_narrow = grad.T.astype(BF16)[None]
            queue.append(grad_narrow)
            down.step(queue)
            gate.step(queue)
            up.step(queue)
            mixed.step(queue)
            gate.step(queue)
            up.step(queue)
            gate.step(queue)
            mixed.step(queue)
            (grad_down,) = assemble(places, [after(down.pieces[0], *queue), *down.pieces[1:]], True)
            queue.append(grad_down)
            up.step(queue)
            mixed.step(queue)
            up.step(queue)
            mixed.step(queue)
            gate.step(queue)
            mixed.step(queue)
            (grad_gate,) = assemble(places, [after(gate.pieces[0], *queue), *gate.pieces[1:]], False)
            queue.append(grad_gate)
            up.step(queue)
            (grad_up,) = assemble(places, [after(up.pieces[0], *queue), *up.pieces[1:]], False)
            queue.append(grad_up)
            mixed.step(queue)
            grad_out, grad_query, grad_key, grad_value = assemble(places, mixed.pieces, False, cuts)
            grad_key, grad_value = grad_key.T, grad_value.T
            gain_grads = reduce_vector(gain_grads).astype(F32)
        else:
            grad_narrow = grad.T.astype(BF16)[None]

            def reduce(value, axis):
                part = lax.psum_scatter(value, "fsdp", scatter_dimension=axis, tiled=True)
                return lax.psum(part, "dp").astype(F32)

            rows = lambda halves: jnp.concatenate([h.reshape(-1, h.shape[2]) for h in halves], axis=1)
            cols = lambda halves: jnp.concatenate([jnp.concatenate([h[0], h[1]], axis=1) for h in halves])
            grad_down = reduce(cols(down_halves).T, 0).T
            grad_gate = reduce(rows(gate_halves), 0)
            grad_up = reduce(rows(up_halves), 0)
            mixed = reduce(rows(mixed_halves), 0)
            grad_out, grad_query, grad_key, grad_value = [mixed[:, low:high] for low, high in cuts]
            gain_grads = reduce(gain_grads, 1)
        return (
            outputs.T.astype(BF16)[None],
            grad_narrow,
            grad_query,
            grad_key,
            grad_value,
            grad_out,
            gain_grads[0],
            gain_grads[1],
            grad_gate,
            grad_up,
            grad_down.T,
        )

    return body


def solution(mesh):
    sequences = P(("dp", "fsdp"), None, None)
    rows = P("fsdp", None)
    vector = P("fsdp")
    in_specs = (
        sequences, P(("dp", "fsdp"), None), rows, rows, rows, rows, vector, vector, rows, rows, rows, sequences,
    )
    out_specs = (sequences, sequences, rows, rows, rows, rows, vector, vector, rows, rows, rows)
    body = make_body(mesh.shape["fsdp"], mesh.shape["dp"])
    return jax.shard_map(body, mesh=mesh, in_specs=in_specs, out_specs=out_specs, check_vma=False)
```

```python
from functools import partial

import jax
import jax.numpy as jnp
from jax import lax
from jax.experimental import pallas as pl
from jax.experimental.pallas import tpu as pltpu
from jax.sharding import PartitionSpec as P

QUERY_HEADS = 15
KEY_VALUE_HEADS = 5
GROUP = QUERY_HEADS // KEY_VALUE_HEADS
HEAD_SIZE = 64
HALF = HEAD_SIZE // 2
LONGEST_DOC = 384
EPSILON = 1e-05
ROPE_BASE = 10000.0
NEGATIVE = -1e30
SCALE = HEAD_SIZE ** (-0.5)
QUERY_BLOCK = 128
BF16 = jnp.bfloat16
F32 = jnp.float32
HBM = pltpu.HBM
FFN_GRANT = 24 << 20
BACK_GRANT = 40 << 20
GRAD_GRANT = 24 << 20
MIXED_GRANT = 36 << 20


def dot(left, right, contract):
    return lax.dot_general(left, right, ((contract[:1], contract[1:]), ((), ())), preferred_element_type=F32)


def key_window(block):
    return (max(0, block * QUERY_BLOCK - LONGEST_DOC), (block + 1) * QUERY_BLOCK)


def fill_mask(start_ref, mask_ref):
    for block in range(mask_ref.shape[0] // QUERY_BLOCK):
        low, high = key_window(block)
        cols = slice(block * QUERY_BLOCK, high)
        shape = (high - low, QUERY_BLOCK)
        key = low + lax.broadcasted_iota(jnp.int32, shape, 0)
        query = block * QUERY_BLOCK + lax.broadcasted_iota(jnp.int32, shape, 1)
        allowed = (key >= start_ref[:, cols]) & (key <= query)
        mask_ref[low:high, cols] = jnp.where(allowed, 0.0, NEGATIVE)


def side_by_side(ref, cols):
    return jnp.concatenate([ref[j * HEAD_SIZE : (j + 1) * HEAD_SIZE, cols] for j in range(GROUP)], axis=1)


def attention_kernel(start_ref, query_ref, key_ref, value_ref, mix_ref, logsum_ref, mask_ref, key_rows_ref):
    @pl.when(pl.program_id(0) == 0)
    def _():
        fill_mask(start_ref, mask_ref)

    key_rows_ref[...] = key_ref[...].T
    for block in range(query_ref.shape[1] // QUERY_BLOCK):
        low, high = key_window(block)
        cols = slice(block * QUERY_BLOCK, high)
        queries = side_by_side(query_ref, cols)
        mask = jnp.concatenate([mask_ref[low:high, cols]] * GROUP, axis=1)
        scores = dot(key_rows_ref[low:high, :], queries, (1, 0)) * SCALE + mask
        top = jnp.max(scores, axis=0, keepdims=True)
        weights = jnp.exp(scores - top)
        total = jnp.sum(weights, axis=0, keepdims=True)
        mix = dot(value_ref[:, low:high], weights.astype(BF16), (1, 0))
        mix = (mix / total).astype(BF16)
        logsum = top + jnp.log(total)
        for j in range(GROUP):
            part = slice(j * QUERY_BLOCK, (j + 1) * QUERY_BLOCK)
            mix_ref[j * HEAD_SIZE : (j + 1) * HEAD_SIZE, cols] = mix[:, part]
            logsum_ref[0, j : j + 1, cols] = logsum[:, part]


def attention(start, qkv):
    length = qkv.shape[1]
    rows = GROUP * HEAD_SIZE
    return pl.pallas_call(
        attention_kernel,
        grid=(KEY_VALUE_HEADS,),
        in_specs=[
            pl.BlockSpec((1, length), lambda g: (0, 0)),
            pl.BlockSpec((rows, length), lambda g: (g, 0)),
            pl.BlockSpec((HEAD_SIZE, length), lambda g: (QUERY_HEADS + g, 0)),
            pl.BlockSpec((HEAD_SIZE, length), lambda g: (QUERY_HEADS + KEY_VALUE_HEADS + g, 0)),
        ],
        out_specs=[
            pl.BlockSpec((rows, length), lambda g: (g, 0)),
            pl.BlockSpec((1, 8, length), lambda g: (g, 0, 0)),
        ],
        out_shape=[
            jax.ShapeDtypeStruct((QUERY_HEADS * HEAD_SIZE, length), BF16),
            jax.ShapeDtypeStruct((KEY_VALUE_HEADS, 8, length), F32),
        ],
        scratch_shapes=[pltpu.VMEM((length, length), F32), pltpu.VMEM((length, HEAD_SIZE), BF16)],
        compiler_params=pltpu.CompilerParams(vmem_limit_bytes=8 << 20),
        cost_estimate=pl.CostEstimate(flops=6_000_000_000, bytes_accessed=4_000_000, transcendentals=4_500_000),
        name="attention",
    )(start, qkv, qkv, qkv)


def unrotate(rows, cosine, sine):
    first = rows[:HALF]
    second = rows[HALF:]
    return (first * cosine + second * sine, second * cosine - first * sine)


def attention_back_kernel(
    start_ref, cosine_ref, sine_ref, query_ref, key_ref, value_ref, mix_ref, logsum_ref, mix_grad_ref,
    out_ref, mask_ref, key_rows_ref, value_rows_ref, key_grad_ref, value_grad_ref,
):
    group = pl.program_id(0)

    @pl.when(group == 0)
    def _():
        fill_mask(start_ref, mask_ref)

    key_rows_ref[...] = key_ref[...].T
    value_rows_ref[...] = value_ref[...].T
    key_grad_ref[...] = jnp.zeros_like(key_grad_ref)
    value_grad_ref[...] = jnp.zeros_like(value_grad_ref)
    for block in range(query_ref.shape[1] // QUERY_BLOCK):
        low, high = key_window(block)
        cols = slice(block * QUERY_BLOCK, high)
        queries = side_by_side(query_ref, cols)
        mix_grads = side_by_side(mix_grad_ref, cols)
        mixes = side_by_side(mix_ref, cols)
        inner = jnp.sum(mix_grads.astype(F32) * mixes.astype(F32), axis=0, keepdims=True)
        logsum = jnp.concatenate([logsum_ref[0, j : j + 1, cols] for j in range(GROUP)], axis=1)
        mask = jnp.concatenate([mask_ref[low:high, cols]] * GROUP, axis=1)
        scores = dot(key_rows_ref[low:high, :], queries, (1, 0)) * SCALE + mask
        weights = jnp.exp(scores - logsum)
        weight_grads = dot(value_rows_ref[low:high, :], mix_grads, (1, 0))
        score_grads = (weights * (weight_grads - inner)).astype(BF16)
        value_grad_ref[:, low:high] += dot(mix_grads, weights.astype(BF16), (1, 1))
        key_grad_ref[:, low:high] += dot(queries, score_grads, (1, 1))
        query_grads = dot(key_ref[:, low:high], score_grads, (1, 0)) * SCALE
        cosine = cosine_ref[:, cols]
        sine = sine_ref[:, cols]
        for j in range(GROUP):
            first, second = unrotate(query_grads[:, j * QUERY_BLOCK : (j + 1) * QUERY_BLOCK], cosine, sine)
            base = group * (GROUP * HEAD_SIZE) + j * HEAD_SIZE
            out_ref[pl.ds(pl.multiple_of(base, HALF), HALF), cols] = first.astype(BF16)
            out_ref[pl.ds(pl.multiple_of(base + HALF, HALF), HALF), cols] = second.astype(BF16)
    first, second = unrotate(key_grad_ref[...] * SCALE, cosine_ref[...], sine_ref[...])
    base = (QUERY_HEADS + group) * HEAD_SIZE
    out_ref[pl.ds(pl.multiple_of(base, HALF), HALF), :] = first.astype(BF16)
    out_ref[pl.ds(pl.multiple_of(base + HALF, HALF), HALF), :] = second.astype(BF16)
    base = (QUERY_HEADS + KEY_VALUE_HEADS + group) * HEAD_SIZE
    out_ref[pl.ds(pl.multiple_of(base, HEAD_SIZE), HEAD_SIZE), :] = value_grad_ref[...].astype(BF16)


def attention_back(start, cosine, sine, qkv, mix, logsum, mix_grad):
    length = qkv.shape[1]
    rows = GROUP * HEAD_SIZE
    return pl.pallas_call(
        attention_back_kernel,
        grid=(KEY_VALUE_HEADS,),
        in_specs=[
            pl.BlockSpec((1, length), lambda g: (0, 0)),
            pl.BlockSpec((HALF, length), lambda g: (0, 0)),
            pl.BlockSpec((HALF, length), lambda g: (0, 0)),
            pl.BlockSpec((rows, length), lambda g: (g, 0)),
            pl.BlockSpec((HEAD_SIZE, length), lambda g: (QUERY_HEADS + g, 0)),
            pl.BlockSpec((HEAD_SIZE, length), lambda g: (QUERY_HEADS + KEY_VALUE_HEADS + g, 0)),
            pl.BlockSpec((rows, length), lambda g: (g, 0)),
            pl.BlockSpec((1, 8, length), lambda g: (g, 0, 0)),
            pl.BlockSpec((rows, length), lambda g: (g, 0)),
        ],
        out_specs=pl.BlockSpec(qkv.shape, lambda g: (0, 0)),
        out_shape=jax.ShapeDtypeStruct(qkv.shape, BF16),
        scratch_shapes=[
            pltpu.VMEM((length, length), F32),
            pltpu.VMEM((length, HEAD_SIZE), BF16),
            pltpu.VMEM((length, HEAD_SIZE), BF16),
            pltpu.VMEM((HEAD_SIZE, length), F32),
            pltpu.VMEM((HEAD_SIZE, length), F32),
        ],
        compiler_params=pltpu.CompilerParams(vmem_limit_bytes=8 << 20),
        cost_estimate=pl.CostEstimate(flops=9_000_000_000, bytes_accessed=9_000_000, transcendentals=4_500_000),
        name="attention_back",
    )(start, cosine, sine, qkv, qkv, qkv, mix, logsum, mix_grad)


ROWS = 256
CHUNK = 512


def row_tiles(count):
    return [slice(row, row + ROWS) for row in range(0, count, ROWS)]


def whole(shape):
    return pl.BlockSpec(shape, lambda k: (0,) * len(shape))


def by_cols(rows):
    return pl.BlockSpec((rows, CHUNK), lambda k: (0, k))


def ffn_kernel(
    middle_ref, gain_ref, gate_w_ref, up_w_ref, down_w_ref,
    out_ref, normed_t_ref, gate_ref, up_ref, hidden_ref, normed_ref,
):
    tiles = row_tiles(middle_ref.shape[1])

    @pl.when(pl.program_id(0) == 0)
    def _():
        for cols in tiles:
            middle = middle_ref[:, cols]
            inverse = lax.rsqrt(jnp.mean(middle * middle, axis=0, keepdims=True) + EPSILON)
            normed = (middle * inverse * gain_ref[...]).astype(BF16)
            normed_t_ref[:, cols] = normed
            normed_ref[cols, :] = normed.T
            out_ref[:, cols] = middle

    for rows in tiles:
        normed = normed_ref[rows, :]
        gate = dot(normed, gate_w_ref[...], (1, 0))
        up = dot(normed, up_w_ref[...], (1, 0))
        gate_ref[rows, :] = gate.astype(BF16)
        up_ref[rows, :] = up.astype(BF16)
        hidden = (gate * jax.nn.sigmoid(gate) * up).astype(BF16)
        hidden_ref[rows, :] = hidden
    out_ref[...] += dot(down_w_ref[...], hidden_ref[...], (1, 1))


def ffn(middle, gain, w_gate, w_up, w_down_t):
    width, length = middle.shape
    hidden = w_gate.shape[1]
    return pl.pallas_call(
        ffn_kernel,
        grid=(hidden // CHUNK,),
        in_specs=[whole((width, length)), whole((width, 1)), by_cols(width), by_cols(width), by_cols(width)],
        out_specs=[whole((width, length)), whole((width, length)), by_cols(length), by_cols(length), by_cols(length)],
        out_shape=[
            jax.ShapeDtypeStruct((width, length), F32),
            HBM((width, length), BF16),
            HBM((length, hidden), BF16),
            HBM((length, hidden), BF16),
            HBM((length, hidden), BF16),
        ],
        scratch_shapes=[pltpu.VMEM((length, width), BF16)],
        compiler_params=pltpu.CompilerParams(vmem_limit_bytes=FFN_GRANT),
        cost_estimate=pl.CostEstimate(
            flops=6 * length * width * hidden, bytes_accessed=40_000_000, transcendentals=length * hidden
        ),
        name="ffn",
    )(middle, gain, w_gate, w_up, w_down_t)


def ffn_up_kernel(
    middle_ref, gain_ref, gate_w_ref, up_w_ref, normed_t_ref, gate_ref, up_ref, hidden_ref, normed_ref,
):
    tiles = row_tiles(middle_ref.shape[1])

    @pl.when(pl.program_id(0) == 0)
    def _():
        for cols in tiles:
            middle = middle_ref[:, cols]
            inverse = lax.rsqrt(jnp.mean(middle * middle, axis=0, keepdims=True) + EPSILON)
            normed = (middle * inverse * gain_ref[...]).astype(BF16)
            normed_t_ref[:, cols] = normed
            normed_ref[cols, :] = normed.T

    for rows in tiles:
        normed = normed_ref[rows, :]
        gate = dot(normed, gate_w_ref[...], (1, 0))
        up = dot(normed, up_w_ref[...], (1, 0))
        gate_ref[rows, :] = gate.astype(BF16)
        up_ref[rows, :] = up.astype(BF16)
        hidden_ref[rows, :] = (gate * jax.nn.sigmoid(gate) * up).astype(BF16)


def ffn_up(middle, gain, w_gate, w_up):
    width, length = middle.shape
    hidden = w_gate.shape[1]
    return pl.pallas_call(
        ffn_up_kernel,
        grid=(hidden // CHUNK,),
        in_specs=[whole((width, length)), whole((width, 1)), by_cols(width), by_cols(width)],
        out_specs=[whole((width, length)), by_cols(length), by_cols(length), by_cols(length)],
        out_shape=[HBM((width, length), BF16)] + [HBM((length, hidden), BF16)] * 3,
        scratch_shapes=[pltpu.VMEM((length, width), BF16)],
        compiler_params=pltpu.CompilerParams(vmem_limit_bytes=FFN_GRANT),
        cost_estimate=pl.CostEstimate(
            flops=4 * length * width * hidden, bytes_accessed=30_000_000, transcendentals=length * hidden
        ),
        name="ffn_up",
    )(middle, gain, w_gate, w_up)


def ffn_back_kernel(
    grad_ref, middle_ref, gain_ref, gate_ref, up_ref, gate_w_ref, up_w_ref, down_w_ref,
    out_ref, out_narrow_ref, gate_grad_ref, up_grad_ref, gain_grad_ref, branch_t_ref, total_ref, branch_ref,
):
    step = pl.program_id(0)
    tiles = row_tiles(middle_ref.shape[1])

    @pl.when(step == 0)
    def _():
        for cols in tiles:
            branch = grad_ref[:, cols].astype(BF16)
            branch_t_ref[:, cols] = branch
            branch_ref[cols, :] = branch.T

    for rows in tiles:
        hidden_grad = dot(branch_ref[rows, :], down_w_ref[...], (1, 0))
        gate = gate_ref[rows, :].astype(F32)
        up = up_ref[rows, :].astype(F32)
        sigmoid = jax.nn.sigmoid(gate)
        scaled = hidden_grad * sigmoid
        up_grad = (scaled * gate).astype(BF16)
        gate_grad = (scaled * up * (1.0 + gate * (1.0 - sigmoid))).astype(BF16)
        gate_grad_ref[rows, :] = gate_grad
        up_grad_ref[rows, :] = up_grad
    part = dot(gate_w_ref[...], gate_grad_ref[...], (1, 1)) + dot(up_w_ref[...], up_grad_ref[...], (1, 1))

    @pl.when(step == 0)
    def _():
        total_ref[...] = part

    @pl.when(step > 0)
    def _():
        total_ref[...] += part

    @pl.when(step == pl.num_programs(0) - 1)
    def _():
        gain_grad = jnp.zeros(gain_ref.shape, F32)
        for cols in tiles:
            middle = middle_ref[:, cols]
            normed_grad = total_ref[:, cols]
            inverse = lax.rsqrt(jnp.mean(middle * middle, axis=0, keepdims=True) + EPSILON)
            unit = middle * inverse
            gain_grad += jnp.sum(normed_grad * unit, axis=1, keepdims=True)
            scaled = gain_ref[...] * normed_grad
            inner = jnp.mean(scaled * unit, axis=0, keepdims=True)
            out = grad_ref[:, cols] + inverse * (scaled - unit * inner)
            out_ref[:, cols] = out
            out_narrow_ref[:, cols] = out.astype(BF16)
        gain_grad_ref[...] = gain_grad


def ffn_back(grad, middle, gain, gate, up, w_gate, w_up, w_down_t):
    width, length = middle.shape
    hidden = w_gate.shape[1]
    full = whole((width, length))
    return pl.pallas_call(
        ffn_back_kernel,
        grid=(hidden // CHUNK,),
        in_specs=[
            full, full, whole((width, 1)), by_cols(length), by_cols(length), by_cols(width), by_cols(width), by_cols(width),
        ],
        out_specs=[full, full, by_cols(length), by_cols(length), whole((width, 1)), full],
        out_shape=[
            HBM((width, length), F32),
            jax.ShapeDtypeStruct((width, length), BF16),
            HBM((length, hidden), BF16),
            HBM((length, hidden), BF16),
            jax.ShapeDtypeStruct((width, 1), F32),
            HBM((width, length), BF16),
        ],
        scratch_shapes=[pltpu.VMEM((width, length), F32), pltpu.VMEM((length, width), BF16)],
        compiler_params=pltpu.CompilerParams(vmem_limit_bytes=BACK_GRANT),
        cost_estimate=pl.CostEstimate(
            flops=6 * length * width * hidden, bytes_accessed=50_000_000, transcendentals=length * hidden
        ),
        name="ffn_back",
    )(grad, middle, gain, gate, up, w_gate, w_up, w_down_t)


def weight_grad_kernel(left_fsdp, transposed, places_ref, left_ref, right_ref, left2_ref, right2_ref, keep_ref, send_ref):
    step = pl.program_id(0)
    contract = (1, 1) if transposed else (1, 0)
    total = dot(left_ref[...], right_ref[...], contract) + dot(left2_ref[...], right2_ref[...], contract)
    total = total.astype(BF16)
    half = total.shape[0] // 2
    fsdp, core = places_ref[0], places_ref[1]
    if left_fsdp:
        for out_ref, here in ((keep_ref, step < 2), (send_ref, step >= 2)):

            @pl.when(here)
            def _():
                out_ref[fsdp] = total[:half]
                out_ref[1 - fsdp] = total[half:]

    else:
        for out_ref, first in ((keep_ref, core), (send_ref, 1 - core)):

            @pl.when(first == 0)
            def _():
                out_ref[0] = total[:half]

            @pl.when(first == 1)
            def _():
                out_ref[0] = total[half:]


def weight_grad(places, products, more_products, left_fsdp):
    left, right = products
    left2, right2 = more_products
    rows, length = left.shape
    cols = right.shape[1]
    block = cols // 4
    left_spec = pl.BlockSpec((rows, length), lambda j, places: (0, 0))
    if left_fsdp:
        right_spec = pl.BlockSpec((length, block), lambda j, places: (0, (2 * places[1] + j) % 4))
        keep_spec = pl.BlockSpec((2, rows // 2, block), lambda j, places: (0, 0, jnp.minimum(j, 1)))
        send_spec = pl.BlockSpec((2, rows // 2, block), lambda j, places: (0, 0, jnp.maximum(j - 2, 0)))
    else:
        right_spec = pl.BlockSpec((length, block), lambda j, places: (0, (2 * places[0] + j) % 4))
        keep_spec = pl.BlockSpec((1, rows // 2, block), lambda j, places: (j // 2, 0, j % 2))
        send_spec = keep_spec
    return pl.pallas_call(
        partial(weight_grad_kernel, left_fsdp, False),
        grid_spec=pltpu.PrefetchScalarGridSpec(
            num_scalar_prefetch=1,
            grid=(4,),
            in_specs=[left_spec, right_spec, left_spec, right_spec],
            out_specs=[keep_spec, send_spec],
        ),
        out_shape=[jax.ShapeDtypeStruct((2, rows // 2, cols // 2), BF16)] * 2,
        compiler_params=pltpu.CompilerParams(vmem_limit_bytes=GRAD_GRANT),
        cost_estimate=pl.CostEstimate(
            flops=4 * rows * length * cols, bytes_accessed=10 * rows * cols, transcendentals=0
        ),
        name="weight_grad",
    )(places, left, right, left2, right2)


def mixed_grad_kernel(
    places_ref, mix_ref, branch_ref, normed_ref, qkv_ref, mix2_ref, branch2_ref, normed2_ref, qkv2_ref,
    keep_ref, send_ref,
):
    width = branch_ref.shape[0]
    half_cols = keep_ref.shape[2]
    out_part = dot(mix_ref[...], branch_ref[...], (1, 1)) + dot(mix2_ref[...], branch2_ref[...], (1, 1))
    qkv_part = dot(normed_ref[...], qkv_ref[...], (1, 1)) + dot(normed2_ref[...], qkv2_ref[...], (1, 1))
    out_part = out_part.astype(BF16)
    qkv_part = qkv_part.astype(BF16)
    first = half_cols - width
    core = places_ref[1]
    for low_ref, high_ref, here in ((keep_ref, send_ref, core == 0), (send_ref, keep_ref, core == 1)):

        @pl.when(here)
        def _():
            low_ref[0, :, :width] = out_part
            low_ref[0, :, width:] = qkv_part[:, :first]
            high_ref[0] = qkv_part[:, first:]


def mixed_grad(places, products, more_products):
    (mix, branch), (normed, qkv) = products
    (mix2, branch2), (normed2, qkv2) = more_products
    rows, length = mix.shape
    cols = branch.shape[0] + qkv.shape[0]
    left = pl.BlockSpec((rows // 2, length), lambda j, places: ((places[0] + j) % 2, 0))
    fixed = lambda shape: pl.BlockSpec(shape, lambda j, places: (0, 0))
    specs = [left, fixed(branch.shape), left, fixed(qkv.shape)]
    return pl.pallas_call(
        mixed_grad_kernel,
        grid_spec=pltpu.PrefetchScalarGridSpec(
            num_scalar_prefetch=1,
            grid=(2,),
            in_specs=specs + specs,
            out_specs=[pl.BlockSpec((1, rows // 2, cols // 2), lambda j, places: (j, 0, 0))] * 2,
        ),
        out_shape=[jax.ShapeDtypeStruct((2, rows // 2, cols // 2), BF16)] * 2,
        compiler_params=pltpu.CompilerParams(vmem_limit_bytes=MIXED_GRANT),
        cost_estimate=pl.CostEstimate(
            flops=4 * rows * length * cols, bytes_accessed=10 * rows * cols, transcendentals=0
        ),
        name="mixed_grad",
    )(places, mix, branch, normed, qkv, mix2, branch2, normed2, qkv2)


def assemble_kernel(stack_cores, cuts, places_ref, *refs):
    core, side = places_ref[1], places_ref[2]
    inputs, outputs = refs[:4], refs[4:]
    count, cols = inputs[0].shape
    whole_ref = outputs[-1]
    for k, piece_ref in enumerate(inputs):
        at_side = jnp.bitwise_xor(side, k % 2)
        at_core = jnp.bitwise_xor(core, k // 2)
        row = at_side * count + (at_core * (2 * count) if stack_cores else 0)
        rows = pl.ds(pl.multiple_of(row, 8), count)
        value = piece_ref[...].astype(F32)
        if stack_cores:
            whole_ref[rows, :] = value
        else:
            whole_ref[rows, pl.ds(pl.multiple_of(at_core * cols, 128), cols)] = value
    for out_ref, (low, high) in zip(outputs[:-1], cuts):
        value = whole_ref[:, low:high]
        out_ref[...] = value.T if out_ref.shape[0] == high - low else value


def assemble(places, pieces, stack_cores, cuts=()):
    count, cols = pieces[0].shape
    shape = (4 * count, cols) if stack_cores else (2 * count, 2 * cols)
    out_shape = [
        jax.ShapeDtypeStruct((high - low, shape[0]) if high - low < shape[0] else (shape[0], high - low), F32)
        for low, high in cuts
    ]
    out_shape = out_shape or [jax.ShapeDtypeStruct(shape, F32)]
    return pl.pallas_call(
        partial(assemble_kernel, stack_cores, cuts),
        grid_spec=pltpu.PrefetchScalarGridSpec(
            num_scalar_prefetch=1,
            grid=(1,),
            in_specs=[pl.BlockSpec((count, cols), lambda j, places: (0, 0))] * 4,
            out_specs=[pl.BlockSpec(out.shape, lambda j, places: (0, 0)) for out in out_shape],
            scratch_shapes=[pltpu.VMEM(shape, F32)] if cuts else [],
        ),
        out_shape=out_shape,
        compiler_params=pltpu.CompilerParams(vmem_limit_bytes=24 << 20),
        cost_estimate=pl.CostEstimate(flops=0, bytes_accessed=24 * count * cols, transcendentals=0),
        name="assemble",
    )(places, *pieces)


def doc_tables(doc_row):
    token_index = jnp.arange(doc_row.shape[0])
    start = jnp.sum((doc_row[:, None] < doc_row[None, :]).astype(jnp.int32), axis=0)
    places = (token_index - start).astype(F32)
    frequency = ROPE_BASE ** (-2.0 * jnp.arange(HALF, dtype=F32) / HEAD_SIZE)
    angles = frequency[:, None] * places[None, :]
    return (start[None, :], jnp.cos(angles), jnp.sin(angles))


def norm_forward(inputs, gain):
    inverse = lax.rsqrt(jnp.mean(inputs * inputs, axis=0, keepdims=True) + EPSILON)
    return (inputs * inverse * gain).astype(BF16)


def norm_backward(inputs, gain, grad):
    inverse = lax.rsqrt(jnp.mean(inputs * inputs, axis=0, keepdims=True) + EPSILON)
    scaled = gain * grad
    inner = jnp.mean(scaled * inputs, axis=0, keepdims=True)
    return (inverse * scaled - inputs * inverse**3 * inner, jnp.sum(grad * inputs * inverse, axis=1, keepdims=True))


def project(inputs, w_qkv, gains, tables):
    _, cosine, sine = tables
    length = inputs.shape[1]
    normed = norm_forward(inputs, gains[0])
    raw = dot(w_qkv, normed, (0, 0))
    heads = QUERY_HEADS + KEY_VALUE_HEADS
    pairs = raw[: heads * HEAD_SIZE].reshape(heads, 2, HALF, length)
    first, second = pairs[:, 0], pairs[:, 1]
    rotated = jnp.stack([first * cosine - second * sine, second * cosine + first * sine], axis=1)
    qkv = jnp.concatenate(
        [rotated.reshape(heads * HEAD_SIZE, length).astype(BF16), raw[heads * HEAD_SIZE :].astype(BF16)], axis=0
    )
    return (normed, qkv)


def project_out(inputs, w_out, mix):
    return inputs + dot(w_out, mix, (0, 0))


def attention_backward(kept, attn_grad, weights, tables):
    start, cosine, sine = tables
    _, _, qkv, logsum, mix = kept
    mix_grad = dot(weights[1], attn_grad, (1, 0)).astype(BF16)
    return attention_back(start, cosine, sine, qkv, mix, logsum, mix_grad)


def input_backward(kept, middle_grad, qkv_grad, weights, gains):
    normed_grad = dot(weights[0], qkv_grad, (1, 0))
    inputs_grad, gain_grad = norm_backward(kept[0], gains[0], normed_grad)
    return (inputs_grad + middle_grad, gain_grad)


def after(value, *earlier):
    return lax.optimization_barrier((value,) + earlier)[0]


def swap_fsdp(value):
    return lax.ppermute(value, "fsdp", [(0, 1), (1, 0)])


def swap_dp(value, bit, size=16):
    return lax.ppermute(value, "dp", [(i, i ^ bit) for i in range(size)])


def fetch(parts, axis, index, pieces):
    sent = [cut_piece(part, index, axis, pieces) for part in parts]
    sent = jnp.concatenate(sent, axis=1) if len(sent) > 1 else sent[0]
    return sent


def cut_piece(value, index, axis, pieces):
    count = value.shape[axis] // pieces
    return lax.dynamic_slice_in_dim(value, index * count, count, axis)


def join_kernel(own_count, shard_axis, piece_axis, index_at, places_ref, *refs):
    own, pieces, out_ref = refs[:own_count], refs[own_count:-1], refs[-1]
    rows, cols = out_ref.shape
    fsdp = places_ref[0]
    index = places_ref[index_at]
    if shard_axis == 0:
        half = pl.ds(pl.multiple_of(fsdp * (rows // 2), 16), rows // 2)
        at = 0
        for ref in own:
            out_ref[half, at : at + ref.shape[1]] = ref[...]
            at += ref.shape[1]
    else:
        out_ref[:, pl.ds(pl.multiple_of(fsdp * (cols // 2), 128), cols // 2)] = own[0][...]
    for flip, ref in enumerate(pieces):
        at = jnp.bitwise_xor(index, flip)
        count, width = ref.shape
        row = at * count if piece_axis == 0 else 0
        col = at * width if piece_axis == 1 else 0
        if shard_axis == 0:
            row = row + (1 - fsdp) * (rows // 2)
        else:
            col = col + (1 - fsdp) * (cols // 2)
        row_at = pl.ds(pl.multiple_of(row, 16), count)
        if shard_axis == 0 and piece_axis == 0:
            out_ref[row_at, :] = ref[...]
        else:
            out_ref[row_at, pl.ds(pl.multiple_of(col, 128), width)] = ref[...]


def join(places, own, pieces, shard_axis, piece_axis, index_at):
    rows, cols = own[0].shape[0], sum(part.shape[1] for part in own)
    shape = (2 * rows, cols) if shard_axis == 0 else (rows, 2 * cols)
    full = lambda shape: pl.BlockSpec(shape, lambda j, places: (0, 0))
    return pl.pallas_call(
        partial(join_kernel, len(own), shard_axis, piece_axis, index_at),
        grid_spec=pltpu.PrefetchScalarGridSpec(
            num_scalar_prefetch=1,
            grid=(1,),
            in_specs=[full(part.shape) for part in (*own, *pieces)],
            out_specs=full(shape),
        ),
        out_shape=jax.ShapeDtypeStruct(shape, BF16),
        compiler_params=pltpu.CompilerParams(vmem_limit_bytes=24 << 20),
        cost_estimate=pl.CostEstimate(flops=0, bytes_accessed=4 * shape[0] * shape[1], transcendentals=0),
        name="join",
    )(places, *own, *pieces)


def add(left, right):
    return (left.astype(F32) + right.astype(F32)).astype(BF16)


def add3(first, second, third):
    return ((first.astype(F32) + second.astype(F32)) + third.astype(F32)).astype(BF16)


def reduce_vector(values):
    total = values
    for bit in (1, 2, 4, 8):
        total = add(total, swap_dp(total, bit))
    total = add(total, swap_fsdp(total))
    count = values.shape[1] // 2
    return lax.dynamic_slice_in_dim(total, lax.axis_index("fsdp") * count, count, 1)


def gather_gains(gains):
    other = swap_fsdp(gains)
    first = lax.axis_index("fsdp") == 0
    return jnp.concatenate([jnp.where(first, gains, other), jnp.where(first, other, gains)], axis=1)


def cut(value, which, axis):
    count = value.shape[axis] // 2
    return lax.dynamic_slice_in_dim(value, which * count, count, axis)


def sides():
    place = lax.axis_index("dp")
    return ((place // 2) % 2, (place // 4) % 2, (place // 8) % 2)


class Reduction:
    def __init__(self, halves, queue=()):
        self.keep, send = halves
        self.received = swap_dp(after(send, *queue), 1)
        self.side, self.lane, _ = sides()
        self.plan = iter((self.fsdp, self.y, self.z_near, self.z_far, self.z_back, self.y_back, self.finish))

    def step(self, queue):
        mine = next(self.plan)(lambda value: after(value, *queue))
        queue[:] = [mine]

    def split(self, value, which, axis, bit):
        mine, self.own = cut(value, 1 - which, axis), cut(value, which, axis)
        self.incoming = swap_dp(mine, bit)
        return mine

    def fsdp(self, gate):
        mine = add(gate(self.keep)[1], self.received[1])
        self.incoming = swap_fsdp(mine)
        return mine

    def fsdp_sum(self, gate):
        return add3(gate(self.keep)[0], self.received[0], self.incoming)

    def y(self, gate):
        return self.split(self.fsdp_sum(gate), self.side, 0, 2)

    def z_near(self, gate):
        return self.split(add(gate(self.own), self.incoming), self.lane, 1, 4)

    def z_far(self, gate):
        self.own = add(gate(self.own), self.incoming)
        self.incoming = swap_dp(self.own, 8)
        return self.own

    def z_back(self, gate):
        self.own = add(gate(self.own), self.incoming)
        self.incoming = swap_dp(self.own, 4)
        return self.own

    def y_back(self, gate):
        mine = self.own = put_together(gate(self.own), self.incoming, self.lane, 1)
        self.across = swap_dp(mine, 2)
        self.beside = swap_dp(mine, 1)
        return mine

    def finish(self, gate):
        mine = gate(self.across)
        self.pieces = (self.own, mine, self.beside, swap_dp(mine, 1))
        return mine


class ReductionOverZ(Reduction):
    def __init__(self, halves, queue=()):
        super().__init__(halves, queue)
        self.far = sides()[2]
        self.plan = iter((self.fsdp, self.first, self.second, self.over_y, self.back_far, self.back_near, self.done))

    def first(self, gate):
        return self.split(self.fsdp_sum(gate), self.lane, 0, 4)

    def second(self, gate):
        return self.split(add(gate(self.own), self.incoming), self.far, 0, 8)

    def over_y(self, gate):
        self.own = add(gate(self.own), self.incoming)
        self.incoming = swap_dp(self.own, 2)
        return self.own

    def back_far(self, gate):
        self.own = add(gate(self.own), self.incoming)
        self.incoming = swap_dp(self.own, 8)
        return self.own

    def back_near(self, gate):
        mine = self.own = put_together(gate(self.own), self.incoming, self.far, 0)
        self.across = swap_dp(mine, 4)
        self.beside = swap_dp(mine, 1)
        return mine

    def done(self, gate):
        mine = gate(self.across)
        self.pieces = (self.own, mine, self.beside, swap_dp(mine, 1))
        return mine


class ReductionBothWays(Reduction):
    def __init__(self, halves, queue=()):
        super().__init__(halves, queue)
        self.plan = iter((self.one, self.two, self.three, self.z_far, self.z_back, self.y_back, self.finish))

    def one(self, gate):
        keep = gate(self.keep)
        half = keep.shape[2] // 2
        theirs = add(keep[1, :, :half], self.received[1, :, :half])
        self.over_x = swap_fsdp(theirs)
        both = add(keep[:, :, half:], self.received[:, :, half:])
        mine, self.both = cut(both, 1 - self.side, 1), cut(both, self.side, 1)
        self.over_y = swap_dp(mine, 2)
        return mine

    def two(self, gate):
        half = self.keep.shape[2] // 2
        first = add3(gate(self.keep)[0, :, :half], self.received[0, :, :half], self.over_x)
        mine, self.first = cut(first, 1 - self.side, 0), cut(first, self.side, 0)
        self.over_y_too = swap_dp(mine, 2)
        theirs = add(gate(self.both)[1], self.over_y[1])
        self.over_x_too = swap_fsdp(theirs)
        return theirs

    def three(self, gate):
        first = add(gate(self.first), self.over_y_too)
        second = add3(gate(self.both)[0], self.over_y[0], self.over_x_too)
        mine = jnp.where(self.lane == 0, second, first)
        self.own = jnp.where(self.lane == 0, first, second)
        self.incoming = swap_dp(mine, 4)
        return mine


def put_together(own, other, which, axis):
    low = jnp.where(which == 0, own, other)
    high = jnp.where(which == 0, other, own)
    return jnp.concatenate([low, high], axis=axis)


def make_body(fsdp_size, dp_size):
    paired = fsdp_size == 2 and dp_size == 16

    def body(
        activations, doc_ids, w_query, key_projection, value_projection, w_out,
        gain_attn, gain_ffn, w_gate, w_up, w_down, cotangent,
    ):
        if paired:
            place = lax.axis_index("dp")
            core, side, lane = place % 2, (place // 2) % 2, (place // 4) % 2
            index_y, index_z = place % 4, core + 2 * lane
            places = jnp.stack([lax.axis_index("fsdp"), core, side, index_y, index_z]).astype(jnp.int32)
            qkv_own = (w_query, key_projection, value_projection)
            qkv_sent = fetch(qkv_own, 0, core, 2)
            out_sent = fetch((after(w_out, qkv_sent),), 0, core, 2)
            gate_sent = fetch((after(w_gate, out_sent),), 1, index_y, 4)
            up_sent = fetch((after(w_up, gate_sent),), 1, index_z, 4)
            down_sent = fetch((after(w_down.T, up_sent),), 0, index_y, 4)
            qkv_mine = swap_fsdp(qkv_sent)
            gains = gather_gains(after(jnp.stack([gain_attn, gain_ffn]), qkv_sent)).astype(F32)
            out_mine, gate_mine, up_mine, down_mine = [
                swap_fsdp(sent) for sent in (out_sent, gate_sent, up_sent, down_sent)
            ]
            w_qkv = join(places, qkv_own, (qkv_mine, swap_dp(qkv_mine, 1)), 0, 0, 1)
        else:
            collect = lambda shard, axis: lax.all_gather(shard, "fsdp", axis=axis, tiled=True)
            gains = collect(jnp.stack([gain_attn, gain_ffn]), 1).astype(F32)
            places = jnp.zeros((4,), jnp.int32)
            qkv_shard = jnp.concatenate([w_query, key_projection, value_projection], axis=1)
            weights = (
                collect(qkv_shard, 0), collect(w_out, 0), collect(w_gate, 0), collect(w_up, 0), collect(w_down, 0).T,
            )
        gains = (gains[0][:, None], gains[1][:, None])
        tables = doc_tables(doc_ids[0])
        start, cosine, sine = tables
        inputs = activations[0].T.astype(F32)

        if paired:
            normed, qkv = project(inputs, w_qkv, gains, tables)
            out_mine = after(out_mine, qkv)
            gate_mine = after(gate_mine, out_mine)
            out_beside = swap_dp(out_mine, 1)
            gate_across, gate_beside = swap_dp(gate_mine, 2), swap_dp(gate_mine, 1)
            mix, logsum = attention(start, qkv)
            up_mine = after(up_mine, mix)
            up_across, up_beside = swap_dp(up_mine, 4), swap_dp(up_mine, 1)
            gate_across = after(gate_across, up_mine)
            gate_corner = swap_dp(gate_across, 1)
            w_out_full = join(places, (w_out,), (out_mine, out_beside), 0, 0, 1)
            middle = project_out(inputs, w_out_full, mix)
            down_mine = after(down_mine, middle)
            down_across, down_beside = swap_dp(down_mine, 2), swap_dp(down_mine, 1)
            gate_pieces = (after(gate_mine, down_mine), gate_beside, gate_across, gate_corner)
            w_gate_full = join(places, (w_gate,), gate_pieces, 0, 1, 3)
            up_across = after(up_across, w_gate_full)
            w_up_full = join(places, (w_up,), (up_mine, up_beside, up_across, swap_dp(up_across, 1)), 0, 1, 4)
            first_normed, first_gate, first_up, first_hidden = ffn_up(middle, gains[1], w_gate_full, w_up_full)
            down_across = after(down_across, first_hidden)
            w_down_full = join(
                places, (w_down.T,), (down_mine, down_beside, down_across, swap_dp(down_across, 1)), 1, 0, 3
            )
            weights = (w_qkv, w_out_full, w_gate_full, w_up_full, w_down_full)
            ffn_weights = weights[2:]
        else:
            ffn_weights = weights[2:]
            normed, qkv = project(inputs, weights[0], gains, tables)
            mix, logsum = attention(start, qkv)
            middle = project_out(inputs, weights[1], mix)
            first_normed, first_gate, first_up, first_hidden = ffn_up(middle, gains[1], *ffn_weights[:2])
        first = (inputs, normed, qkv, logsum, mix)
        inputs2 = middle + dot(ffn_weights[2], first_hidden, (1, 1))
        normed2, qkv2 = project(inputs2, weights[0], gains, tables)
        mix2, logsum2 = attention(start, qkv2)
        middle2 = project_out(inputs2, weights[1], mix2)
        second = (inputs2, normed2, qkv2, logsum2, mix2)
        outputs, second_normed, second_gate, second_up, second_hidden = ffn(middle2, gains[1], *ffn_weights)

        grad = cotangent[0].T.astype(F32)
        grad, attn_grad2, gate_grad2, up_grad2, ffn_gain2, branch2 = ffn_back(
            grad, middle2, gains[1], second_gate, second_up, *ffn_weights
        )
        qkv_grad2 = attention_backward(second, attn_grad2, weights, tables)
        grad, attn_gain2 = input_backward(second, grad, qkv_grad2, weights, gains)

        down_halves = weight_grad(
            places, (branch2, second_hidden), (grad.astype(BF16), first_hidden), False
        )
        queue = []
        if paired:
            down = Reduction(down_halves)
            down.step(queue)
            grad = after(grad, *queue)
        else:
            grad = after(grad, *down_halves)
        grad, attn_grad, gate_grad, up_grad, ffn_gain, _ = ffn_back(
            grad, middle, gains[1], first_gate, first_up, *ffn_weights
        )
        if paired:
            down.step(queue)
            gate_grad = after(gate_grad, *queue)
        gate_halves = weight_grad(places, (second_normed, gate_grad2), (first_normed, gate_grad), True)
        if paired:
            queue.append(gate_halves[0])
            down.step(queue)
            gate = Reduction(gate_halves, queue)
        mix_grad_in = after(attn_grad, *gate_halves)
        mix_grad = dot(weights[1], mix_grad_in, (1, 0)).astype(BF16)
        if paired:
            queue.append(mix_grad)
            gate.step(queue)
            up_grad = after(up_grad, *queue)
        up_halves = weight_grad(places, (second_normed, up_grad2), (first_normed, up_grad), True)
        if paired:
            queue.append(up_halves[0])
            down.step(queue)
            up = Reduction(up_halves, queue)
            up.step(queue)
            mix_grad = after(mix_grad, *queue)
        qkv_grad = attention_back(start, cosine, sine, first[2], first[4], first[3], mix_grad)
        if paired:
            queue.append(qkv_grad)
            down.step(queue)
            gate.step(queue)
            qkv_grad = after(qkv_grad, *queue)
        mixed_halves = mixed_grad(
            places,
            ((second[4], attn_grad2), (second[1], qkv_grad2)),
            ((first[4], attn_grad), (first[1], qkv_grad)),
        )
        if paired:
            mixed = Reduction(mixed_halves)
            queue.append(mixed_halves[0])
            down.step(queue)
            gate.step(queue)
            up.step(queue)
            mixed.step(queue)
            grad = after(grad, *queue)
        grad, attn_gain = input_backward(first, grad, after(qkv_grad, *mixed_halves), weights, gains)
        gain_grads = jnp.concatenate([attn_gain + attn_gain2, ffn_gain + ffn_gain2], axis=1).T.astype(BF16)

        width = w_query.shape[1]
        key_end = width + key_projection.shape[1]
        value_end = key_end + value_projection.shape[1]
        cuts = ((0, width), (width, 2 * width), (2 * width, width + key_end), (width + key_end, width + value_end))
        if paired:
            grad_narrow = grad.T.astype(BF16)[None]
            queue.append(grad_narrow)
            down.step(queue)
            gate.step(queue)
            up.step(queue)
            mixed.step(queue)
            gate.step(queue)
            up.step(queue)
            gate.step(queue)
            mixed.step(queue)
            (grad_down,) = assemble(places, [after(down.pieces[0], *queue), *down.pieces[1:]], True)
            queue.append(grad_down)
            up.step(queue)
            mixed.step(queue)
            up.step(queue)
            mixed.step(queue)
            gate.step(queue)
            mixed.step(queue)
            up.step(queue)
            (grad_gate,) = assemble(places, [after(gate.pieces[0], *queue), *gate.pieces[1:]], False)
            queue.append(grad_gate)
            (grad_up,) = assemble(places, [after(up.pieces[0], *queue), *up.pieces[1:]], False)
            queue.append(grad_up)
            mixed.step(queue)
            grad_out, grad_query, grad_key, grad_value = assemble(places, mixed.pieces, False, cuts)
            grad_key, grad_value = grad_key.T, grad_value.T
            gain_grads = reduce_vector(gain_grads).astype(F32)
        else:
            grad_narrow = grad.T.astype(BF16)[None]

            def reduce(value, axis):
                part = lax.psum_scatter(value, "fsdp", scatter_dimension=axis, tiled=True)
                return lax.psum(part, "dp").astype(F32)

            rows = lambda halves: jnp.concatenate([h.reshape(-1, h.shape[2]) for h in halves], axis=1)
            cols = lambda halves: jnp.concatenate([jnp.concatenate([h[0], h[1]], axis=1) for h in halves])
            grad_down = reduce(cols(down_halves).T, 0).T
            grad_gate = reduce(rows(gate_halves), 0)
            grad_up = reduce(rows(up_halves), 0)
            mixed = reduce(rows(mixed_halves), 0)
            grad_out, grad_query, grad_key, grad_value = [mixed[:, low:high] for low, high in cuts]
            gain_grads = reduce(gain_grads, 1)
        return (
            outputs.T.astype(BF16)[None],
            grad_narrow,
            grad_query,
            grad_key,
            grad_value,
            grad_out,
            gain_grads[0],
            gain_grads[1],
            grad_gate,
            grad_up,
            grad_down.T,
        )

    return body


def solution(mesh):
    sequences = P(("dp", "fsdp"), None, None)
    rows = P("fsdp", None)
    vector = P("fsdp")
    in_specs = (
        sequences, P(("dp", "fsdp"), None), rows, rows, rows, rows, vector, vector, rows, rows, rows, sequences,
    )
    out_specs = (sequences, sequences, rows, rows, rows, rows, vector, vector, rows, rows, rows)
    body = make_body(mesh.shape["fsdp"], mesh.shape["dp"])
    return jax.shard_map(body, mesh=mesh, in_specs=in_specs, out_specs=out_specs, check_vma=False)
```
